32 devices in a mesh: sub: 8 (over z, x), crs: 4 (over y, core).
Axes of the slice: x: 2, y: 2, z: 4, core: 2. Of those that a mesh axis runs over, the one named last changes fastest.
Arguments:
- schur_block: float32 [64, 1536, 1536], P('sub', 'crs'), as said below
- rigid_modes: float32 [64, 6, 1536], P('sub'), may hold values from -0.4375 to 0.4375
- coarse_inverse: float32 [384, 384], P('crs'), as said below
- dual_rhs: float32 [32, 64, 1536], P('crs', 'sub'), may hold values from -6 to 6
- stiff_diag: float32 [64, 1536], P('sub'), may hold values from 0.25 to 2.5
- face_length: int32 [64, 6], P('sub'), may hold values from 0 to 256, as said below
Outputs:
- multipliers: float32 [32, 64, 1536], P('crs', 'sub')
- projected: float32 [32, 64, 1536], P('crs', 'sub')
The draws below stay inside these ranges and needn't reach their ends.
Inputs may be any that keep to these rules, and one draw needn't show every extreme that they name: Equal on the two sides of a face: face_length[s, c] = face_length[partner(s, c), c]; 0 where partner(s, c) does not exist; at least 64 where it exists. Each schur_block[s] is symmetric positive definite. coarse_inverse is symmetric.
All inputs are finite; a program needn't handle non-finite values.
Results may differ from the reference program's by a relative error of at most 0.0003.
Values sent between devices are 32-bit elements; how exact they have to be, the bound alone decides.
A program may use at most 64 MiB of HBM per device.

```python
import math
import jax
import jax.numpy as jnp
import numpy as np
from jax import lax

NI = 1536
MODES = 6
LOADS = 32
ITERS = 2
SY = 2
SZ = 4
SUBS = 8
SLOT = 256
NSUB = 64
NC = 384


def schur_single(sub_key):
    first_key = jax.random.fold_in(sub_key, 1)
    second_key = jax.random.fold_in(sub_key, 2)
    raw = jax.random.normal(first_key, (NI, NI), jnp.float32)
    symmetric = (raw + raw.T) * (0.5 / math.sqrt(NI))
    diagonal = jax.random.uniform(second_key, (NI,), jnp.float32, 2.0, 3.5)
    rows_idx = lax.broadcasted_iota(jnp.int32, (NI, NI), 0)
    cols_idx = lax.broadcasted_iota(jnp.int32, (NI, NI), 1)
    return jnp.where(rows_idx == cols_idx, diagonal[:, None], symmetric)


def draw_schur_block(key, part):
    base_key = jax.random.fold_in(key, 11)
    return lax.map(lambda number: schur_single(jax.random.fold_in(base_key, number)), jnp.arange(NSUB, dtype=jnp.int32))


def draw_coarse_inverse(key, part):
    first_key = jax.random.fold_in(key, 21)
    second_key = jax.random.fold_in(key, 22)
    raw = jax.random.normal(first_key, (NC, NC), jnp.float32)
    symmetric = (raw + raw.T) * (0.1 / math.sqrt(NC))
    diagonal = jax.random.uniform(second_key, (NC,), jnp.float32, 0.4, 0.8)
    rows_idx = lax.broadcasted_iota(jnp.int32, (NC, NC), 0)
    cols_idx = lax.broadcasted_iota(jnp.int32, (NC, NC), 1)
    return jnp.where(rows_idx == cols_idx, diagonal[:, None], symmetric)


def draw_face_length(key, part):
    indices = jnp.arange(NSUB, dtype=jnp.int32)
    coords = [indices // SUBS, indices % SUBS // SZ, indices % SZ]
    extent = [NSUB // SUBS, SY, SZ]
    stride = [SUBS, SZ, 1]
    drawn = jax.random.randint(jax.random.fold_in(key, 31), (NSUB, 6), SLOT // 4, SLOT + 1, dtype=jnp.int32)
    drawn = drawn.at[0, 0].set(SLOT)
    columns = []
    for colour in range(6):
        axis_pick = colour // 2
        anchor = coords[axis_pick]
        offset = jnp.where(anchor % 2 == colour % 2, 1, -1)
        target = anchor + offset
        inside = (target >= 0) & (target < extent[axis_pick])
        lower = jnp.clip(jnp.minimum(indices, indices + offset * stride[axis_pick]), 0, NSUB - 1)
        columns.append(jnp.where(inside, drawn[lower, colour], 0))
    return jnp.stack(columns, axis=1).astype(jnp.int32)


def block_scale(rng, shape, shards, smallest, largest):
    def one(axis_at, shards_of):
        heights = jax.random.uniform(jax.random.fold_in(jax.random.fold_in(rng, 6), axis_at), (shards_of,), jnp.float32, smallest / len(shards), largest / len(shards))
        return jnp.repeat(jnp.exp(heights), shape[axis_at] // shards_of).reshape((-1,) + (1,) * (len(shape) - axis_at - 1))

    level = one(*shards[0])
    for cut in shards[1:]:
        level = level * one(*cut)
    return level


def normal_values(key, dims, spread, most, split=(), held_as=jnp.bfloat16):
    result = spread * jax.random.normal(key, dims, jnp.float32)
    if split:
        result = result * block_scale(key, dims, split, -0.22, 0.18)
    return jnp.clip(result, -most, most).astype(held_as)


def setup_inputs(seed: int = 0) -> dict:
    splits = jax.random.split(jax.random.key(seed), 7)
    return {
        "schur_block": draw_schur_block(jax.random.fold_in(splits[6], 71), 0),
        "rigid_modes": normal_values(splits[1], (NSUB, MODES, NI), (NI // 8) ** -0.5, 0.4375, ((0, 8),), jnp.float32),
        "coarse_inverse": draw_coarse_inverse(jax.random.fold_in(splits[6], 71), 0),
        "dual_rhs": normal_values(splits[3], (LOADS, NSUB, NI), 1.0, 6.0, ((0, 4), (1, 8)), jnp.float32),
        "stiff_diag": jnp.clip(jnp.exp(math.log(2.5) - 2.3025851 * jax.random.uniform(splits[4], (NSUB, NI), jnp.float32) ** block_scale(splits[4], (NSUB, NI), ((0, 8),), -0.2, 0.2)), 0.25, 2.5),
        "face_length": draw_face_length(jax.random.fold_in(splits[6], 71), 0),
    }


PRECISE = lax.Precision.HIGHEST


def partner_lookup():
    indices = np.arange(NSUB)
    coords = [indices // SUBS, (indices % SUBS) // SZ, indices % SZ]
    extent = [NSUB // SUBS, SY, SZ]
    stride = [SUBS, SZ, 1]
    lookup = np.zeros((6, NSUB), np.int32)
    for colour in range(6):
        axis_pick = colour // 2
        anchor = coords[axis_pick]
        offset = np.where(anchor % 2 == colour % 2, 1, -1)
        target = anchor + offset
        inside = (target >= 0) & (target < extent[axis_pick])
        lookup[colour] = np.where(inside, indices + offset * stride[axis_pick], indices)
    return lookup


def partner_values(vector, lookup):
    pieces = []
    for colour in range(6):
        window = vector[..., colour * SLOT:(colour + 1) * SLOT]
        pieces.append(jnp.take(window, jnp.asarray(lookup[colour]), axis=-2))
    return jnp.concatenate(pieces, axis=-1)


def inner(first_vec, second_vec):
    return 0.5 * jnp.sum(first_vec * second_vec, axis=(1, 2))


def reference(schur_block, rigid_modes, coarse_inverse, dual_rhs, stiff_diag, face_length):
    lookup = partner_lookup()
    positions = (jnp.arange(NI) % SLOT).astype(jnp.int32)
    usable = (jnp.repeat(face_length, SLOT, axis=1) > positions[None, :]).astype(jnp.float32)

    def assemble(vector):
        return usable * (vector - partner_values(vector, lookup))

    precond = usable * (stiff_diag + partner_values(stiff_diag, lookup))

    def project(vector):
        coarse = jnp.einsum('lsi,smi->lsm', vector, rigid_modes, precision=PRECISE).reshape(LOADS, NC)
        solved = jnp.einsum('lb,ab->la', coarse, coarse_inverse, precision=PRECISE).reshape(LOADS, NSUB, MODES)
        lifted = jnp.einsum('lsm,smi->lsi', solved, rigid_modes, precision=PRECISE)
        return vector - assemble(lifted)

    residual = assemble(dual_rhs)
    multipliers = jnp.zeros_like(residual)
    projected = project(residual)
    scaled = precond * projected
    energy = inner(projected, scaled)
    search = project(scaled)
    for iteration in range(ITERS):
        image = assemble(jnp.einsum('sij,lsj->lsi', schur_block, search, precision=PRECISE))
        step_size = energy / inner(search, image)
        multipliers = multipliers + step_size[:, None, None] * search
        residual = residual - step_size[:, None, None] * image
        projected = project(residual)
        if iteration + 1 < ITERS:
            scaled = precond * projected
            energy_new = inner(projected, scaled)
            search = project(scaled) + (energy_new / energy)[:, None, None] * search
            energy = energy_new
    return multipliers, projected
```

```python
import functools

import jax
import jax.numpy as jnp
import numpy as np
from jax import lax
from jax.experimental import pallas as pl
from jax.experimental.pallas import tpu as pltpu
from jax.sharding import PartitionSpec as P

ITERS = 2
SY = 2
SZ = 4
SUBS = 8

PRECISE = lax.Precision.HIGHEST
SPLIT = lax.Precision.HIGH


def local_lookup():
    indices = np.arange(SUBS)
    coords = [indices // SZ, indices % SZ]
    extent = [SY, SZ]
    stride = [SZ, 1]
    lookup = np.zeros((4, SUBS), np.int32)
    for colour in range(4):
        axis_pick = colour // 2
        anchor = coords[axis_pick]
        offset = np.where(anchor % 2 == colour % 2, 1, -1)
        target = anchor + offset
        inside = (target >= 0) & (target < extent[axis_pick])
        lookup[colour] = np.where(inside, indices + offset * stride[axis_pick], indices)
    return lookup


def by_collectives(schur_block, rigid_modes, coarse_inverse, dual_rhs, stiff_diag, face_length):
    loads, subs, interface = dual_rhs.shape
    slot = interface // 6
    modes = rigid_modes.shape[1]
    own = subs * modes
    nsub = lax.axis_size("sub")
    sub_index = lax.axis_index("sub")
    even = sub_index % 2 == 0
    lookup = local_lookup()
    positions = jnp.arange(interface) % slot
    usable = (jnp.repeat(face_length, slot, axis=1) > positions[None, :]).astype(jnp.float32)
    up = [(i, i + 1) for i in range(nsub - 1)]
    down = [(i + 1, i) for i in range(nsub - 1)]

    def partner(vector):
        first = vector[..., :slot]
        second = vector[..., slot : 2 * slot]
        from_left = lax.ppermute(jnp.where(even, first, second), "sub", up)
        from_right = lax.ppermute(jnp.where(even, second, first), "sub", down)
        pieces = [jnp.where(even, from_right, from_left), jnp.where(even, from_left, from_right)]
        for colour in range(2, 6):
            window = vector[..., colour * slot : (colour + 1) * slot]
            pieces.append(
                jnp.concatenate([window[..., t : t + 1, :] for t in lookup[colour - 2]], axis=-2)
            )
        return jnp.concatenate(pieces, axis=-1)

    modes_first = jnp.swapaxes(rigid_modes, 0, 1)
    together = jnp.concatenate([dual_rhs, modes_first, stiff_diag[None]], axis=0)
    across = partner(together)
    residual = usable * (dual_rhs - across[:loads])
    modes_across = across[loads : loads + modes]
    precond = usable * (stiff_diag + across[-1])

    inverse = lax.all_gather(coarse_inverse, "crs", axis=0, tiled=True)

    def by_slot(array):
        return array.reshape(array.shape[:-1] + (6, slot))

    basis = by_slot(usable * jnp.concatenate([modes_first, -modes_across], axis=0))

    weighted = by_slot(modes_first * precond)
    blocks = jnp.einsum("msck,nsck->scmn", weighted, basis, precision=PRECISE)
    total_subs = nsub * subs
    here = sub_index * subs + jnp.arange(subs)
    left = here - subs
    right = here + subs
    targets = [jnp.where(even, right, left), jnp.where(even, left, right)]
    for colour in range(2, 6):
        targets.append(sub_index * subs + jnp.asarray(lookup[colour - 2]))
    targets = jnp.stack(targets, axis=1)
    hot_across = (targets[:, :, None] == jnp.arange(total_subs)).astype(jnp.float32)
    hot_here = (here[:, None] == jnp.arange(total_subs)).astype(jnp.float32)
    dense = jnp.einsum("smn,st->smtn", blocks[..., :modes].sum(axis=1), hot_here, precision=PRECISE)
    dense = dense + jnp.einsum("scmn,sct->smtn", blocks[..., modes:], hot_across, precision=PRECISE)
    dense = dense.reshape(own, total_subs * modes)
    middle = lax.all_gather(dense, "sub", axis=0, tiled=True)

    def coarse(vector):
        return jnp.einsum("lsi,msi->lsm", vector, modes_first, precision=PRECISE).reshape(loads, own)

    def dots(a, b):
        return jnp.sum(a * b, axis=(1, 2))[:, None]

    def shared(parts):
        gathered = lax.all_gather(jnp.concatenate(parts, axis=1), "sub", axis=0)
        count = own * (sum(part.shape[1] == own for part in parts))
        outs = []
        for at in range(0, count, own):
            outs.append(jnp.swapaxes(gathered[:, :, at : at + own], 0, 1).reshape(loads, nsub * own))
        sums = jnp.sum(gathered[:, :, count:], axis=0)
        return outs, [sums[:, j : j + 1] for j in range(sums.shape[1])]

    def solve(values):
        return jnp.einsum("lb,ab->la", values, inverse, precision=PRECISE)

    def lifted(values):
        grid = values.reshape(loads, nsub, subs, modes)
        padded = jnp.pad(grid, ((0, 0), (1, 1), (0, 0), (0, 0)))
        near = lax.dynamic_slice_in_dim(padded, sub_index, 3, axis=1)
        before, mine, after = near[:, 0], near[:, 1], near[:, 2]
        pieces = [jnp.where(even, after, before), jnp.where(even, before, after)]
        for colour in range(2, 6):
            pieces.append(jnp.stack([mine[:, t] for t in lookup[colour - 2]], axis=1))
        other = jnp.stack(pieces, axis=2)
        mine = jnp.broadcast_to(mine[:, :, None], other.shape)
        factors = jnp.concatenate([mine, other], axis=-1)
        out = jnp.einsum("lscm,msck->lsck", factors, basis, precision=PRECISE)
        return out.reshape(loads, subs, interface)

    def direction(residual, c_res, c_scaled, power):
        y = solve(c_res)
        my = jnp.einsum("lb,ab->la", y, middle, precision=PRECISE)
        energy = 0.5 * power - 2.0 * jnp.sum(y * c_scaled, axis=1, keepdims=True)
        energy = energy + jnp.sum(y * my, axis=1, keepdims=True)
        t = solve(c_scaled - my)
        return precond * (residual - lifted(y)) - lifted(t), energy

    scaled = precond * residual
    (c_res, c_scaled), (power,) = shared([coarse(residual), coarse(scaled), dots(residual, scaled)])
    search, energy = direction(residual, c_res, c_scaled, power)
    multipliers = None
    for iteration in range(ITERS):
        by_rows = jnp.einsum(
            "sij,lsj->lsi",
            schur_block,
            lax.all_gather(search, "crs", axis=0, tiled=True),
            precision=SPLIT,
        )
        product = lax.all_to_all(by_rows, "crs", split_axis=0, concat_axis=2, tiled=True)
        image = usable * (product - partner(product))
        last = iteration + 1 == ITERS
        curve = dots(search, product)
        if last:
            (c_image,), (curve,) = shared([coarse(image), curve])
        else:
            scaled_image = precond * image
            parts = [
                coarse(image),
                coarse(scaled_image),
                curve,
                dots(residual, scaled_image),
                dots(image, scaled_image),
            ]
            (c_image, c_scaled_image), (curve, cross, square) = shared(parts)
        step = energy / curve
        moved = step[:, :, None] * search
        multipliers = moved if multipliers is None else multipliers + moved
        residual = residual - step[:, :, None] * image
        c_res = c_res - step * c_image
        if last:
            projected = residual - lifted(solve(c_res))
        else:
            c_scaled = c_scaled - step * c_scaled_image
            power = power - 2.0 * step * cross + step * step * square
            fresh, energy_new = direction(residual, c_res, c_scaled, power)
            search = fresh + (energy_new / energy)[:, :, None] * search
            energy = energy_new
    return (multipliers, projected)


MESH = pl.DeviceIdType.MESH
F32 = jnp.float32
BF16 = jnp.bfloat16
NSUB = 8
NCRS = 4


def across_rows(a, b):
    return lax.dot_general(a, b, (((1,), (1,)), ((), ())), preferred_element_type=F32)


def along(a, b):
    return jnp.dot(a, b, preferred_element_type=F32)


def halves(x):
    high = x.astype(BF16)
    return high, (x - high.astype(F32)).astype(BF16)


def stacked(x):
    high = x.astype(BF16).astype(F32)
    return jnp.concatenate([high, x - high], axis=0).astype(BF16)


def folded(x):
    rows = x.shape[0] // 2
    return x[:rows] + x[rows:]


def by_two(product, x, pair):
    both = stacked(x)
    return folded(product(both, pair[0]) + product(both, pair[1]))


def near_of(block):
    low = block - 1 if block % 2 == 0 else block + 1
    return block ^ 1, (low if 0 <= low < NSUB else None)


def remote(src, dst, send, recv, target):
    return pltpu.make_async_remote_copy(
        src_ref=src,
        dst_ref=dst,
        send_sem=send,
        recv_sem=recv,
        device_id=target,
        device_id_type=MESH,
    )


class Place:
    def __init__(self):
        self.me = me = lax.axis_index("sub")
        self.q = q = lax.axis_index("crs")
        core = q % 2
        self.twin = q + 1 - 2 * core
        self.far = (q + 2) % NCRS
        self.diagonal = (self.twin + 2) % NCRS
        odd = me % 2
        self.first = me + 1 - 2 * odd
        self.second = me - 1 + 2 * odd
        self.has_second = jnp.logical_and(self.second >= 0, self.second < NSUB)

    def faces(self, src, dst, send, recv):
        return (
            remote(src(0), dst.at[0], send.at[0], recv.at[0], (self.first, self.q)),
            remote(src(1), dst.at[1], send.at[1], recv.at[1], (self.second, self.q)),
        )

    def start_faces(self, copies):
        copies[0].start()

        @pl.when(self.has_second)
        def _():
            copies[1].start()

    def wait_faces(self, copies):
        copies[0].wait()

        @pl.when(self.has_second)
        def _():
            copies[1].wait()

    def everywhere(self, src, gat, send, recv):
        def copy(k, block):
            return remote(
                src, gat.at[block], send.at[k], recv.at[k], ((self.me + k) % NSUB, self.q)
            )

        def start():
            for k in range(1, NSUB):
                copy(k, self.me).start()

        def wait():
            for k in range(1, NSUB):
                copy(k, (self.me + NSUB - k) % NSUB).wait_recv()
            for k in range(1, NSUB):
                copy(k, self.me).wait_send()

        return start, wait


def chunk_size(p):
    return 5 if p == 3 else 7


def operate(at, packed, hold, res, product, buffers):
    gath, gsend, grecv, asend, arecv = buffers
    me, q = at.me, at.q
    rows = hold.shape[2]
    loads = packed.shape[2]

    def to_far(p, n, block):
        return remote(
            packed.at[p, pl.ds(0, n)],
            gath.at[p, block, pl.ds(0, n)],
            gsend.at[1, p],
            grecv.at[1, p],
            (me, at.far),
        )

    def to_twin(p, n, block):
        return remote(
            packed.at[p, pl.ds(0, n)],
            gath.at[p, block, pl.ds(0, n)],
            gsend.at[0, p],
            grecv.at[0, p],
            (me, at.twin),
        )

    def relay(p, n, source, block):
        return remote(
            gath.at[p, source, pl.ds(0, n)],
            gath.at[p, block, pl.ds(0, n)],
            gsend.at[2, p],
            grecv.at[2, p],
            (me, at.twin),
        )

    for p in range(4):
        n = chunk_size(p)
        to_far(p, n, q).start()
        to_twin(p, n, q).start()
    for p in range(4):
        n = chunk_size(p)
        gath[p, q, 0:n] = packed[p, 0:n]

    def sized(p, action):
        @pl.when(p < 3)
        def _():
            action(7)

        @pl.when(p == 3)
        def _():
            action(5)

    def forward(p, n):
        to_far(p, n, at.far).wait_recv()
        relay(p, n, at.far, at.far).start()

    def arrived(p, n):
        to_twin(p, n, at.twin).wait_recv()
        relay(p, n, at.far, at.diagonal).wait_recv()

    peers = (at.twin, at.far, at.diagonal)

    def pieces(owner, p):
        if owner == 0:
            return [(lambda b: res.at[:, p, b], product.at[:, p, :, 0:384], 0, None)]
        if owner == 1:
            return [
                (lambda b: res.at[0, p, b], product.at[0, p, :, 384:768], 0, None),
                (lambda b: res.at[1, p, b, :, 0:128], product.at[1, p, :, 384:512], 1, None),
            ]
        odd = p % 2 == 1
        if owner == 2:
            source = lambda b: res.at[:, p - 1, b, :, 256:384]
            return [(source, product.at[:, p - 1, :, 1024:1152], 0, odd)]
        source = lambda b: res.at[:, p - 1, b, :, 0:128]
        inner = lambda b: res.at[:, 1, b, :, 128:384]
        return [
            (source, product.at[:, p - 1, :, 1152:1280], 0, odd),
            (inner, product.at[:, 1, :, 1280:1536], 1, p == 2),
        ]

    def give(piece, p, j):
        source, target, i, _ = piece
        return remote(
            source(peers[j]), target, asend.at[j, p, i], arecv.at[q, p, i], (me, peers[j])
        )

    def guarded(condition, action):
        if condition is None or condition is True:
            action()
        elif condition is not False:
            pl.when(condition)(action)

    def send_back(p):
        for owner in range(NCRS):

            @pl.when(q == owner)
            def _():
                for n, piece in enumerate(pieces(owner, p)):

                    def action():
                        if owner == 1 and n == 0:
                            res[0, p, :, :, 128:384] = (
                                res[0, p, :, :, 128:384] - res[1, p, :, :, 128:384]
                            )
                        if owner == 2:
                            res[:, p - 1, :, :, 256:384] = (
                                res[:, p - 1, :, :, 256:384] - res[:, p, :, :, 256:384]
                            )
                        if owner == 3 and n == 0:
                            res[:, p - 1, :, :, 0:128] = (
                                res[:, p - 1, :, :, 0:128] - res[:, p, :, :, 0:128]
                            )
                        if owner == 3 and n == 1:
                            res[:, 1, :, :, 128:384] = (
                                res[:, 1, :, :, 128:384] - res[:, 2, :, :, 128:384]
                            )
                        for j in range(3):
                            give(piece, p, j).start()
                        source, target, _, _ = piece
                        target[...] = source(owner)[...]

                    guarded(piece[3], action)

    forward(0, 7)

    def multiply(p, carry):
        @pl.when(p < 3)
        def _():
            sized(p + 1, lambda n: forward(p + 1, n))

        sized(p, lambda n: arrived(p, n))
        sign = (1 - 2 * (p % 2)).astype(F32)
        last = jnp.where(p == 1, 1, jnp.where(p == 2, -1, 0)).astype(F32)
        even = p - p % 2
        held = jnp.where(p == 0, 0, 1)

        def block(chunk, j):
            return gath[chunk, :, j].reshape(NCRS * loads, 256)

        for y in range(2):
            middle = block(p, 4)
            x_a = jnp.concatenate(
                [block(p, 2 * y), block(p, 2 * y + 1), middle if y == 0 else -middle], axis=1
            )
            x_b = jnp.concatenate(
                [sign * block(even, 5 + y), last * block(held, 5 + y)], axis=1
            )
            x_a, x_b = stacked(x_a), stacked(x_b)
            high_a, low_a = halves(hold[y, p, :, 0:768])
            high_b, low_b = halves(hold[y, p, :, 1024:1536])
            n = NCRS * loads
            both = across_rows(x_a, high_a) + across_rows(x_b, high_b)
            out = folded(both) + across_rows(x_a[:n], low_a) + across_rows(x_b[:n], low_b)
            res[y, p] = out.reshape(NCRS, loads, rows)
        send_back(p)
        return carry

    lax.fori_loop(0, 4, multiply, 0)

    for owner in range(NCRS):

        @pl.when(q != owner)
        def _():
            for p in range(4):
                for piece in pieces(owner, p):
                    if piece[3] is None or piece[3]:
                        _, target, i, _ = piece
                        remote(
                            target, target, asend.at[0, p, i], arecv.at[owner, p, i], (me, at.twin)
                        ).wait_recv()

    def drain():
        for p in range(4):
            n = chunk_size(p)
            to_far(p, n, q).wait_send()
            to_twin(p, n, q).wait_send()
            relay(p, n, at.far, at.far).wait_send()
        for owner in range(NCRS):

            @pl.when(q == owner)
            def _():
                for p in range(4):
                    for piece in pieces(owner, p):
                        if piece[3] is None or piece[3]:
                            for j in range(3):
                                give(piece, p, j).wait_send()

    return drain


def inner_partner(c, s):
    if c == 2:
        return s ^ 4
    if c == 4:
        return s ^ 1
    return s ^ 3 if s % 4 in (1, 2) else None


def main_kernel(names, schur, modes_in, inverse_in, rhs_in, stiff_in, length_in, *refs):
    mult_out, proj_out = refs[:2]
    k = dict(zip(names, refs[2:], strict=True))
    loads, subs, interface = rhs_in.shape
    slot = interface // 6
    modes = modes_in.shape[0]
    at = Place()
    me, q = at.me, at.q
    hold, load_sem = k["hold"], k["load_sem"]

    def lanes(c):
        return slice(c * slot, (c + 1) * slot)

    def load(s):
        return pltpu.make_async_copy(
            schur.at[s], hold.at[s // 4, s % 4], load_sem.at[s]
        )

    for s in range(subs):
        load(s).start()

    barrier = pltpu.get_barrier_semaphore()
    for j in range(1, NSUB):
        pl.semaphore_signal(
            barrier, inc=1, device_id=((me + j) % NSUB, q), device_id_type=MESH
        )
    for j in range(1, NCRS):
        pl.semaphore_signal(barrier, inc=1, device_id=(me, (q + j) % NCRS), device_id_type=MESH)

    edges, across = k["edges"], k["across"]
    for c in range(2):
        edges[c, 0:loads] = rhs_in[:, :, lanes(c)]
        edges[c, loads : loads + modes] = modes_in[:, :, lanes(c)]
        edges[c, loads + modes] = stiff_in[:, lanes(c)]
    pl.semaphore_wait(barrier, NSUB + NCRS - 2)

    begin = at.faces(lambda c: edges.at[c], across, k["bsend"], k["brecv"])
    at.start_faces(begin)
    inverse, isend, irecv = k["inverse"], k["isend"], k["irecv"]

    def inverse_far(block):
        return remote(inverse_in, inverse.at[block], isend.at[1], irecv.at[1], (me, at.far))

    def inverse_twin(block):
        return remote(inverse_in, inverse.at[block], isend.at[0], irecv.at[0], (me, at.twin))

    def inverse_relay(block):
        return remote(
            inverse.at[at.far], inverse.at[block], isend.at[2], irecv.at[2], (me, at.twin)
        )

    inverse_far(q).start()
    inverse_twin(q).start()
    inverse[q] = inverse_in[...]

    @pl.when(jnp.logical_not(at.has_second))
    def _():
        across[1] = jnp.zeros(across.shape[1:], F32)

    wide, rhs, mask, precond = k["wide"], k["rhs"], k["mask"], k["precond"]
    position = lax.broadcasted_iota(jnp.int32, (subs, slot), 1)
    for c in range(6):
        mask[:, lanes(c)] = (length_in[:, c : c + 1] > position).astype(F32)
    blank = jnp.zeros((8 - modes, interface), F32)
    for s in range(subs):
        rhs[s] = rhs_in[:, s, :]
        wide[s] = jnp.concatenate([modes_in[:, s, :], blank], axis=0)
    precond[:, lanes(3)] = jnp.zeros((subs, slot), F32)
    for c in (2, 4, 5):
        other = jnp.concatenate(
            [
                stiff_in[t : t + 1, lanes(c)]
                for t in [inner_partner(c, s) or 0 for s in range(subs)]
            ],
            axis=0,
        )
        precond[:, lanes(c)] = mask[:, lanes(c)] * (stiff_in[:, lanes(c)] + other)

    high, low = k["basis_high"], k["basis_low"]

    def put(s, rows, window, value):
        a, b = halves(value)
        high[s, rows, window] = a
        low[s, rows, window] = b

    zero = jnp.zeros((8, slot), F32)
    for s in range(subs):
        inner = {}
        for c in (2, 4, 5):
            t = inner_partner(c, s)
            inner[c] = zero if t is None else -mask[s : s + 1, lanes(c)] * wide[t, :, lanes(c)]
        for c in range(6):
            upper = inner[2] if c == 2 else zero
            if c >= 2:
                put(s, slice(16, 32), lanes(c), jnp.concatenate([zero, upper], axis=0))
                own = mask[s : s + 1, lanes(c)] * wide[s, :, lanes(c)]
                put(s, slice(0, 16), lanes(c), jnp.concatenate([own, zero], axis=0))
            last = jnp.concatenate(
                [inner[4] if c == 4 else zero, inner[5] if c == 5 else zero], axis=0
            )
            put(s, slice(32, 48), lanes(c), last)

    at.wait_faces(begin)
    residual = k["residual"]
    for c in range(2):
        precond[:, lanes(c)] = mask[:, lanes(c)] * (
            stiff_in[:, lanes(c)] + across[c, loads + modes]
        )
    small = jnp.zeros((8 - modes, slot), F32)
    for s in range(subs):
        for c in range(2):
            line = mask[s : s + 1, lanes(c)]
            residual[s, :, lanes(c)] = line * (rhs[s, :, lanes(c)] - across[c, 0:loads, s, :])
            own = line * wide[s, :, lanes(c)]
            outer = -line * jnp.concatenate(
                [across[c, loads : loads + modes, s, :], small], axis=0
            )
            put(
                s,
                slice(0, 16),
                lanes(c),
                jnp.concatenate([own, outer if c == 0 else zero], axis=0),
            )
            put(
                s,
                slice(16, 32),
                lanes(c),
                jnp.concatenate([outer if c == 1 else zero, zero], axis=0),
            )
        residual[s, :, lanes(3)] = jnp.zeros((loads, slot), F32)
        for c in (2, 4, 5):
            t = inner_partner(c, s)
            residual[s, :, lanes(c)] = mask[s : s + 1, lanes(c)] * (
                rhs[s, :, lanes(c)] - rhs[0 if t is None else t, :, lanes(c)]
            )

    middle_msg, middle_all = k["middle_msg"], k["middle_all"]
    middle_msg[...] = jnp.zeros(middle_msg.shape, F32)
    for s in range(subs):
        weighted = wide[s] * precond[s : s + 1]
        block = by_two(across_rows, weighted, (high[s], low[s]))
        line, first = 8 * (s % 4), 64 * (s // 4)
        middle_msg[line : line + 8, first : first + 48] = block
    start_middle, wait_middle = at.everywhere(
        middle_msg, middle_all, k["msend"], k["mrecv"]
    )
    start_middle()
    middle_all[me] = middle_msg[...]

    gats = [(k[f"gat{n}"], k[f"esend{n}"], k[f"erecv{n}"], k[f"msg{n}"]) for n in range(4)]

    def coarse(msg, vector, tiles, scaled):
        for s in range(subs):
            v = vector[s]
            if scaled:
                v = jnp.concatenate([v, precond[s : s + 1] * v], axis=0)
            out = by_two(across_rows, v, (high[s, 0:32], low[s, 0:32]))
            for t in range(tiles):
                part = out[:, 8 * t : 8 * t + 8]
                msg[t, :, 8 * s : 8 * s + 8] = part[:loads]
                if scaled:
                    msg[t, :, 64 + 8 * s : 72 + 8 * s] = part[loads:]

    lane = lax.broadcasted_iota(jnp.int32, (loads, 128), 1)
    gat, esend, erecv, msg = gats[0]
    coarse(msg, residual, 1, True)
    start, wait_first = at.everywhere(msg, gat, esend, erecv)
    start()
    gat[me] = msg[...]

    inverse_far(at.far).wait_recv()
    inverse_relay(at.far).start()
    order = NSUB * 64
    full_order = NSUB * subs * modes
    row = lax.broadcasted_iota(jnp.int32, (order, full_order), 0)
    column = lax.broadcasted_iota(jnp.int32, (order, full_order), 1)
    widen = jnp.where((row % 8 < modes) & (row // 8 * modes + row % 8 == column), 1.0, 0.0)
    widen = widen.astype(BF16)
    row = lax.broadcasted_iota(jnp.int32, (order, 192), 0)
    column = lax.broadcasted_iota(jnp.int32, (order, 192), 1)
    s_of, j_of, n_of = row // 64, row // 8 % 8, row % 8
    source = jnp.where(j_of == 3, s_of ^ 4, jnp.where(j_of == 4, s_of ^ 1, s_of))
    source = jnp.where(j_of == 5, s_of ^ 3, source)
    wanted = jnp.where(j_of <= 2, 64 * j_of, 0) + 8 * source + n_of
    choose = jnp.where((j_of <= 5) & (wanted == column), 1.0, 0.0).astype(BF16)
    inverse_twin(at.twin).wait_recv()
    inverse_relay(at.diagonal).wait_recv()
    all_rows = inverse[...].reshape(full_order, full_order)
    present = at.has_second.astype(F32)
    there = jnp.where(at.has_second, at.second, 0)
    for part, whole, chosen in zip(
        halves(all_rows), (k["q_high"], k["q_low"]), (k["near_high"], k["near_low"])
    ):
        tall = along(widen, part).astype(BF16)
        whole[...] = across_rows(tall, widen).astype(BF16)
        near = jnp.concatenate(
            [
                whole[pl.ds(pl.multiple_of(64 * me, 64), 64), :].astype(F32),
                whole[pl.ds(pl.multiple_of(64 * at.first, 64), 64), :].astype(F32),
                present * whole[pl.ds(pl.multiple_of(64 * there, 64), 64), :].astype(F32),
            ],
            axis=0,
        ).astype(BF16)
        chosen[...] = along(choose, near).astype(BF16)
    q_pair = (k["q_high"], k["q_low"])
    near_pair = (k["near_high"], k["near_low"])
    m_pair = (k["m_high"], k["m_low"])
    for ref in m_pair:
        ref[...] = jnp.zeros(ref.shape, BF16)
    inverse_far(q).wait_send()
    inverse_twin(q).wait_send()
    inverse_relay(at.far).wait_send()

    wait_middle()
    row = lax.broadcasted_iota(jnp.int32, (64, 384), 0)
    column = lax.broadcasted_iota(jnp.int32, (64, 384), 1)
    spread = jnp.where(row == column // 64 * 8 + column % 8, 1.0, 0.0).astype(BF16)
    row = lax.broadcasted_iota(jnp.int32, (64, 64), 0) // 8
    column = lax.broadcasted_iota(jnp.int32, (64, 64), 1) // 8
    same = (row == column).astype(F32)
    inner_masks = [(row ^ flip == column).astype(F32) for flip in (4, 1, 3)]
    compact = [middle_all[t, :, 64 * h : 64 * h + 64] for t in range(NSUB) for h in range(2)]
    for part, whole in zip(halves(jnp.concatenate(compact, axis=0)), m_pair):
        wide_part = along(part, spread)
        for t in range(NSUB):
            piece = wide_part[64 * t : 64 * t + 64]
            own = same * piece[:, 0:64]
            for j in range(3):
                own = own + inner_masks[j] * piece[:, 64 * (j + 3) : 64 * (j + 4)]
            first, second = near_of(t)
            whole[64 * t : 64 * t + 64, 64 * t : 64 * t + 64] = own.astype(BF16)
            whole[64 * t : 64 * t + 64, 64 * first : 64 * first + 64] = (
                same * piece[:, 64:128]
            ).astype(BF16)
            if second is not None:
                whole[64 * t : 64 * t + 64, 64 * second : 64 * second + 64] = (
                    same * piece[:, 128:192]
                ).astype(BF16)

    def pair_of(pair):
        return pair[0][...], pair[1][...]

    def joined(tiles, half):
        return jnp.concatenate([t[:, 64 * half : 64 * half + 64] for t in tiles], axis=1)

    def lift_of(coefficients, s):
        part = coefficients[:, 64 * s : 64 * s + 48]
        return by_two(along, part, (high[s], low[s]))

    packed = k["packed"]

    def pack(value, s):
        y, z = s // 4, s % 4
        packed[z, 2 * y] = value[:, lanes(0)]
        packed[z, 2 * y + 1] = value[:, lanes(1)]
        if y == 0:
            packed[z, 4] = value[:, lanes(2)]
        if z % 2 == 0:
            packed[z, 5 + y] = value[:, lanes(4)]
        if z == 1:
            packed[z, 5 + y] = value[:, lanes(5)]

    def direction(c_res, c_scaled, target):
        y = by_two(across_rows, c_res, pair_of(q_pair))
        c_scaled = c_scaled - by_two(across_rows, y, pair_of(m_pair))
        both = jnp.concatenate([c_res, c_scaled], axis=0)
        near = by_two(across_rows, both, pair_of(near_pair))
        total = jnp.zeros((loads, interface), F32)
        for s in range(subs):
            lifted = lift_of(near, s)
            projected = residual[s] - lifted[:loads]
            scaled = precond[s : s + 1] * projected
            total = total + projected * scaled
            value = scaled - lifted[loads:]
            target[s] = value
            pack(value, s)
        return 0.5 * jnp.sum(total, axis=1, keepdims=True)

    wait_first()
    tiles = [gat[t, 0] for t in range(NSUB)]
    c_res, c_scaled = joined(tiles, 0), joined(tiles, 1)
    search, fresh = k["search"], k["fresh"]
    partial = direction(c_res, c_scaled, search)
    for s in range(subs):
        load(s).wait()
    product = k["product"]
    image = [k["image0"], k["image1"]]

    def mixed(target, s):
        y, z = s // 4, s % 4
        for c in range(2):
            target[s, :, lanes(c)] = mask[s : s + 1, lanes(c)] * product[y, z, :, lanes(c)]
        target[s, :, lanes(3)] = jnp.zeros((loads, slot), F32)
        for c in (2, 4, 5):
            t = inner_partner(c, s)
            if t is None:
                target[s, :, lanes(c)] = jnp.zeros((loads, slot), F32)
                continue
            owner = min(s, t)
            value = mask[s : s + 1, lanes(c)] * product[owner // 4, owner % 4, :, lanes(c)]
            target[s, :, lanes(c)] = value if s == owner else -value

    def finish_image(target, arriving):
        for s in range(subs):
            for c in range(2):
                target[s, :, lanes(c)] = (
                    target[s, :, lanes(c)] - mask[s : s + 1, lanes(c)] * arriving[c, s]
                )

    def curve_of(direct, values):
        total = jnp.zeros((loads, 2 * slot), F32)
        inner = jnp.zeros((loads, 4 * slot), F32)
        for s in range(subs):
            total = total + direct[s, :, 0 : 2 * slot] * values[s, :, 0 : 2 * slot]
            inner = inner + direct[s, :, 2 * slot :] * values[s, :, 2 * slot :]
        total = jnp.sum(total, axis=1, keepdims=True)
        return total + 0.5 * jnp.sum(inner, axis=1, keepdims=True)

    def no_second():
        for n in range(2):
            k[f"arriving{n}"][1] = jnp.zeros(k[f"arriving{n}"].shape[1:], F32)

    pl.when(jnp.logical_not(at.has_second))(no_second)

    def gathered(gat, scaled):
        tiles = []
        for t in range(NSUB):
            first, second = near_of(t)
            if scaled:
                tile = gat[t, 0] + gat[first, 1]
                if second is not None:
                    tile = tile + gat[second, 2]
            else:
                tile = gat[t, 0][:, 0:64] + gat[first, 1][:, 0:64]
                if second is not None:
                    tile = tile + gat[second, 2][:, 0:64]
            tiles.append(tile)
        return tiles

    def summed(gat, at_lane):
        total = gat[0, 0]
        for t in range(1, NSUB):
            total = total + gat[t, 0]
        return [total[:, n : n + 1] for n in at_lane]

    buffers = [k[f"op0_{n}"] for n in range(5)]
    drain_first = operate(at, packed, hold, k["res"], product, buffers)
    for s in range(subs):
        mixed(image[0], s)
    copies_0 = at.faces(
        lambda c: image[0].at[:, :, lanes(c)], k["arriving0"], k["fsend0"], k["frecv0"]
    )
    at.start_faces(copies_0)
    gat, esend, erecv, msg = gats[1]
    coarse(msg, image[0], 3, True)
    curve = curve_of(search, image[0])
    msg[0] = jnp.where(lane == 6, curve, jnp.where(lane == 7, partial, msg[0]))
    start, wait = at.everywhere(msg, gat, esend, erecv)
    start()
    gat[me] = msg[...]
    drain_first()
    at.wait_faces(copies_0)
    finish_image(image[0], k["arriving0"])
    wait()
    tiles = gathered(gat, True)
    curve, energy = summed(gat, (6, 7))
    step_0 = energy / curve
    c_res = c_res - step_0 * joined(tiles, 0)
    c_scaled = c_scaled - step_0 * joined(tiles, 1)
    for s in range(subs):
        residual[s] = residual[s] - step_0 * image[0][s]
    partial = direction(c_res, c_scaled, fresh)

    gat_e, esend, erecv, msg = gats[2]
    msg[0] = jnp.broadcast_to(partial, (loads, 128))
    start, wait_energy = at.everywhere(msg, gat_e, esend, erecv)
    buffers = [k[f"op1_{n}"] for n in range(5)]
    start()
    gat_e[me] = msg[...]
    drain_second = operate(at, packed, hold, k["res"], product, buffers)
    wait_energy()
    ratio = summed(gat_e, (0,))[0] / energy
    for s in range(subs):
        mixed(image[1], s)
        for c in range(2):
            before = image[0][s, :, lanes(c)] + mask[s : s + 1, lanes(c)] * k["arriving0"][c, s]
            image[1][s, :, lanes(c)] = image[1][s, :, lanes(c)] + ratio * before
        at_rest = slice(2 * slot, interface)
        image[1][s, :, at_rest] = image[1][s, :, at_rest] + ratio * image[0][s, :, at_rest]
    copies_1 = at.faces(
        lambda c: image[1].at[:, :, lanes(c)], k["arriving1"], k["fsend1"], k["frecv1"]
    )
    at.start_faces(copies_1)
    for s in range(subs):
        fresh[s] = fresh[s] + ratio * search[s]
    gat, esend, erecv, msg = gats[3]
    coarse(msg, image[1], 3, False)
    curve = curve_of(fresh, image[1])
    msg[0] = jnp.where(lane == 6, curve, msg[0])
    start, wait = at.everywhere(msg, gat, esend, erecv)
    start()
    gat[me] = msg[...]
    energy = summed(gat_e, (0,))[0]
    drain_second()
    at.wait_faces(copies_1)
    finish_image(image[1], k["arriving1"])
    wait()
    tiles = gathered(gat, False)
    step_1 = energy / summed(gat, (6,))[0]
    c_res = c_res - step_1 * jnp.concatenate(tiles, axis=1)
    near = by_two(across_rows, c_res, pair_of(near_pair))
    for s in range(subs):
        mult_out[:, s, :] = step_0 * search[s] + step_1 * fresh[s]
        proj_out[:, s, :] = residual[s] - step_1 * image[1][s] - lift_of(near, s)


def by_kernels(schur_block, rigid_modes, coarse_inverse, dual_rhs, stiff_diag, face_length):
    loads, subs, interface = dual_rhs.shape
    rows = schur_block.shape[1]
    slot = interface // 6
    modes = rigid_modes.shape[1]
    vmem = pl.BlockSpec(memory_space=pltpu.VMEM)
    anywhere = pl.BlockSpec(memory_space=pl.ANY)
    dma = pltpu.SemaphoreType.DMA
    order = NSUB * 64
    vector = pltpu.VMEM((subs, loads, interface), F32)
    edge = pltpu.VMEM((2, loads + modes + 1, subs, slot), F32)
    face = pltpu.VMEM((2, subs, loads, slot), F32)
    basis = pltpu.VMEM((subs, 48, interface), BF16)
    square = pltpu.VMEM((order, order), BF16)
    scratch = {
        "hold": pltpu.VMEM((2, subs // 2, rows, interface), F32),
        "load_sem": dma((subs,)),
        "edges": edge,
        "across": edge,
        "bsend": dma((2,)),
        "brecv": dma((2,)),
        "inverse": pltpu.VMEM((NCRS,) + coarse_inverse.shape, F32),
        "isend": dma((3,)),
        "irecv": dma((3,)),
        "wide": pltpu.VMEM((subs, 8, interface), F32),
        "rhs": vector,
        "mask": pltpu.VMEM((subs, interface), F32),
        "precond": pltpu.VMEM((subs, interface), F32),
        "basis_high": basis,
        "basis_low": basis,
        "residual": vector,
        "middle_msg": pltpu.VMEM((32, 128), F32),
        "middle_all": pltpu.VMEM((NSUB, 32, 128), F32),
        "msend": dma((NSUB,)),
        "mrecv": dma((NSUB,)),
        "q_high": square,
        "q_low": square,
        "near_high": square,
        "near_low": square,
        "m_high": square,
        "m_low": square,
        "packed": pltpu.VMEM((4, 7, loads, slot), F32),
        "search": vector,
        "fresh": vector,
        "product": pltpu.VMEM((2, subs // 2, loads, interface), F32),
        "image0": vector,
        "image1": vector,
        "res": pltpu.VMEM((2, subs // 2, NCRS, loads, rows), F32),
    }
    for n, tiles in enumerate((1, 3, 1, 3)):
        scratch[f"msg{n}"] = pltpu.VMEM((tiles, loads, 128), F32)
        scratch[f"gat{n}"] = pltpu.VMEM((NSUB, tiles, loads, 128), F32)
        scratch[f"esend{n}"] = dma((NSUB,))
        scratch[f"erecv{n}"] = dma((NSUB,))
    for n in range(ITERS):
        scratch[f"op{n}_0"] = pltpu.VMEM((4, NCRS, 7, loads, slot), F32)
        scratch[f"op{n}_1"] = dma((3, 4))
        scratch[f"op{n}_2"] = dma((3, 4))
        scratch[f"op{n}_3"] = dma((3, 4, 2))
        scratch[f"op{n}_4"] = dma((NCRS, 4, 2))
        scratch[f"arriving{n}"] = face
        scratch[f"fsend{n}"] = dma((2,))
        scratch[f"frecv{n}"] = dma((2,))
    out = jax.ShapeDtypeStruct((loads, subs, interface), F32)
    return pl.pallas_call(
        functools.partial(main_kernel, list(scratch)),
        out_shape=(out, out),
        in_specs=[anywhere] + [vmem] * 5,
        out_specs=(vmem, vmem),
        scratch_shapes=list(scratch.values()),
        compiler_params=pltpu.CompilerParams(
            collective_id=0, has_side_effects=True, vmem_limit_bytes=56 * 1024 * 1024
        ),
        name="main",
    )(
        schur_block,
        jnp.swapaxes(rigid_modes, 0, 1),
        coarse_inverse,
        dual_rhs,
        stiff_diag,
        face_length,
    )


def shards(schur_block, rigid_modes, coarse_inverse, dual_rhs, stiff_diag, face_length):
    fits = dual_rhs.shape[0] == 8 and lax.axis_size("crs") == NCRS and lax.axis_size("sub") == NSUB
    build = by_kernels if fits else by_collectives
    return build(schur_block, rigid_modes, coarse_inverse, dual_rhs, stiff_diag, face_length)


def solution(mesh):
    return jax.shard_map(
        shards,
        mesh=mesh,
        in_specs=(
            P("sub", "crs", None),
            P("sub", None, None),
            P("crs", None),
            P("crs", "sub", None),
            P("sub", None),
            P("sub", None),
        ),
        out_specs=(P("crs", "sub", None), P("crs", "sub", None)),
        check_vma=False,
    )
```

```python
import functools

import jax
import jax.numpy as jnp
import numpy as np
from jax import lax
from jax.experimental import pallas as pl
from jax.experimental.pallas import tpu as pltpu
from jax.sharding import PartitionSpec as P

ITERS = 2
SY = 2
SZ = 4
SUBS = 8

PRECISE = lax.Precision.HIGHEST
SPLIT = lax.Precision.HIGH


def local_lookup():
    indices = np.arange(SUBS)
    coords = [indices // SZ, indices % SZ]
    extent = [SY, SZ]
    stride = [SZ, 1]
    lookup = np.zeros((4, SUBS), np.int32)
    for colour in range(4):
        axis_pick = colour // 2
        anchor = coords[axis_pick]
        offset = np.where(anchor % 2 == colour % 2, 1, -1)
        target = anchor + offset
        inside = (target >= 0) & (target < extent[axis_pick])
        lookup[colour] = np.where(inside, indices + offset * stride[axis_pick], indices)
    return lookup


def by_collectives(schur_block, rigid_modes, coarse_inverse, dual_rhs, stiff_diag, face_length):
    loads, subs, interface = dual_rhs.shape
    slot = interface // 6
    modes = rigid_modes.shape[1]
    own = subs * modes
    nsub = lax.axis_size("sub")
    sub_index = lax.axis_index("sub")
    even = sub_index % 2 == 0
    lookup = local_lookup()
    positions = jnp.arange(interface) % slot
    usable = (jnp.repeat(face_length, slot, axis=1) > positions[None, :]).astype(jnp.float32)
    up = [(i, i + 1) for i in range(nsub - 1)]
    down = [(i + 1, i) for i in range(nsub - 1)]

    def partner(vector):
        first = vector[..., :slot]
        second = vector[..., slot : 2 * slot]
        from_left = lax.ppermute(jnp.where(even, first, second), "sub", up)
        from_right = lax.ppermute(jnp.where(even, second, first), "sub", down)
        pieces = [jnp.where(even, from_right, from_left), jnp.where(even, from_left, from_right)]
        for colour in range(2, 6):
            window = vector[..., colour * slot : (colour + 1) * slot]
            pieces.append(
                jnp.concatenate([window[..., t : t + 1, :] for t in lookup[colour - 2]], axis=-2)
            )
        return jnp.concatenate(pieces, axis=-1)

    modes_first = jnp.swapaxes(rigid_modes, 0, 1)
    together = jnp.concatenate([dual_rhs, modes_first, stiff_diag[None]], axis=0)
    across = partner(together)
    residual = usable * (dual_rhs - across[:loads])
    modes_across = across[loads : loads + modes]
    precond = usable * (stiff_diag + across[-1])

    inverse = lax.all_gather(coarse_inverse, "crs", axis=0, tiled=True)

    def by_slot(array):
        return array.reshape(array.shape[:-1] + (6, slot))

    basis = by_slot(usable * jnp.concatenate([modes_first, -modes_across], axis=0))

    weighted = by_slot(modes_first * precond)
    blocks = jnp.einsum("msck,nsck->scmn", weighted, basis, precision=PRECISE)
    total_subs = nsub * subs
    here = sub_index * subs + jnp.arange(subs)
    left = here - subs
    right = here + subs
    targets = [jnp.where(even, right, left), jnp.where(even, left, right)]
    for colour in range(2, 6):
        targets.append(sub_index * subs + jnp.asarray(lookup[colour - 2]))
    targets = jnp.stack(targets, axis=1)
    hot_across = (targets[:, :, None] == jnp.arange(total_subs)).astype(jnp.float32)
    hot_here = (here[:, None] == jnp.arange(total_subs)).astype(jnp.float32)
    dense = jnp.einsum("smn,st->smtn", blocks[..., :modes].sum(axis=1), hot_here, precision=PRECISE)
    dense = dense + jnp.einsum("scmn,sct->smtn", blocks[..., modes:], hot_across, precision=PRECISE)
    dense = dense.reshape(own, total_subs * modes)
    middle = lax.all_gather(dense, "sub", axis=0, tiled=True)

    def coarse(vector):
        return jnp.einsum("lsi,msi->lsm", vector, modes_first, precision=PRECISE).reshape(loads, own)

    def dots(a, b):
        return jnp.sum(a * b, axis=(1, 2))[:, None]

    def shared(parts):
        gathered = lax.all_gather(jnp.concatenate(parts, axis=1), "sub", axis=0)
        count = own * (sum(part.shape[1] == own for part in parts))
        outs = []
        for at in range(0, count, own):
            outs.append(jnp.swapaxes(gathered[:, :, at : at + own], 0, 1).reshape(loads, nsub * own))
        sums = jnp.sum(gathered[:, :, count:], axis=0)
        return outs, [sums[:, j : j + 1] for j in range(sums.shape[1])]

    def solve(values):
        return jnp.einsum("lb,ab->la", values, inverse, precision=PRECISE)

    def lifted(values):
        grid = values.reshape(loads, nsub, subs, modes)
        padded = jnp.pad(grid, ((0, 0), (1, 1), (0, 0), (0, 0)))
        near = lax.dynamic_slice_in_dim(padded, sub_index, 3, axis=1)
        before, mine, after = near[:, 0], near[:, 1], near[:, 2]
        pieces = [jnp.where(even, after, before), jnp.where(even, before, after)]
        for colour in range(2, 6):
            pieces.append(jnp.stack([mine[:, t] for t in lookup[colour - 2]], axis=1))
        other = jnp.stack(pieces, axis=2)
        mine = jnp.broadcast_to(mine[:, :, None], other.shape)
        factors = jnp.concatenate([mine, other], axis=-1)
        out = jnp.einsum("lscm,msck->lsck", factors, basis, precision=PRECISE)
        return out.reshape(loads, subs, interface)

    def direction(residual, c_res, c_scaled, power):
        y = solve(c_res)
        my = jnp.einsum("lb,ab->la", y, middle, precision=PRECISE)
        energy = 0.5 * power - 2.0 * jnp.sum(y * c_scaled, axis=1, keepdims=True)
        energy = energy + jnp.sum(y * my, axis=1, keepdims=True)
        t = solve(c_scaled - my)
        return precond * (residual - lifted(y)) - lifted(t), energy

    scaled = precond * residual
    (c_res, c_scaled), (power,) = shared([coarse(residual), coarse(scaled), dots(residual, scaled)])
    search, energy = direction(residual, c_res, c_scaled, power)
    multipliers = None
    for iteration in range(ITERS):
        by_rows = jnp.einsum(
            "sij,lsj->lsi",
            schur_block,
            lax.all_gather(search, "crs", axis=0, tiled=True),
            precision=SPLIT,
        )
        product = lax.all_to_all(by_rows, "crs", split_axis=0, concat_axis=2, tiled=True)
        image = usable * (product - partner(product))
        last = iteration + 1 == ITERS
        curve = dots(search, product)
        if last:
            (c_image,), (curve,) = shared([coarse(image), curve])
        else:
            scaled_image = precond * image
            parts = [
                coarse(image),
                coarse(scaled_image),
                curve,
                dots(residual, scaled_image),
                dots(image, scaled_image),
            ]
            (c_image, c_scaled_image), (curve, cross, square) = shared(parts)
        step = energy / curve
        moved = step[:, :, None] * search
        multipliers = moved if multipliers is None else multipliers + moved
        residual = residual - step[:, :, None] * image
        c_res = c_res - step * c_image
        if last:
            projected = residual - lifted(solve(c_res))
        else:
            c_scaled = c_scaled - step * c_scaled_image
            power = power - 2.0 * step * cross + step * step * square
            fresh, energy_new = direction(residual, c_res, c_scaled, power)
            search = fresh + (energy_new / energy)[:, :, None] * search
            energy = energy_new
    return (multipliers, projected)


MESH = pl.DeviceIdType.MESH
F32 = jnp.float32
BF16 = jnp.bfloat16
NSUB = 8
NCRS = 4


def across_rows(a, b):
    return lax.dot_general(a, b, (((1,), (1,)), ((), ())), preferred_element_type=F32)


def along(a, b):
    return jnp.dot(a, b, preferred_element_type=F32)


def halves(x):
    high = x.astype(BF16)
    return high, (x - high.astype(F32)).astype(BF16)


def stacked(x):
    high = x.astype(BF16).astype(F32)
    return jnp.concatenate([high, x - high], axis=0).astype(BF16)


def folded(x):
    rows = x.shape[0] // 2
    return x[:rows] + x[rows:]


def by_two(product, x, pair):
    both = stacked(x)
    return folded(product(both, pair[0]) + product(both, pair[1]))


def near_of(block):
    low = block - 1 if block % 2 == 0 else block + 1
    return block ^ 1, (low if 0 <= low < NSUB else None)


def remote(src, dst, send, recv, target):
    return pltpu.make_async_remote_copy(
        src_ref=src,
        dst_ref=dst,
        send_sem=send,
        recv_sem=recv,
        device_id=target,
        device_id_type=MESH,
    )


class Place:
    def __init__(self):
        self.me = me = lax.axis_index("sub")
        self.q = q = lax.axis_index("crs")
        core = q % 2
        self.twin = q + 1 - 2 * core
        self.far = (q + 2) % NCRS
        self.diagonal = (self.twin + 2) % NCRS
        odd = me % 2
        self.first = me + 1 - 2 * odd
        self.second = me - 1 + 2 * odd
        self.has_second = jnp.logical_and(self.second >= 0, self.second < NSUB)

    def faces(self, src, dst, send, recv):
        return (
            remote(src(0), dst.at[0], send.at[0], recv.at[0], (self.first, self.q)),
            remote(src(1), dst.at[1], send.at[1], recv.at[1], (self.second, self.q)),
        )

    def start_faces(self, copies):
        copies[0].start()

        @pl.when(self.has_second)
        def _():
            copies[1].start()

    def wait_faces(self, copies):
        copies[0].wait()

        @pl.when(self.has_second)
        def _():
            copies[1].wait()

    def everywhere(self, src, gat, send, recv):
        def copy(k, block):
            return remote(
                src, gat.at[block], send.at[k], recv.at[k], ((self.me + k) % NSUB, self.q)
            )

        def start():
            for k in range(1, NSUB):
                copy(k, self.me).start()

        def wait():
            for k in range(1, NSUB):
                copy(k, (self.me + NSUB - k) % NSUB).wait_recv()
            for k in range(1, NSUB):
                copy(k, self.me).wait_send()

        return start, wait


def chunk_size(p):
    return 5 if p == 3 else 7


def operate(at, packed, hold, res, product, buffers, arriving, fsend, frecv):
    gath, gsend, grecv, asend, arecv = buffers
    me, q = at.me, at.q
    rows = hold.shape[2]
    loads = packed.shape[2]

    def to_far(p, n, block):
        return remote(
            packed.at[p, pl.ds(0, n)],
            gath.at[p, block, pl.ds(0, n)],
            gsend.at[1, p],
            grecv.at[1, p],
            (me, at.far),
        )

    def to_twin(p, n, block):
        return remote(
            packed.at[p, pl.ds(0, n)],
            gath.at[p, block, pl.ds(0, n)],
            gsend.at[0, p],
            grecv.at[0, p],
            (me, at.twin),
        )

    def relay(p, n, source, block):
        return remote(
            gath.at[p, source, pl.ds(0, n)],
            gath.at[p, block, pl.ds(0, n)],
            gsend.at[2, p],
            grecv.at[2, p],
            (me, at.twin),
        )

    def send(p):
        n = chunk_size(p)
        to_far(p, n, q).start()
        to_twin(p, n, q).start()
        gath[p, q, 0:n] = packed[p, 0:n]

    def sized(p, action):
        @pl.when(p < 3)
        def _():
            action(7)

        @pl.when(p == 3)
        def _():
            action(5)

    def forward(p, n):
        to_far(p, n, at.far).wait_recv()
        relay(p, n, at.far, at.far).start()

    def arrived(p, n):
        to_twin(p, n, at.twin).wait_recv()
        relay(p, n, at.far, at.diagonal).wait_recv()

    peers = (at.twin, at.far, at.diagonal)

    def pieces(owner, p):
        if owner == 0:
            return [(lambda b: res.at[:, p, b], product.at[:, p, :, 0:384], 0, None)]
        if owner == 1:
            return [
                (lambda b: res.at[0, p, b], product.at[0, p, :, 384:768], 0, None),
                (lambda b: res.at[1, p, b, :, 0:128], product.at[1, p, :, 384:512], 1, None),
            ]
        odd = p % 2 == 1
        if owner == 2:
            source = lambda b: res.at[:, p - 1, b, :, 256:384]
            return [(source, product.at[:, p - 1, :, 1024:1152], 0, odd)]
        source = lambda b: res.at[:, p - 1, b, :, 0:128]
        inner = lambda b: res.at[:, 1, b, :, 128:384]
        return [
            (source, product.at[:, p - 1, :, 1152:1280], 0, odd),
            (inner, product.at[:, 1, :, 1280:1536], 1, p == 2),
        ]

    def give(piece, p, j):
        source, target, i, _ = piece
        return remote(
            source(peers[j]), target, asend.at[j, p, i], arecv.at[q, p, i], (me, peers[j])
        )

    def guarded(condition, action):
        if condition is None or condition is True:
            action()
        elif condition is not False:
            pl.when(condition)(action)

    def send_back(p):
        for owner in range(NCRS):

            @pl.when(q == owner)
            def _():
                for n, piece in enumerate(pieces(owner, p)):

                    def action():
                        if owner == 1 and n == 0:
                            res[0, p, :, :, 128:384] = (
                                res[0, p, :, :, 128:384] - res[1, p, :, :, 128:384]
                            )
                        if owner == 2:
                            res[:, p - 1, :, :, 256:384] = (
                                res[:, p - 1, :, :, 256:384] - res[:, p, :, :, 256:384]
                            )
                        if owner == 3 and n == 0:
                            res[:, p - 1, :, :, 0:128] = (
                                res[:, p - 1, :, :, 0:128] - res[:, p, :, :, 0:128]
                            )
                        if owner == 3 and n == 1:
                            res[:, 1, :, :, 128:384] = (
                                res[:, 1, :, :, 128:384] - res[:, 2, :, :, 128:384]
                            )
                        for j in range(3):
                            give(piece, p, j).start()
                        source, target, _, _ = piece
                        target[...] = source(owner)[...]

                    guarded(piece[3], action)

    def multiply(p, carry):
        @pl.when(p < 3)
        def _():
            sized(p + 1, lambda n: forward(p + 1, n))

        sized(p, lambda n: arrived(p, n))
        sign = (1 - 2 * (p % 2)).astype(F32)
        last = jnp.where(p == 1, 1, jnp.where(p == 2, -1, 0)).astype(F32)
        even = p - p % 2
        held = jnp.where(p == 0, 0, 1)

        def block(chunk, j):
            return gath[chunk, :, j].reshape(NCRS * loads, 256)

        for y in range(2):
            middle = block(p, 4)
            x_a = jnp.concatenate(
                [block(p, 2 * y), block(p, 2 * y + 1), middle if y == 0 else -middle], axis=1
            )
            x_b = jnp.concatenate(
                [sign * block(even, 5 + y), last * block(held, 5 + y)], axis=1
            )
            x_a, x_b = stacked(x_a), stacked(x_b)
            high_a, low_a = halves(hold[y, p, :, 0:768])
            high_b, low_b = halves(hold[y, p, :, 1024:1536])
            n = NCRS * loads
            both = across_rows(x_a, high_a) + across_rows(x_b, high_b)
            out = folded(both) + across_rows(x_a[:n], low_a) + across_rows(x_b[:n], low_b)
            res[y, p] = out.reshape(NCRS, loads, rows)
        send_back(p)
        return carry

    def run():
        forward(0, 7)
        lax.fori_loop(0, 4, multiply, 0)

    def face(c, p):
        return remote(
            product.at[:, p, :, pl.ds(256 * c, 256)],
            arriving.at[c, :, p],
            fsend.at[c, p],
            frecv.at[c, p],
            (at.second if c else at.first, q),
        )

    def returned(owner, p):
        for piece in pieces(owner, p):
            if piece[3] is None or piece[3]:
                _, target, i, _ = piece
                remote(
                    target, target, asend.at[0, p, i], arecv.at[owner, p, i], (me, at.twin)
                ).wait_recv()

    def settle(p):
        for owner in range(2):
            pl.when(q != owner)(functools.partial(returned, owner, p))
        face(0, p).start()
        pl.when(at.has_second)(face(1, p).start)
        for owner in (2, 3):
            if any(piece[3] for piece in pieces(owner, p)):
                pl.when(q != owner)(functools.partial(returned, owner, p))

    def faces():
        for p in range(4):
            face(0, p).wait()
            pl.when(at.has_second)(face(1, p).wait)

    def drain():
        for p in range(4):
            n = chunk_size(p)
            to_far(p, n, q).wait_send()
            to_twin(p, n, q).wait_send()
            relay(p, n, at.far, at.far).wait_send()
        for owner in range(NCRS):

            @pl.when(q == owner)
            def _():
                for p in range(4):
                    for piece in pieces(owner, p):
                        if piece[3] is None or piece[3]:
                            for j in range(3):
                                give(piece, p, j).wait_send()

    return send, run, settle, drain, faces


def inner_partner(c, s):
    if c == 2:
        return s ^ 4
    if c == 4:
        return s ^ 1
    return s ^ 3 if s % 4 in (1, 2) else None


def main_kernel(names, schur, *refs):
    sources, (mult_out, proj_out) = refs[:5], refs[5:7]
    k = dict(zip(names, refs[7:], strict=True))
    inputs = [k[f"input{n}"] for n in range(5)]
    modes_in, inverse_in, rhs_in, stiff_in, length_in = inputs
    fetches = [
        pltpu.make_async_copy(source, held, k["input_sem"].at[n])
        for n, (source, held) in enumerate(zip(sources, inputs))
    ]
    for copy in fetches:
        copy.start()
    loads, subs, interface = rhs_in.shape
    slot = interface // 6
    modes = modes_in.shape[0]
    at = Place()
    me, q = at.me, at.q
    hold, load_sem = k["hold"], k["load_sem"]

    def lanes(c):
        return slice(c * slot, (c + 1) * slot)

    def load(s):
        return pltpu.make_async_copy(
            schur.at[s], hold.at[s // 4, s % 4], load_sem.at[s]
        )

    barrier = pltpu.get_barrier_semaphore()
    for j in range(1, NSUB):
        pl.semaphore_signal(
            barrier, inc=1, device_id=((me + j) % NSUB, q), device_id_type=MESH
        )
    for j in range(1, NCRS):
        pl.semaphore_signal(barrier, inc=1, device_id=(me, (q + j) % NCRS), device_id_type=MESH)

    for copy in fetches:
        copy.wait()
    edges, across = k["edges"], k["across"]
    for c in range(2):
        edges[c, 0:modes] = modes_in[:, :, lanes(c)]
        edges[c, modes] = stiff_in[:, lanes(c)]
    pl.semaphore_wait(barrier, NSUB + NCRS - 2)

    core = q % 2

    def begin(c):
        target = (at.second if c else at.first, q)
        return remote(edges.at[c], across.at[c], k["bsend"].at[c], k["brecv"].at[c], target)

    def share(c):
        return remote(
            across.at[c], across.at[c], k["tsend"].at[c], k["trecv"].at[c], (me, at.twin)
        )

    pl.when(core == 0)(lambda: begin(0).start())
    pl.when((core == 1) & at.has_second)(lambda: begin(1).start())
    beyond = k["beyond"]
    right = at.faces(lambda c: rhs_in.at[:, :, lanes(c)], beyond, k["rsend"], k["rrecv"])
    at.start_faces(right)
    inverse, isend, irecv = k["inverse"], k["isend"], k["irecv"]

    def inverse_far(block):
        return remote(inverse_in, inverse.at[block], isend.at[1], irecv.at[1], (me, at.far))

    def inverse_twin(block):
        return remote(inverse_in, inverse.at[block], isend.at[0], irecv.at[0], (me, at.twin))

    def inverse_relay(block):
        return remote(
            inverse.at[at.far], inverse.at[block], isend.at[2], irecv.at[2], (me, at.twin)
        )

    inverse_far(q).start()
    inverse_twin(q).start()
    inverse[q] = inverse_in[...]

    @pl.when(jnp.logical_not(at.has_second))
    def _():
        across[1] = jnp.zeros(across.shape[1:], F32)
        beyond[1] = jnp.zeros(beyond.shape[1:], F32)

    wide, rhs, mask, precond = k["wide"], k["rhs"], k["mask"], k["precond"]
    position = lax.broadcasted_iota(jnp.int32, (subs, slot), 1)
    for c in range(6):
        mask[:, lanes(c)] = (length_in[:, c : c + 1] > position).astype(F32)
    blank = jnp.zeros((8 - modes, interface), F32)
    for s in range(subs):
        rhs[s] = rhs_in[:, s, :]
        wide[s] = jnp.concatenate([modes_in[:, s, :], blank], axis=0)
    precond[:, lanes(3)] = jnp.zeros((subs, slot), F32)
    for c in (2, 4, 5):
        other = jnp.concatenate(
            [
                stiff_in[t : t + 1, lanes(c)]
                for t in [inner_partner(c, s) or 0 for s in range(subs)]
            ],
            axis=0,
        )
        precond[:, lanes(c)] = mask[:, lanes(c)] * (stiff_in[:, lanes(c)] + other)

    high, low = k["basis_high"], k["basis_low"]

    def put(s, rows, window, value):
        a, b = halves(value)
        high[s, rows, window] = a
        low[s, rows, window] = b

    zero = jnp.zeros((8, slot), F32)
    for s in range(subs):
        inner = {}
        for c in (2, 4, 5):
            t = inner_partner(c, s)
            inner[c] = zero if t is None else -mask[s : s + 1, lanes(c)] * wide[t, :, lanes(c)]
        for c in range(6):
            upper = inner[2] if c == 2 else zero
            if c >= 2:
                put(s, slice(16, 32), lanes(c), jnp.concatenate([zero, upper], axis=0))
                own = mask[s : s + 1, lanes(c)] * wide[s, :, lanes(c)]
                put(s, slice(0, 16), lanes(c), jnp.concatenate([own, zero], axis=0))
            last = jnp.concatenate(
                [inner[4] if c == 4 else zero, inner[5] if c == 5 else zero], axis=0
            )
            put(s, slice(32, 48), lanes(c), last)


    @pl.when(core == 0)
    def _():
        begin(0).wait()
        share(0).start()
        pl.when(at.has_second)(lambda: share(1).wait_recv())
        share(0).wait_send()

    @pl.when(core == 1)
    def _():
        @pl.when(at.has_second)
        def _():
            begin(1).wait()
            share(1).start()

        share(0).wait_recv()
        pl.when(at.has_second)(lambda: share(1).wait_send())

    for c in range(2):
        precond[:, lanes(c)] = mask[:, lanes(c)] * (stiff_in[:, lanes(c)] + across[c, modes])
    small = jnp.zeros((8 - modes, slot), F32)
    for s in range(subs):
        for c in range(2):
            line = mask[s : s + 1, lanes(c)]
            own = line * wide[s, :, lanes(c)]
            outer = -line * jnp.concatenate([across[c, 0:modes, s, :], small], axis=0)
            put(
                s,
                slice(0, 16),
                lanes(c),
                jnp.concatenate([own, outer if c == 0 else zero], axis=0),
            )
            put(
                s,
                slice(16, 32),
                lanes(c),
                jnp.concatenate([outer if c == 1 else zero, zero], axis=0),
            )

    middle_msg, middle_all = k["middle_msg"], k["middle_all"]
    middle_msg[...] = jnp.zeros(middle_msg.shape, F32)
    for s in range(subs):
        weighted = wide[s] * precond[s : s + 1]
        block = by_two(across_rows, weighted, (high[s], low[s]))
        line, first = 8 * (s % 4), 64 * (s // 4)
        middle_msg[line : line + 8, first : first + 48] = block
    start_middle, wait_middle = at.everywhere(
        middle_msg, middle_all, k["msend"], k["mrecv"]
    )
    start_middle()
    middle_all[me] = middle_msg[...]

    residual = k["residual"]
    for s in range(subs):
        residual[s, :, lanes(3)] = jnp.zeros((loads, slot), F32)
        for c in (2, 4, 5):
            t = inner_partner(c, s)
            residual[s, :, lanes(c)] = mask[s : s + 1, lanes(c)] * (
                rhs[s, :, lanes(c)] - rhs[0 if t is None else t, :, lanes(c)]
            )
    at.wait_faces(right)
    for s in range(subs):
        for c in range(2):
            residual[s, :, lanes(c)] = mask[s : s + 1, lanes(c)] * (
                rhs[s, :, lanes(c)] - beyond[c, :, s, :]
            )

    gats = [(k[f"gat{n}"], k[f"esend{n}"], k[f"erecv{n}"], k[f"msg{n}"]) for n in range(4)]

    def coarse(msg, vector, tiles, scaled, chosen):
        for s in chosen:
            v = vector[s]
            if scaled:
                v = jnp.concatenate([v, precond[s : s + 1] * v], axis=0)
            out = by_two(across_rows, v, (high[s, 0:32], low[s, 0:32]))
            for t in range(tiles):
                part = out[:, 8 * t : 8 * t + 8]
                msg[t, :, 8 * s : 8 * s + 8] = part[:loads]
                if scaled:
                    msg[t, :, 64 + 8 * s : 72 + 8 * s] = part[loads:]

    lane = lax.broadcasted_iota(jnp.int32, (loads, 128), 1)
    gat, esend, erecv, msg = gats[0]
    coarse(msg, residual, 1, True, range(subs))
    start, wait_first = at.everywhere(msg, gat, esend, erecv)
    start()
    gat[me] = msg[...]
    for s in range(subs):
        load(s).start()

    inverse_far(at.far).wait_recv()
    inverse_relay(at.far).start()
    order = NSUB * 64
    full_order = NSUB * subs * modes
    row = lax.broadcasted_iota(jnp.int32, (order, full_order), 0)
    column = lax.broadcasted_iota(jnp.int32, (order, full_order), 1)
    widen = jnp.where((row % 8 < modes) & (row // 8 * modes + row % 8 == column), 1.0, 0.0)
    widen = widen.astype(BF16)
    row = lax.broadcasted_iota(jnp.int32, (order, 192), 0)
    column = lax.broadcasted_iota(jnp.int32, (order, 192), 1)
    s_of, j_of, n_of = row // 64, row // 8 % 8, row % 8
    source = jnp.where(j_of == 3, s_of ^ 4, jnp.where(j_of == 4, s_of ^ 1, s_of))
    source = jnp.where(j_of == 5, s_of ^ 3, source)
    wanted = jnp.where(j_of <= 2, 64 * j_of, 0) + 8 * source + n_of
    choose = jnp.where((j_of <= 5) & (wanted == column), 1.0, 0.0).astype(BF16)
    inverse_twin(at.twin).wait_recv()
    inverse_relay(at.diagonal).wait_recv()
    all_rows = inverse[...].reshape(full_order, full_order)
    present = at.has_second.astype(F32)
    there = jnp.where(at.has_second, at.second, 0)
    for part, whole, chosen in zip(
        halves(all_rows), (k["q_high"], k["q_low"]), (k["near_high"], k["near_low"])
    ):
        tall = along(widen, part).astype(BF16)
        whole[...] = across_rows(tall, widen).astype(BF16)
        near = jnp.concatenate(
            [
                whole[pl.ds(pl.multiple_of(64 * me, 64), 64), :].astype(F32),
                whole[pl.ds(pl.multiple_of(64 * at.first, 64), 64), :].astype(F32),
                present * whole[pl.ds(pl.multiple_of(64 * there, 64), 64), :].astype(F32),
            ],
            axis=0,
        ).astype(BF16)
        chosen[...] = along(choose, near).astype(BF16)
    q_pair = (k["q_high"], k["q_low"])
    near_pair = (k["near_high"], k["near_low"])
    m_pair = (k["m_high"], k["m_low"])
    for ref in m_pair:
        ref[...] = jnp.zeros(ref.shape, BF16)
    inverse_far(q).wait_send()
    inverse_twin(q).wait_send()
    inverse_relay(at.far).wait_send()

    wait_middle()
    row = lax.broadcasted_iota(jnp.int32, (64, 384), 0)
    column = lax.broadcasted_iota(jnp.int32, (64, 384), 1)
    spread = jnp.where(row == column // 64 * 8 + column % 8, 1.0, 0.0).astype(BF16)
    row = lax.broadcasted_iota(jnp.int32, (64, 64), 0) // 8
    column = lax.broadcasted_iota(jnp.int32, (64, 64), 1) // 8
    same = (row == column).astype(F32)
    inner_masks = [(row ^ flip == column).astype(F32) for flip in (4, 1, 3)]
    compact = [middle_all[t, :, 64 * h : 64 * h + 64] for t in range(NSUB) for h in range(2)]
    for part, whole in zip(halves(jnp.concatenate(compact, axis=0)), m_pair):
        wide_part = along(part, spread)
        for t in range(NSUB):
            piece = wide_part[64 * t : 64 * t + 64]
            own = same * piece[:, 0:64]
            for j in range(3):
                own = own + inner_masks[j] * piece[:, 64 * (j + 3) : 64 * (j + 4)]
            first, second = near_of(t)
            whole[64 * t : 64 * t + 64, 64 * t : 64 * t + 64] = own.astype(BF16)
            whole[64 * t : 64 * t + 64, 64 * first : 64 * first + 64] = (
                same * piece[:, 64:128]
            ).astype(BF16)
            if second is not None:
                whole[64 * t : 64 * t + 64, 64 * second : 64 * second + 64] = (
                    same * piece[:, 128:192]
                ).astype(BF16)

    def pair_of(pair):
        return pair[0][...], pair[1][...]

    def joined(tiles, half):
        return jnp.concatenate([t[:, 64 * half : 64 * half + 64] for t in tiles], axis=1)

    def lift_of(coefficients, s):
        part = coefficients[:, 64 * s : 64 * s + 48]
        return by_two(along, part, (high[s], low[s]))

    packed = k["packed"]

    def pack(value, s):
        y, z = s // 4, s % 4
        packed[z, 2 * y] = value[:, lanes(0)]
        packed[z, 2 * y + 1] = value[:, lanes(1)]
        if y == 0:
            packed[z, 4] = value[:, lanes(2)]
        if z % 2 == 0:
            packed[z, 5 + y] = value[:, lanes(4)]
        if z == 1:
            packed[z, 5 + y] = value[:, lanes(5)]

    def direction(c_res, c_scaled, target, send):
        y = by_two(across_rows, c_res, pair_of(q_pair))
        c_scaled = c_scaled - by_two(across_rows, y, pair_of(m_pair))
        both = jnp.concatenate([c_res, c_scaled], axis=0)
        near = by_two(across_rows, both, pair_of(near_pair))
        total = jnp.zeros((loads, interface), F32)
        for p in range(subs // 2):
            for s in (p, p + subs // 2):
                lifted = lift_of(near, s)
                projected = residual[s] - lifted[:loads]
                scaled = precond[s : s + 1] * projected
                total = total + projected * scaled
                value = scaled - lifted[loads:]
                target[s] = value
                pack(value, s)
            send(p)
        return 0.5 * jnp.sum(total, axis=1, keepdims=True)

    wait_first()
    tiles = [gat[t, 0] for t in range(NSUB)]
    c_res, c_scaled = joined(tiles, 0), joined(tiles, 1)
    search, fresh = k["search"], k["fresh"]
    product = k["product"]
    arrivals = [[k[f"{name}{n}"] for name in ("arriving", "fsend", "frecv")] for n in range(2)]
    ops = [
        operate(
            at,
            packed,
            hold,
            k["res"],
            product,
            [k[f"op{n}_{i}"] for i in range(5)],
            *arrivals[n],
        )
        for n in range(ITERS)
    ]
    send, run, settle, drain, faces = ops[0]
    partial = direction(c_res, c_scaled, search, send)
    for s in range(subs):
        load(s).wait()
    image = [k["image0"], k["image1"]]

    def mixed(target, s):
        y, z = s // 4, s % 4
        for c in range(2):
            target[s, :, lanes(c)] = mask[s : s + 1, lanes(c)] * product[y, z, :, lanes(c)]
        target[s, :, lanes(3)] = jnp.zeros((loads, slot), F32)
        for c in (2, 4, 5):
            t = inner_partner(c, s)
            if t is None:
                target[s, :, lanes(c)] = jnp.zeros((loads, slot), F32)
                continue
            owner = min(s, t)
            value = mask[s : s + 1, lanes(c)] * product[owner // 4, owner % 4, :, lanes(c)]
            target[s, :, lanes(c)] = value if s == owner else -value

    def finish_image(target, arriving):
        for s in range(subs):
            for c in range(2):
                target[s, :, lanes(c)] = (
                    target[s, :, lanes(c)]
                    - mask[s : s + 1, lanes(c)] * arriving[c, s // 4, s % 4]
                )

    def curve_of(direct, values, chosen, sums):
        for s in chosen:
            both = direct[s] * values[s]
            sums = (sums[0] + both[:, : 2 * slot], sums[1] + both[:, 2 * slot :])
        return sums

    def curve_end(sums):
        total = jnp.sum(sums[0], axis=1, keepdims=True)
        return total + 0.5 * jnp.sum(sums[1], axis=1, keepdims=True)

    groups = [[s for s in range(subs) if s % 4 // 2 == half] for half in range(2)]
    nothing = (jnp.zeros((loads, 2 * slot), F32), jnp.zeros((loads, 4 * slot), F32))

    def no_second():
        for n in range(2):
            k[f"arriving{n}"][1] = jnp.zeros(k[f"arriving{n}"].shape[1:], F32)

    pl.when(jnp.logical_not(at.has_second))(no_second)

    def gathered(gat, scaled):
        tiles = []
        for t in range(NSUB):
            first, second = near_of(t)
            if scaled:
                tile = gat[t, 0] + gat[first, 1]
                if second is not None:
                    tile = tile + gat[second, 2]
            else:
                tile = gat[t, 0][:, 0:64] + gat[first, 1][:, 0:64]
                if second is not None:
                    tile = tile + gat[second, 2][:, 0:64]
            tiles.append(tile)
        return tiles

    def summed(gat, at_lane):
        total = gat[0, 0]
        for t in range(1, NSUB):
            total = total + gat[t, 0]
        return [total[:, n : n + 1] for n in at_lane]

    run()
    gat, esend, erecv, msg = gats[1]
    sums = nothing
    for p in range(4):
        settle(p)
        if p >= 2:
            chosen = groups[p - 2]
            for s in chosen:
                mixed(image[0], s)
            coarse(msg, image[0], 3, True, chosen)
            sums = curve_of(search, image[0], chosen, sums)
    curve = curve_end(sums)
    msg[0] = jnp.where(lane == 6, curve, jnp.where(lane == 7, partial, msg[0]))
    start, wait = at.everywhere(msg, gat, esend, erecv)
    start()
    gat[me] = msg[...]
    drain()
    faces()
    finish_image(image[0], k["arriving0"])
    wait()
    tiles = gathered(gat, True)
    curve, energy = summed(gat, (6, 7))
    step_0 = energy / curve
    c_res = c_res - step_0 * joined(tiles, 0)
    c_scaled = c_scaled - step_0 * joined(tiles, 1)
    for s in range(subs):
        residual[s] = residual[s] - step_0 * image[0][s]
    send, run, settle, drain, faces = ops[1]
    partial = direction(c_res, c_scaled, fresh, send)

    gat_e, esend, erecv, msg = gats[2]
    msg[0] = jnp.broadcast_to(partial, (loads, 128))
    start, wait_energy = at.everywhere(msg, gat_e, esend, erecv)
    start()
    gat_e[me] = msg[...]
    run()
    wait_energy()
    fresh_energy = summed(gat_e, (0,))[0]
    ratio = fresh_energy / energy
    gat, esend, erecv, msg = gats[3]
    sums = nothing
    at_rest = slice(2 * slot, interface)
    for p in range(4):
        settle(p)
        if p < 2:
            continue
        chosen = groups[p - 2]
        for s in chosen:
            fresh[s] = fresh[s] + ratio * search[s]
            mixed(image[1], s)
            for c in range(2):
                before = image[0][s, :, lanes(c)] + (
                    mask[s : s + 1, lanes(c)] * k["arriving0"][c, s // 4, s % 4]
                )
                image[1][s, :, lanes(c)] = image[1][s, :, lanes(c)] + ratio * before
            image[1][s, :, at_rest] = image[1][s, :, at_rest] + ratio * image[0][s, :, at_rest]
        coarse(msg, image[1], 3, False, chosen)
        sums = curve_of(fresh, image[1], chosen, sums)
    curve = curve_end(sums)
    msg[0] = jnp.where(lane == 6, curve, msg[0])
    start, wait = at.everywhere(msg, gat, esend, erecv)
    start()
    gat[me] = msg[...]
    drain()
    faces()
    k["arriving1"][...] = k["arriving1"][...] + ratio * k["arriving0"][...]
    finish_image(image[1], k["arriving1"])
    wait()
    tiles = gathered(gat, False)
    step_1 = fresh_energy / summed(gat, (6,))[0]
    c_res = c_res - step_1 * jnp.concatenate(tiles, axis=1)
    near = by_two(across_rows, c_res, pair_of(near_pair))
    for s in range(subs):
        mult_out[:, s, :] = step_0 * search[s] + step_1 * fresh[s]
        proj_out[:, s, :] = residual[s] - step_1 * image[1][s] - lift_of(near, s)


def deliver_kernel(first_in, second_in, first_out, second_out, held, sems):
    parts = held.shape[1]

    def copy(n, out):
        which, part = n // parts, n % parts
        middle = held.at[which, part]
        if out:
            target = (first_out, second_out)[which].at[part]
            return pltpu.make_async_copy(middle, target, sems.at[1, n])
        source = (first_in, second_in)[which].at[part]
        return pltpu.make_async_copy(source, middle, sems.at[0, n])

    for n in range(2 * parts):
        copy(n, False).start()
    for n in range(2 * parts):
        copy(n, False).wait()
        copy(n, True).start()
    for n in range(2 * parts):
        copy(n, True).wait()


def by_kernels(schur_block, rigid_modes, coarse_inverse, dual_rhs, stiff_diag, face_length):
    loads, subs, interface = dual_rhs.shape
    rows = schur_block.shape[1]
    slot = interface // 6
    modes = rigid_modes.shape[1]
    vmem = pl.BlockSpec(memory_space=pltpu.VMEM)
    hbm = pl.BlockSpec(memory_space=pltpu.HBM)
    dma = pltpu.SemaphoreType.DMA
    order = NSUB * 64
    vector = pltpu.VMEM((subs, loads, interface), F32)
    edge = pltpu.VMEM((2, modes + 1, subs, slot), F32)
    face = pltpu.VMEM((2, 2, subs // 2, loads, slot), F32)
    basis = pltpu.VMEM((subs, 48, interface), BF16)
    square = pltpu.VMEM((order, order), BF16)
    scratch = {
        "hold": pltpu.VMEM((2, subs // 2, rows, interface), F32),
        "load_sem": dma((subs,)),
        "input_sem": dma((5,)),
        "edges": edge,
        "across": edge,
        "beyond": pltpu.VMEM((2, loads, subs, slot), F32),
        "rsend": dma((2,)),
        "rrecv": dma((2,)),
        "tsend": dma((2,)),
        "trecv": dma((2,)),
        "bsend": dma((2,)),
        "brecv": dma((2,)),
        "inverse": pltpu.VMEM((NCRS,) + coarse_inverse.shape, F32),
        "isend": dma((3,)),
        "irecv": dma((3,)),
        "wide": pltpu.VMEM((subs, 8, interface), F32),
        "rhs": vector,
        "mask": pltpu.VMEM((subs, interface), F32),
        "precond": pltpu.VMEM((subs, interface), F32),
        "basis_high": basis,
        "basis_low": basis,
        "residual": vector,
        "middle_msg": pltpu.VMEM((32, 128), F32),
        "middle_all": pltpu.VMEM((NSUB, 32, 128), F32),
        "msend": dma((NSUB,)),
        "mrecv": dma((NSUB,)),
        "q_high": square,
        "q_low": square,
        "near_high": square,
        "near_low": square,
        "m_high": square,
        "m_low": square,
        "packed": pltpu.VMEM((4, 7, loads, slot), F32),
        "search": vector,
        "fresh": vector,
        "product": pltpu.VMEM((2, subs // 2, loads, interface), F32),
        "image0": vector,
        "image1": vector,
        "res": pltpu.VMEM((2, subs // 2, NCRS, loads, rows), F32),
    }
    sources = [
        jnp.swapaxes(rigid_modes, 0, 1),
        coarse_inverse,
        dual_rhs,
        stiff_diag,
        face_length,
    ]
    for n, source in enumerate(sources):
        scratch[f"input{n}"] = pltpu.VMEM(source.shape, source.dtype)
    for n, tiles in enumerate((1, 3, 1, 3)):
        scratch[f"msg{n}"] = pltpu.VMEM((tiles, loads, 128), F32)
        scratch[f"gat{n}"] = pltpu.VMEM((NSUB, tiles, loads, 128), F32)
        scratch[f"esend{n}"] = dma((NSUB,))
        scratch[f"erecv{n}"] = dma((NSUB,))
    for n in range(ITERS):
        scratch[f"op{n}_0"] = pltpu.VMEM((4, NCRS, 7, loads, slot), F32)
        scratch[f"op{n}_1"] = dma((3, 4))
        scratch[f"op{n}_2"] = dma((3, 4))
        scratch[f"op{n}_3"] = dma((3, 4, 2))
        scratch[f"op{n}_4"] = dma((NCRS, 4, 2))
        scratch[f"arriving{n}"] = face
        scratch[f"fsend{n}"] = dma((2, 4))
        scratch[f"frecv{n}"] = dma((2, 4))
    out = jax.ShapeDtypeStruct((loads, subs, interface), F32)
    results = pl.pallas_call(
        functools.partial(main_kernel, list(scratch)),
        out_shape=(out, out),
        in_specs=[hbm] * 6,
        out_specs=(vmem, vmem),
        scratch_shapes=list(scratch.values()),
        compiler_params=pltpu.CompilerParams(
            collective_id=0, has_side_effects=True, vmem_limit_bytes=56 * 1024 * 1024
        ),
        name="main",
    )(schur_block, *sources)
    return pl.pallas_call(
        deliver_kernel,
        out_shape=(out, out),
        in_specs=[hbm] * 2,
        out_specs=(hbm, hbm),
        scratch_shapes=[pltpu.VMEM((2, loads, subs, interface), F32), dma((2, 2 * loads))],
        compiler_params=pltpu.CompilerParams(vmem_limit_bytes=56 * 1024 * 1024),
        name="deliver",
    )(*results)


def shards(schur_block, rigid_modes, coarse_inverse, dual_rhs, stiff_diag, face_length):
    fits = dual_rhs.shape[0] == 8 and lax.axis_size("crs") == NCRS and lax.axis_size("sub") == NSUB
    build = by_kernels if fits else by_collectives
    return build(schur_block, rigid_modes, coarse_inverse, dual_rhs, stiff_diag, face_length)


def solution(mesh):
    return jax.shard_map(
        shards,
        mesh=mesh,
        in_specs=(
            P("sub", "crs", None),
            P("sub", None, None),
            P("crs", None),
            P("crs", "sub", None),
            P("sub", None),
            P("sub", None),
        ),
        out_specs=(P("crs", "sub", None), P("crs", "sub", None)),
        check_vma=False,
    )
```

```python
import functools

import jax
import jax.numpy as jnp
import numpy as np
from jax import lax
from jax.experimental import pallas as pl
from jax.experimental.pallas import tpu as pltpu
from jax.sharding import PartitionSpec as P

ITERS = 2
SY = 2
SZ = 4
SUBS = 8

PRECISE = lax.Precision.HIGHEST
SPLIT = lax.Precision.HIGH


def local_lookup():
    indices = np.arange(SUBS)
    coords = [indices // SZ, indices % SZ]
    extent = [SY, SZ]
    stride = [SZ, 1]
    lookup = np.zeros((4, SUBS), np.int32)
    for colour in range(4):
        axis_pick = colour // 2
        anchor = coords[axis_pick]
        offset = np.where(anchor % 2 == colour % 2, 1, -1)
        target = anchor + offset
        inside = (target >= 0) & (target < extent[axis_pick])
        lookup[colour] = np.where(inside, indices + offset * stride[axis_pick], indices)
    return lookup


def by_collectives(schur_block, rigid_modes, coarse_inverse, dual_rhs, stiff_diag, face_length):
    loads, subs, interface = dual_rhs.shape
    slot = interface // 6
    modes = rigid_modes.shape[1]
    own = subs * modes
    nsub = lax.axis_size("sub")
    sub_index = lax.axis_index("sub")
    even = sub_index % 2 == 0
    lookup = local_lookup()
    positions = jnp.arange(interface) % slot
    usable = (jnp.repeat(face_length, slot, axis=1) > positions[None, :]).astype(jnp.float32)
    up = [(i, i + 1) for i in range(nsub - 1)]
    down = [(i + 1, i) for i in range(nsub - 1)]

    def partner(vector):
        first = vector[..., :slot]
        second = vector[..., slot : 2 * slot]
        from_left = lax.ppermute(jnp.where(even, first, second), "sub", up)
        from_right = lax.ppermute(jnp.where(even, second, first), "sub", down)
        pieces = [jnp.where(even, from_right, from_left), jnp.where(even, from_left, from_right)]
        for colour in range(2, 6):
            window = vector[..., colour * slot : (colour + 1) * slot]
            pieces.append(
                jnp.concatenate([window[..., t : t + 1, :] for t in lookup[colour - 2]], axis=-2)
            )
        return jnp.concatenate(pieces, axis=-1)

    modes_first = jnp.swapaxes(rigid_modes, 0, 1)
    together = jnp.concatenate([dual_rhs, modes_first, stiff_diag[None]], axis=0)
    across = partner(together)
    residual = usable * (dual_rhs - across[:loads])
    modes_across = across[loads : loads + modes]
    precond = usable * (stiff_diag + across[-1])

    inverse = lax.all_gather(coarse_inverse, "crs", axis=0, tiled=True)

    def by_slot(array):
        return array.reshape(array.shape[:-1] + (6, slot))

    basis = by_slot(usable * jnp.concatenate([modes_first, -modes_across], axis=0))

    weighted = by_slot(modes_first * precond)
    blocks = jnp.einsum("msck,nsck->scmn", weighted, basis, precision=PRECISE)
    total_subs = nsub * subs
    here = sub_index * subs + jnp.arange(subs)
    left = here - subs
    right = here + subs
    targets = [jnp.where(even, right, left), jnp.where(even, left, right)]
    for colour in range(2, 6):
        targets.append(sub_index * subs + jnp.asarray(lookup[colour - 2]))
    targets = jnp.stack(targets, axis=1)
    hot_across = (targets[:, :, None] == jnp.arange(total_subs)).astype(jnp.float32)
    hot_here = (here[:, None] == jnp.arange(total_subs)).astype(jnp.float32)
    dense = jnp.einsum("smn,st->smtn", blocks[..., :modes].sum(axis=1), hot_here, precision=PRECISE)
    dense = dense + jnp.einsum("scmn,sct->smtn", blocks[..., modes:], hot_across, precision=PRECISE)
    dense = dense.reshape(own, total_subs * modes)
    middle = lax.all_gather(dense, "sub", axis=0, tiled=True)

    def coarse(vector):
        return jnp.einsum("lsi,msi->lsm", vector, modes_first, precision=PRECISE).reshape(loads, own)

    def dots(a, b):
        return jnp.sum(a * b, axis=(1, 2))[:, None]

    def shared(parts):
        gathered = lax.all_gather(jnp.concatenate(parts, axis=1), "sub", axis=0)
        count = own * (sum(part.shape[1] == own for part in parts))
        outs = []
        for at in range(0, count, own):
            outs.append(jnp.swapaxes(gathered[:, :, at : at + own], 0, 1).reshape(loads, nsub * own))
        sums = jnp.sum(gathered[:, :, count:], axis=0)
        return outs, [sums[:, j : j + 1] for j in range(sums.shape[1])]

    def solve(values):
        return jnp.einsum("lb,ab->la", values, inverse, precision=PRECISE)

    def lifted(values):
        grid = values.reshape(loads, nsub, subs, modes)
        padded = jnp.pad(grid, ((0, 0), (1, 1), (0, 0), (0, 0)))
        near = lax.dynamic_slice_in_dim(padded, sub_index, 3, axis=1)
        before, mine, after = near[:, 0], near[:, 1], near[:, 2]
        pieces = [jnp.where(even, after, before), jnp.where(even, before, after)]
        for colour in range(2, 6):
            pieces.append(jnp.stack([mine[:, t] for t in lookup[colour - 2]], axis=1))
        other = jnp.stack(pieces, axis=2)
        mine = jnp.broadcast_to(mine[:, :, None], other.shape)
        factors = jnp.concatenate([mine, other], axis=-1)
        out = jnp.einsum("lscm,msck->lsck", factors, basis, precision=PRECISE)
        return out.reshape(loads, subs, interface)

    def direction(residual, c_res, c_scaled, power):
        y = solve(c_res)
        my = jnp.einsum("lb,ab->la", y, middle, precision=PRECISE)
        energy = 0.5 * power - 2.0 * jnp.sum(y * c_scaled, axis=1, keepdims=True)
        energy = energy + jnp.sum(y * my, axis=1, keepdims=True)
        t = solve(c_scaled - my)
        return precond * (residual - lifted(y)) - lifted(t), energy

    scaled = precond * residual
    (c_res, c_scaled), (power,) = shared([coarse(residual), coarse(scaled), dots(residual, scaled)])
    search, energy = direction(residual, c_res, c_scaled, power)
    multipliers = None
    for iteration in range(ITERS):
        by_rows = jnp.einsum(
            "sij,lsj->lsi",
            schur_block,
            lax.all_gather(search, "crs", axis=0, tiled=True),
            precision=SPLIT,
        )
        product = lax.all_to_all(by_rows, "crs", split_axis=0, concat_axis=2, tiled=True)
        image = usable * (product - partner(product))
        last = iteration + 1 == ITERS
        curve = dots(search, product)
        if last:
            (c_image,), (curve,) = shared([coarse(image), curve])
        else:
            scaled_image = precond * image
            parts = [
                coarse(image),
                coarse(scaled_image),
                curve,
                dots(residual, scaled_image),
                dots(image, scaled_image),
            ]
            (c_image, c_scaled_image), (curve, cross, square) = shared(parts)
        step = energy / curve
        moved = step[:, :, None] * search
        multipliers = moved if multipliers is None else multipliers + moved
        residual = residual - step[:, :, None] * image
        c_res = c_res - step * c_image
        if last:
            projected = residual - lifted(solve(c_res))
        else:
            c_scaled = c_scaled - step * c_scaled_image
            power = power - 2.0 * step * cross + step * step * square
            fresh, energy_new = direction(residual, c_res, c_scaled, power)
            search = fresh + (energy_new / energy)[:, :, None] * search
            energy = energy_new
    return (multipliers, projected)


MESH = pl.DeviceIdType.MESH
F32 = jnp.float32
BF16 = jnp.bfloat16
NSUB = 8
NCRS = 4


def across_rows(a, b):
    return lax.dot_general(a, b, (((1,), (1,)), ((), ())), preferred_element_type=F32)


def along(a, b):
    return jnp.dot(a, b, preferred_element_type=F32)


def halves(x):
    high = x.astype(BF16)
    return high, (x - high.astype(F32)).astype(BF16)


def stacked(x):
    high = x.astype(BF16).astype(F32)
    return jnp.concatenate([high, x - high], axis=0).astype(BF16)


def folded(x):
    rows = x.shape[0] // 2
    return x[:rows] + x[rows:]


def by_two(product, x, pair):
    both = stacked(x)
    return folded(product(both, pair[0]) + product(both, pair[1]))


def near_of(block):
    low = block - 1 if block % 2 == 0 else block + 1
    return block ^ 1, (low if 0 <= low < NSUB else None)


def remote(src, dst, send, recv, target):
    return pltpu.make_async_remote_copy(
        src_ref=src,
        dst_ref=dst,
        send_sem=send,
        recv_sem=recv,
        device_id=target,
        device_id_type=MESH,
    )


class Place:
    def __init__(self):
        self.me = me = lax.axis_index("sub")
        self.q = q = lax.axis_index("crs")
        core = q % 2
        self.twin = q + 1 - 2 * core
        self.far = (q + 2) % NCRS
        self.diagonal = (self.twin + 2) % NCRS
        odd = me % 2
        self.first = me + 1 - 2 * odd
        self.second = me - 1 + 2 * odd
        self.has_second = jnp.logical_and(self.second >= 0, self.second < NSUB)

    def faces(self, src, dst, send, recv):
        return (
            remote(src(0), dst.at[0], send.at[0], recv.at[0], (self.first, self.q)),
            remote(src(1), dst.at[1], send.at[1], recv.at[1], (self.second, self.q)),
        )

    def start_faces(self, copies):
        copies[0].start()

        @pl.when(self.has_second)
        def _():
            copies[1].start()

    def wait_faces(self, copies):
        copies[0].wait()

        @pl.when(self.has_second)
        def _():
            copies[1].wait()

    def everywhere(self, src, gat, send, recv):
        def copy(k, block):
            return remote(
                src, gat.at[block], send.at[k], recv.at[k], ((self.me + k) % NSUB, self.q)
            )

        def start():
            for k in range(1, NSUB):
                copy(k, self.me).start()

        def wait():
            for k in range(1, NSUB):
                copy(k, (self.me + NSUB - k) % NSUB).wait_recv()
            for k in range(1, NSUB):
                copy(k, self.me).wait_send()

        return start, wait


def chunk_size(p):
    return 5 if p == 3 else 7


def operate(at, packed, hold, res, product, buffers, arriving, fsend, frecv):
    gath, gsend, grecv, asend, arecv, cres, ctwin, csend, crecv = buffers
    me, q = at.me, at.q
    lower = q < 2
    upper = q >= 2
    rows = hold.shape[2]
    loads = packed.shape[2]

    def to_far(p, n, block):
        return remote(
            packed.at[p, pl.ds(0, n)],
            gath.at[p, block, pl.ds(0, n)],
            gsend.at[1, p],
            grecv.at[1, p],
            (me, at.far),
        )

    def to_twin(p, n, block):
        return remote(
            packed.at[p, pl.ds(0, n)],
            gath.at[p, block, pl.ds(0, n)],
            gsend.at[0, p],
            grecv.at[0, p],
            (me, at.twin),
        )

    def relay(p, n, source, block):
        return remote(
            gath.at[p, source, pl.ds(0, n)],
            gath.at[p, block, pl.ds(0, n)],
            gsend.at[2, p],
            grecv.at[2, p],
            (me, at.twin),
        )

    def by_side(p, action):
        if p == 3:
            action(5)
        else:
            pl.when(lower)(functools.partial(action, 7))
            pl.when(upper)(functools.partial(action, 5))

    def send(p):
        n = chunk_size(p)
        by_side(p, lambda n: to_far(p, n, q).start())
        to_twin(p, n, q).start()
        gath[p, q, 0:n] = packed[p, 0:n]

    def sized(small, action):
        pl.when(jnp.logical_not(small))(functools.partial(action, 7))
        pl.when(small)(functools.partial(action, 5))

    def forward(p, n):
        to_far(p, n, at.far).wait_recv()
        relay(p, n, at.far, at.far).start()

    def few(p):
        return jnp.logical_or(lower, p == 3)

    peers = (at.twin, at.far, at.diagonal)

    def pieces(owner, p):
        if owner == 0:
            return [(lambda b: res.at[:, p, b], product.at[:, p, :, 0:384], 0, None)]
        if owner == 1:
            return [
                (lambda b: res.at[0, p, b], product.at[0, p, :, 384:768], 0, None),
                (lambda b: res.at[1, p, b, :, 0:128], product.at[1, p, :, 384:512], 1, None),
            ]
        odd = p % 2 == 1
        if owner == 2:
            source = lambda b: res.at[:, p - 1, b, :, 256:384]
            return [(source, product.at[:, p - 1, :, 1024:1152], 0, odd)]
        source = lambda b: res.at[:, p - 1, b, :, 0:128]
        inner = lambda b: res.at[:, 1, b, :, 128:384]
        return [
            (source, product.at[:, p - 1, :, 1152:1280], 0, odd),
            (inner, product.at[:, 1, :, 1280:1536], 1, p == 2),
        ]

    def give(piece, p, j):
        source, target, i, _ = piece
        return remote(
            source(peers[j]), target, asend.at[j, p, i], arecv.at[q, p, i], (me, peers[j])
        )

    def guarded(condition, action):
        if condition is None or condition is True:
            action()
        elif condition is not False:
            pl.when(condition)(action)

    def send_back(p):
        for owner in range(NCRS):

            @pl.when(q == owner)
            def _():
                for n, piece in enumerate(pieces(owner, p)):

                    def action():
                        if owner == 1 and n == 0:
                            res[0, p, :, :, 128:384] = (
                                res[0, p, :, :, 128:384] - res[1, p, :, :, 128:384]
                            )
                        if owner == 2:
                            res[:, p - 1, :, :, 256:384] = (
                                res[:, p - 1, :, :, 256:384] - res[:, p, :, :, 256:384]
                            )
                        if owner == 3 and n == 0:
                            res[:, p - 1, :, :, 0:128] = (
                                res[:, p - 1, :, :, 0:128] - res[:, p, :, :, 0:128]
                            )
                        if owner == 3 and n == 1:
                            res[:, 1, :, :, 128:384] = (
                                res[:, 1, :, :, 128:384] - res[:, 2, :, :, 128:384]
                            )
                        for j in range(3):
                            give(piece, p, j).start()
                        source, target, _, _ = piece
                        target[...] = source(owner)[...]

                    guarded(piece[3], action)

    def tripled(product_of, x, w):
        high_w, low_w = halves(w)
        return folded(product_of(x, high_w)) + product_of(x[: x.shape[0] // 2], low_w)

    def block(chunk, j, first, last):
        return gath[chunk, first:last, j].reshape((last - first) * loads, 256)

    def signs(p):
        sign = (1 - 2 * (p % 2)).astype(F32)
        last = jnp.where(p == 1, 1, jnp.where(p == 2, -1, 0)).astype(F32)
        return sign, p - p % 2, last, jnp.where(p == 0, 0, 1)

    def outer_slots(p, y):
        middle = block(p, 4, 0, NCRS)
        return stacked(
            jnp.concatenate(
                [
                    block(p, 2 * y, 0, NCRS),
                    block(p, 2 * y + 1, 0, NCRS),
                    middle if y == 0 else -middle,
                ],
                axis=1,
            )
        )

    def fifth(p):
        return jnp.logical_or(p == 1, p == 2)

    def share(p):
        return remote(
            cres.at[:, p, at.twin % 2], ctwin.at[:, p], csend.at[p], crecv.at[p], (me, at.twin)
        )

    def prepare(p, carry):
        sized(p == 3, lambda n: to_twin(p, n, at.twin).wait_recv())
        sign, even, last, held = signs(p)

        @pl.when(lower)
        def _():
            for y in range(2):
                x = stacked(sign * block(even, 5 + y, 0, 2))
                out = tripled(across_rows, x, hold[y, p, :, 1024:1280])
                res[y, p, 0:2] = out.reshape(2, loads, rows)

            @pl.when(fifth(p))
            def _():
                for y in range(2):
                    x = stacked(last * block(held, 5 + y, 0, 2))
                    out = tripled(across_rows, x, hold[y, p, :, 1280:1536])
                    res[y, p, 0:2] = res[y, p, 0:2] + out.reshape(2, loads, rows)

        @pl.when(upper)
        def _():
            def part(x, y, first, end):
                return tripled(along, stacked(x), hold[y, p, first:end, 0:768])

            @pl.when(q == 2)
            def _():
                for y in range(2):
                    x = sign * block(even, 5 + y, 2, 4)
                    out = part(x[:, 0:128], y, 256, 384)
                    cres[y, p] = out.reshape(2, loads, 768)

            @pl.when(q == 3)
            def _():
                for y in range(2):
                    x = sign * block(even, 5 + y, 2, 4)
                    out = part(x[:, 128:256], y, 0, 128)
                    cres[y, p] = out.reshape(2, loads, 768)

                @pl.when(fifth(p))
                def _():
                    for y in range(2):
                        out = part(last * block(held, 5 + y, 2, 4), y, 128, 384)
                        cres[y, p] = cres[y, p] + out.reshape(2, loads, 768)

            cres[0, p, :, :, 512:768] = cres[0, p, :, :, 512:768] - cres[1, p, :, :, 512:768]
            share(p).start()

        return carry

    def multiply(p, carry):
        @pl.when(p < 3)
        def _():
            sized(few(p + 1), lambda n: forward(p + 1, n))

        sized(few(p), lambda n: relay(p, n, at.far, at.diagonal).wait_recv())
        sign, even, last, held = signs(p)

        @pl.when(lower)
        def _():
            for y in range(2):
                out = tripled(across_rows, outer_slots(p, y), hold[y, p, :, 0:768])
                out = out.reshape(NCRS, loads, rows)
                res[y, p, 0:2] = res[y, p, 0:2] + out[0:2]
                res[y, p, 2:4] = out[2:4]

        def upper_rows(first, end, with_fifth):
            for y in range(2):
                inner = sign * block(even, 5 + y, 0, NCRS)
                size = 256
                if with_fifth:
                    inner = jnp.concatenate([inner, last * block(held, 5 + y, 0, NCRS)], axis=1)
                    size = 512
                out = tripled(across_rows, outer_slots(p, y), hold[y, p, first:end, 0:768])
                out = out + tripled(
                    across_rows, stacked(inner), hold[y, p, first:end, 1024 : 1024 + size]
                )
                res[y, p, :, :, first:end] = out.reshape(NCRS, loads, end - first)

        pl.when(q == 2)(lambda: upper_rows(256, 384, True))

        @pl.when(q == 3)
        def _():
            pl.when(fifth(p))(lambda: upper_rows(0, 384, True))
            pl.when(jnp.logical_not(fifth(p)))(lambda: upper_rows(0, 128, False))

        send_back(p)
        return carry

    def run():
        lax.fori_loop(0, 4, prepare, 0)
        sized(few(0), lambda n: forward(0, n))
        lax.fori_loop(0, 4, multiply, 0)

    def face(c, p):
        return remote(
            product.at[:, p, :, pl.ds(256 * c, 256)],
            arriving.at[c, :, p],
            fsend.at[c, p],
            frecv.at[c, p],
            (at.second if c else at.first, q),
        )

    def returned(owner, p):
        for piece in pieces(owner, p):
            if piece[3] is None or piece[3]:
                _, target, i, _ = piece
                remote(
                    target, target, asend.at[0, p, i], arecv.at[owner, p, i], (me, at.twin)
                ).wait_recv()

    def settle(p):
        for owner in range(2):
            pl.when(q != owner)(functools.partial(returned, owner, p))

        @pl.when(upper)
        def _():
            share(p).wait_recv()
            mine = q % 2
            for y in range(2):
                span = slice(0, 768 if y == 0 else 512)
                product[y, p, :, span] = product[y, p, :, span] + (
                    cres[y, p, mine, :, span] + ctwin[y, p, :, span]
                )

        face(0, p).start()
        pl.when(at.has_second)(face(1, p).start)
        for owner in (2, 3):
            if any(piece[3] for piece in pieces(owner, p)):
                pl.when(q != owner)(functools.partial(returned, owner, p))

    def faces():
        for p in range(4):
            face(0, p).wait()
            pl.when(at.has_second)(face(1, p).wait)

    def drain():
        for p in range(4):
            n = chunk_size(p)
            by_side(p, lambda n: to_far(p, n, q).wait_send())
            to_twin(p, n, q).wait_send()
            if p == 3:
                relay(p, 5, at.far, at.far).wait_send()
            else:
                pl.when(lower)(lambda: relay(p, 5, at.far, at.far).wait_send())
                pl.when(upper)(lambda: relay(p, 7, at.far, at.far).wait_send())
            pl.when(upper)(lambda: share(p).wait_send())
        for owner in range(NCRS):

            @pl.when(q == owner)
            def _():
                for p in range(4):
                    for piece in pieces(owner, p):
                        if piece[3] is None or piece[3]:
                            for j in range(3):
                                give(piece, p, j).wait_send()

    return send, run, settle, drain, faces


def inner_partner(c, s):
    if c == 2:
        return s ^ 4
    if c == 4:
        return s ^ 1
    return s ^ 3 if s % 4 in (1, 2) else None


def main_kernel(names, schur, *refs):
    sources, (mult_out, proj_out) = refs[:5], refs[5:7]
    k = dict(zip(names, refs[7:], strict=True))
    inputs = [k[f"input{n}"] for n in range(5)]
    modes_in, inverse_in, rhs_in, stiff_in, length_in = inputs
    fetches = [
        pltpu.make_async_copy(source, held, k["input_sem"].at[n])
        for n, (source, held) in enumerate(zip(sources, inputs))
    ]
    for copy in fetches:
        copy.start()
    loads, subs, interface = rhs_in.shape
    slot = interface // 6
    modes = modes_in.shape[0]
    at = Place()
    me, q = at.me, at.q
    hold, load_sem = k["hold"], k["load_sem"]

    def lanes(c):
        return slice(c * slot, (c + 1) * slot)

    def load(s):
        return pltpu.make_async_copy(
            schur.at[s], hold.at[s // 4, s % 4], load_sem.at[s]
        )

    barrier = pltpu.get_barrier_semaphore()
    for j in range(1, NSUB):
        pl.semaphore_signal(
            barrier, inc=1, device_id=((me + j) % NSUB, q), device_id_type=MESH
        )
    for j in range(1, NCRS):
        pl.semaphore_signal(barrier, inc=1, device_id=(me, (q + j) % NCRS), device_id_type=MESH)

    for copy in fetches:
        copy.wait()
    edges, across = k["edges"], k["across"]
    for c in range(2):
        edges[c, 0:modes] = modes_in[:, :, lanes(c)]
        edges[c, modes] = stiff_in[:, lanes(c)]
    pl.semaphore_wait(barrier, NSUB + NCRS - 2)

    core = q % 2

    def begin(c):
        target = (at.second if c else at.first, q)
        return remote(edges.at[c], across.at[c], k["bsend"].at[c], k["brecv"].at[c], target)

    def share(c):
        return remote(
            across.at[c], across.at[c], k["tsend"].at[c], k["trecv"].at[c], (me, at.twin)
        )

    pl.when(core == 0)(lambda: begin(0).start())
    pl.when((core == 1) & at.has_second)(lambda: begin(1).start())
    beyond = k["beyond"]
    right = at.faces(lambda c: rhs_in.at[:, :, lanes(c)], beyond, k["rsend"], k["rrecv"])
    at.start_faces(right)
    inverse, isend, irecv = k["inverse"], k["isend"], k["irecv"]

    def inverse_far(block):
        return remote(inverse_in, inverse.at[block], isend.at[1], irecv.at[1], (me, at.far))

    def inverse_twin(block):
        return remote(inverse_in, inverse.at[block], isend.at[0], irecv.at[0], (me, at.twin))

    def inverse_relay(block):
        return remote(
            inverse.at[at.far], inverse.at[block], isend.at[2], irecv.at[2], (me, at.twin)
        )

    inverse_far(q).start()
    inverse_twin(q).start()
    inverse[q] = inverse_in[...]

    @pl.when(jnp.logical_not(at.has_second))
    def _():
        across[1] = jnp.zeros(across.shape[1:], F32)
        beyond[1] = jnp.zeros(beyond.shape[1:], F32)

    wide, rhs, mask, precond = k["wide"], k["rhs"], k["mask"], k["precond"]
    position = lax.broadcasted_iota(jnp.int32, (subs, slot), 1)
    for c in range(6):
        mask[:, lanes(c)] = (length_in[:, c : c + 1] > position).astype(F32)
    blank = jnp.zeros((8 - modes, interface), F32)
    for s in range(subs):
        rhs[s] = rhs_in[:, s, :]
        wide[s] = jnp.concatenate([modes_in[:, s, :], blank], axis=0)
    precond[:, lanes(3)] = jnp.zeros((subs, slot), F32)
    for c in (2, 4, 5):
        other = jnp.concatenate(
            [
                stiff_in[t : t + 1, lanes(c)]
                for t in [inner_partner(c, s) or 0 for s in range(subs)]
            ],
            axis=0,
        )
        precond[:, lanes(c)] = mask[:, lanes(c)] * (stiff_in[:, lanes(c)] + other)

    high, low = k["basis_high"], k["basis_low"]

    def put(s, rows, window, value):
        a, b = halves(value)
        high[s, rows, window] = a
        low[s, rows, window] = b

    zero = jnp.zeros((8, slot), F32)
    for s in range(subs):
        inner = {}
        for c in (2, 4, 5):
            t = inner_partner(c, s)
            inner[c] = zero if t is None else -mask[s : s + 1, lanes(c)] * wide[t, :, lanes(c)]
        for c in range(6):
            upper = inner[2] if c == 2 else zero
            if c >= 2:
                put(s, slice(16, 32), lanes(c), jnp.concatenate([zero, upper], axis=0))
                own = mask[s : s + 1, lanes(c)] * wide[s, :, lanes(c)]
                put(s, slice(0, 16), lanes(c), jnp.concatenate([own, zero], axis=0))
            last = jnp.concatenate(
                [inner[4] if c == 4 else zero, inner[5] if c == 5 else zero], axis=0
            )
            put(s, slice(32, 48), lanes(c), last)


    @pl.when(core == 0)
    def _():
        begin(0).wait()
        share(0).start()
        pl.when(at.has_second)(lambda: share(1).wait_recv())
        share(0).wait_send()

    @pl.when(core == 1)
    def _():
        @pl.when(at.has_second)
        def _():
            begin(1).wait()
            share(1).start()

        share(0).wait_recv()
        pl.when(at.has_second)(lambda: share(1).wait_send())

    for c in range(2):
        precond[:, lanes(c)] = mask[:, lanes(c)] * (stiff_in[:, lanes(c)] + across[c, modes])
    small = jnp.zeros((8 - modes, slot), F32)
    for s in range(subs):
        for c in range(2):
            line = mask[s : s + 1, lanes(c)]
            own = line * wide[s, :, lanes(c)]
            outer = -line * jnp.concatenate([across[c, 0:modes, s, :], small], axis=0)
            put(
                s,
                slice(0, 16),
                lanes(c),
                jnp.concatenate([own, outer if c == 0 else zero], axis=0),
            )
            put(
                s,
                slice(16, 32),
                lanes(c),
                jnp.concatenate([outer if c == 1 else zero, zero], axis=0),
            )

    middle_msg, middle_all = k["middle_msg"], k["middle_all"]
    middle_msg[...] = jnp.zeros(middle_msg.shape, F32)
    for s in range(subs):
        weighted = wide[s] * precond[s : s + 1]
        block = by_two(across_rows, weighted, (high[s], low[s]))
        line, first = 8 * (s % 4), 64 * (s // 4)
        middle_msg[line : line + 8, first : first + 48] = block
    start_middle, wait_middle = at.everywhere(
        middle_msg, middle_all, k["msend"], k["mrecv"]
    )
    start_middle()
    middle_all[me] = middle_msg[...]

    residual = k["residual"]
    for s in range(subs):
        residual[s, :, lanes(3)] = jnp.zeros((loads, slot), F32)
        for c in (2, 4, 5):
            t = inner_partner(c, s)
            residual[s, :, lanes(c)] = mask[s : s + 1, lanes(c)] * (
                rhs[s, :, lanes(c)] - rhs[0 if t is None else t, :, lanes(c)]
            )
    at.wait_faces(right)
    for s in range(subs):
        for c in range(2):
            residual[s, :, lanes(c)] = mask[s : s + 1, lanes(c)] * (
                rhs[s, :, lanes(c)] - beyond[c, :, s, :]
            )

    gats = [(k[f"gat{n}"], k[f"esend{n}"], k[f"erecv{n}"], k[f"msg{n}"]) for n in range(4)]

    def coarse(msg, vector, tiles, scaled, chosen):
        for s in chosen:
            v = vector[s]
            if scaled:
                v = jnp.concatenate([v, precond[s : s + 1] * v], axis=0)
            out = by_two(across_rows, v, (high[s, 0:32], low[s, 0:32]))
            for t in range(tiles):
                part = out[:, 8 * t : 8 * t + 8]
                msg[t, :, 8 * s : 8 * s + 8] = part[:loads]
                if scaled:
                    msg[t, :, 64 + 8 * s : 72 + 8 * s] = part[loads:]

    lane = lax.broadcasted_iota(jnp.int32, (loads, 128), 1)
    gat, esend, erecv, msg = gats[0]
    coarse(msg, residual, 1, True, range(subs))
    start, wait_first = at.everywhere(msg, gat, esend, erecv)
    start()
    gat[me] = msg[...]
    for s in range(subs):
        load(s).start()

    inverse_far(at.far).wait_recv()
    inverse_relay(at.far).start()
    order = NSUB * 64
    full_order = NSUB * subs * modes
    row = lax.broadcasted_iota(jnp.int32, (order, full_order), 0)
    column = lax.broadcasted_iota(jnp.int32, (order, full_order), 1)
    widen = jnp.where((row % 8 < modes) & (row // 8 * modes + row % 8 == column), 1.0, 0.0)
    widen = widen.astype(BF16)
    row = lax.broadcasted_iota(jnp.int32, (order, 192), 0)
    column = lax.broadcasted_iota(jnp.int32, (order, 192), 1)
    s_of, j_of, n_of = row // 64, row // 8 % 8, row % 8
    source = jnp.where(j_of == 3, s_of ^ 4, jnp.where(j_of == 4, s_of ^ 1, s_of))
    source = jnp.where(j_of == 5, s_of ^ 3, source)
    wanted = jnp.where(j_of <= 2, 64 * j_of, 0) + 8 * source + n_of
    choose = jnp.where((j_of <= 5) & (wanted == column), 1.0, 0.0).astype(BF16)
    inverse_twin(at.twin).wait_recv()
    inverse_relay(at.diagonal).wait_recv()
    all_rows = inverse[...].reshape(full_order, full_order)
    present = at.has_second.astype(F32)
    there = jnp.where(at.has_second, at.second, 0)
    for part, whole, chosen in zip(
        halves(all_rows), (k["q_high"], k["q_low"]), (k["near_high"], k["near_low"])
    ):
        tall = along(widen, part).astype(BF16)
        whole[...] = across_rows(tall, widen).astype(BF16)
        near = jnp.concatenate(
            [
                whole[pl.ds(pl.multiple_of(64 * me, 64), 64), :].astype(F32),
                whole[pl.ds(pl.multiple_of(64 * at.first, 64), 64), :].astype(F32),
                present * whole[pl.ds(pl.multiple_of(64 * there, 64), 64), :].astype(F32),
            ],
            axis=0,
        ).astype(BF16)
        chosen[...] = along(choose, near).astype(BF16)
    q_pair = (k["q_high"], k["q_low"])
    near_pair = (k["near_high"], k["near_low"])
    m_pair = (k["m_high"], k["m_low"])
    for ref in m_pair:
        ref[...] = jnp.zeros(ref.shape, BF16)
    inverse_far(q).wait_send()
    inverse_twin(q).wait_send()
    inverse_relay(at.far).wait_send()

    wait_middle()
    row = lax.broadcasted_iota(jnp.int32, (64, 384), 0)
    column = lax.broadcasted_iota(jnp.int32, (64, 384), 1)
    spread = jnp.where(row == column // 64 * 8 + column % 8, 1.0, 0.0).astype(BF16)
    row = lax.broadcasted_iota(jnp.int32, (64, 64), 0) // 8
    column = lax.broadcasted_iota(jnp.int32, (64, 64), 1) // 8
    same = (row == column).astype(F32)
    inner_masks = [(row ^ flip == column).astype(F32) for flip in (4, 1, 3)]
    compact = [middle_all[t, :, 64 * h : 64 * h + 64] for t in range(NSUB) for h in range(2)]
    for part, whole in zip(halves(jnp.concatenate(compact, axis=0)), m_pair):
        wide_part = along(part, spread)
        for t in range(NSUB):
            piece = wide_part[64 * t : 64 * t + 64]
            own = same * piece[:, 0:64]
            for j in range(3):
                own = own + inner_masks[j] * piece[:, 64 * (j + 3) : 64 * (j + 4)]
            first, second = near_of(t)
            whole[64 * t : 64 * t + 64, 64 * t : 64 * t + 64] = own.astype(BF16)
            whole[64 * t : 64 * t + 64, 64 * first : 64 * first + 64] = (
                same * piece[:, 64:128]
            ).astype(BF16)
            if second is not None:
                whole[64 * t : 64 * t + 64, 64 * second : 64 * second + 64] = (
                    same * piece[:, 128:192]
                ).astype(BF16)

    def pair_of(pair):
        return pair[0][...], pair[1][...]

    def joined(tiles, half):
        return jnp.concatenate([t[:, 64 * half : 64 * half + 64] for t in tiles], axis=1)

    def lift_of(coefficients, s):
        part = coefficients[:, 64 * s : 64 * s + 48]
        return by_two(along, part, (high[s], low[s]))

    packed = k["packed"]

    def pack(value, s):
        y, z = s // 4, s % 4
        packed[z, 2 * y] = value[:, lanes(0)]
        packed[z, 2 * y + 1] = value[:, lanes(1)]
        if y == 0:
            packed[z, 4] = value[:, lanes(2)]
        if z % 2 == 0:
            packed[z, 5 + y] = value[:, lanes(4)]
        if z == 1:
            packed[z, 5 + y] = value[:, lanes(5)]

    def direction(c_res, c_scaled, target, send):
        y = by_two(across_rows, c_res, pair_of(q_pair))
        c_scaled = c_scaled - by_two(across_rows, y, pair_of(m_pair))
        both = jnp.concatenate([c_res, c_scaled], axis=0)
        near = by_two(across_rows, both, pair_of(near_pair))
        total = jnp.zeros((loads, interface), F32)
        for p in range(subs // 2):
            for s in (p, p + subs // 2):
                lifted = lift_of(near, s)
                projected = residual[s] - lifted[:loads]
                scaled = precond[s : s + 1] * projected
                total = total + projected * scaled
                value = scaled - lifted[loads:]
                target[s] = value
                pack(value, s)
            send(p)
        return 0.5 * jnp.sum(total, axis=1, keepdims=True)

    wait_first()
    tiles = [gat[t, 0] for t in range(NSUB)]
    c_res, c_scaled = joined(tiles, 0), joined(tiles, 1)
    search, fresh = k["search"], k["fresh"]
    product = k["product"]
    arrivals = [[k[f"{name}{n}"] for name in ("arriving", "fsend", "frecv")] for n in range(2)]
    ops = [
        operate(
            at,
            packed,
            hold,
            k["res"],
            product,
            [k[f"op{n}_{i}"] for i in range(5)]
            + [k["cres"], k[f"ctwin{n}"], k[f"csend{n}"], k[f"crecv{n}"]],
            *arrivals[n],
        )
        for n in range(ITERS)
    ]
    send, run, settle, drain, faces = ops[0]
    partial = direction(c_res, c_scaled, search, send)
    for s in range(subs):
        load(s).wait()
    image = [k["image0"], k["image1"]]

    def mixed(target, s):
        y, z = s // 4, s % 4
        for c in range(2):
            target[s, :, lanes(c)] = mask[s : s + 1, lanes(c)] * product[y, z, :, lanes(c)]
        target[s, :, lanes(3)] = jnp.zeros((loads, slot), F32)
        for c in (2, 4, 5):
            t = inner_partner(c, s)
            if t is None:
                target[s, :, lanes(c)] = jnp.zeros((loads, slot), F32)
                continue
            owner = min(s, t)
            value = mask[s : s + 1, lanes(c)] * product[owner // 4, owner % 4, :, lanes(c)]
            target[s, :, lanes(c)] = value if s == owner else -value

    def finish_image(target, arriving):
        for s in range(subs):
            for c in range(2):
                target[s, :, lanes(c)] = (
                    target[s, :, lanes(c)]
                    - mask[s : s + 1, lanes(c)] * arriving[c, s // 4, s % 4]
                )

    def curve_of(direct, values, chosen, sums):
        for s in chosen:
            both = direct[s] * values[s]
            sums = (sums[0] + both[:, : 2 * slot], sums[1] + both[:, 2 * slot :])
        return sums

    def curve_end(sums):
        total = jnp.sum(sums[0], axis=1, keepdims=True)
        return total + 0.5 * jnp.sum(sums[1], axis=1, keepdims=True)

    groups = [[s for s in range(subs) if s % 4 // 2 == half] for half in range(2)]
    nothing = (jnp.zeros((loads, 2 * slot), F32), jnp.zeros((loads, 4 * slot), F32))

    def no_second():
        for n in range(2):
            k[f"arriving{n}"][1] = jnp.zeros(k[f"arriving{n}"].shape[1:], F32)

    pl.when(jnp.logical_not(at.has_second))(no_second)

    def gathered(gat, scaled):
        tiles = []
        for t in range(NSUB):
            first, second = near_of(t)
            if scaled:
                tile = gat[t, 0] + gat[first, 1]
                if second is not None:
                    tile = tile + gat[second, 2]
            else:
                tile = gat[t, 0][:, 0:64] + gat[first, 1][:, 0:64]
                if second is not None:
                    tile = tile + gat[second, 2][:, 0:64]
            tiles.append(tile)
        return tiles

    def summed(gat, at_lane):
        total = gat[0, 0]
        for t in range(1, NSUB):
            total = total + gat[t, 0]
        return [total[:, n : n + 1] for n in at_lane]

    run()
    gat, esend, erecv, msg = gats[1]
    sums = nothing
    for p in range(4):
        settle(p)
        if p >= 2:
            chosen = groups[p - 2]
            for s in chosen:
                mixed(image[0], s)
            coarse(msg, image[0], 3, True, chosen)
            sums = curve_of(search, image[0], chosen, sums)
    curve = curve_end(sums)
    msg[0] = jnp.where(lane == 6, curve, jnp.where(lane == 7, partial, msg[0]))
    start, wait = at.everywhere(msg, gat, esend, erecv)
    start()
    gat[me] = msg[...]
    drain()
    faces()
    finish_image(image[0], k["arriving0"])
    wait()
    tiles = gathered(gat, True)
    curve, energy = summed(gat, (6, 7))
    step_0 = energy / curve
    c_res = c_res - step_0 * joined(tiles, 0)
    c_scaled = c_scaled - step_0 * joined(tiles, 1)
    for s in range(subs):
        residual[s] = residual[s] - step_0 * image[0][s]
    send, run, settle, drain, faces = ops[1]
    partial = direction(c_res, c_scaled, fresh, send)

    gat_e, esend, erecv, msg = gats[2]
    msg[0] = jnp.broadcast_to(partial, (loads, 128))
    start, wait_energy = at.everywhere(msg, gat_e, esend, erecv)
    start()
    gat_e[me] = msg[...]
    run()
    wait_energy()
    fresh_energy = summed(gat_e, (0,))[0]
    ratio = fresh_energy / energy
    gat, esend, erecv, msg = gats[3]
    sums = nothing
    at_rest = slice(2 * slot, interface)
    for p in range(4):
        settle(p)
        if p < 2:
            continue
        chosen = groups[p - 2]
        for s in chosen:
            fresh[s] = fresh[s] + ratio * search[s]
            mixed(image[1], s)
            for c in range(2):
                before = image[0][s, :, lanes(c)] + (
                    mask[s : s + 1, lanes(c)] * k["arriving0"][c, s // 4, s % 4]
                )
                image[1][s, :, lanes(c)] = image[1][s, :, lanes(c)] + ratio * before
            image[1][s, :, at_rest] = image[1][s, :, at_rest] + ratio * image[0][s, :, at_rest]
        coarse(msg, image[1], 3, False, chosen)
        sums = curve_of(fresh, image[1], chosen, sums)
    curve = curve_end(sums)
    msg[0] = jnp.where(lane == 6, curve, msg[0])
    start, wait = at.everywhere(msg, gat, esend, erecv)
    start()
    gat[me] = msg[...]
    drain()
    faces()
    k["arriving1"][...] = k["arriving1"][...] + ratio * k["arriving0"][...]
    finish_image(image[1], k["arriving1"])
    wait()
    tiles = gathered(gat, False)
    step_1 = fresh_energy / summed(gat, (6,))[0]
    c_res = c_res - step_1 * jnp.concatenate(tiles, axis=1)
    near = by_two(across_rows, c_res, pair_of(near_pair))
    for s in range(subs):
        mult_out[:, s, :] = step_0 * search[s] + step_1 * fresh[s]
        proj_out[:, s, :] = residual[s] - step_1 * image[1][s] - lift_of(near, s)


def deliver_kernel(first_in, second_in, first_out, second_out, held, sems):
    parts, depth = 2, held.shape[1] // 2

    def copy(n, out):
        which, part = n // parts, n % parts
        rows = pl.ds(part * depth, depth)
        middle = held.at[which, rows]
        if out:
            target = (first_out, second_out)[which].at[rows]
            return pltpu.make_async_copy(middle, target, sems.at[1, n])
        source = (first_in, second_in)[which].at[rows]
        return pltpu.make_async_copy(source, middle, sems.at[0, n])

    for n in range(2 * parts):
        copy(n, False).start()
    for n in range(2 * parts):
        copy(n, False).wait()
        copy(n, True).start()
    for n in range(2 * parts):
        copy(n, True).wait()


def by_kernels(schur_block, rigid_modes, coarse_inverse, dual_rhs, stiff_diag, face_length):
    loads, subs, interface = dual_rhs.shape
    rows = schur_block.shape[1]
    slot = interface // 6
    modes = rigid_modes.shape[1]
    vmem = pl.BlockSpec(memory_space=pltpu.VMEM)
    hbm = pl.BlockSpec(memory_space=pltpu.HBM)
    dma = pltpu.SemaphoreType.DMA
    order = NSUB * 64
    vector = pltpu.VMEM((subs, loads, interface), F32)
    edge = pltpu.VMEM((2, modes + 1, subs, slot), F32)
    face = pltpu.VMEM((2, 2, subs // 2, loads, slot), F32)
    basis = pltpu.VMEM((subs, 48, interface), BF16)
    square = pltpu.VMEM((order, order), BF16)
    scratch = {
        "hold": pltpu.VMEM((2, subs // 2, rows, interface), F32),
        "load_sem": dma((subs,)),
        "input_sem": dma((5,)),
        "edges": edge,
        "across": edge,
        "beyond": pltpu.VMEM((2, loads, subs, slot), F32),
        "rsend": dma((2,)),
        "rrecv": dma((2,)),
        "tsend": dma((2,)),
        "trecv": dma((2,)),
        "bsend": dma((2,)),
        "brecv": dma((2,)),
        "inverse": pltpu.VMEM((NCRS,) + coarse_inverse.shape, F32),
        "isend": dma((3,)),
        "irecv": dma((3,)),
        "wide": pltpu.VMEM((subs, 8, interface), F32),
        "rhs": vector,
        "mask": pltpu.VMEM((subs, interface), F32),
        "precond": pltpu.VMEM((subs, interface), F32),
        "basis_high": basis,
        "basis_low": basis,
        "residual": vector,
        "middle_msg": pltpu.VMEM((32, 128), F32),
        "middle_all": pltpu.VMEM((NSUB, 32, 128), F32),
        "msend": dma((NSUB,)),
        "mrecv": dma((NSUB,)),
        "q_high": square,
        "q_low": square,
        "near_high": square,
        "near_low": square,
        "m_high": square,
        "m_low": square,
        "packed": pltpu.VMEM((4, 7, loads, slot), F32),
        "search": vector,
        "fresh": vector,
        "product": pltpu.VMEM((2, subs // 2, loads, interface), F32),
        "image0": vector,
        "image1": vector,
        "res": pltpu.VMEM((2, subs // 2, NCRS, loads, rows), F32),
    }
    sources = [
        jnp.swapaxes(rigid_modes, 0, 1),
        coarse_inverse,
        dual_rhs,
        stiff_diag,
        face_length,
    ]
    scratch["cres"] = pltpu.VMEM((2, subs // 2, 2, loads, 3 * slot), F32)
    for n, source in enumerate(sources):
        scratch[f"input{n}"] = pltpu.VMEM(source.shape, source.dtype)
    for n, tiles in enumerate((1, 3, 1, 3)):
        scratch[f"msg{n}"] = pltpu.VMEM((tiles, loads, 128), F32)
        scratch[f"gat{n}"] = pltpu.VMEM((NSUB, tiles, loads, 128), F32)
        scratch[f"esend{n}"] = dma((NSUB,))
        scratch[f"erecv{n}"] = dma((NSUB,))
    for n in range(ITERS):
        scratch[f"op{n}_0"] = pltpu.VMEM((4, NCRS, 7, loads, slot), F32)
        scratch[f"op{n}_1"] = dma((3, 4))
        scratch[f"op{n}_2"] = dma((3, 4))
        scratch[f"op{n}_3"] = dma((3, 4, 2))
        scratch[f"op{n}_4"] = dma((NCRS, 4, 2))
        scratch[f"ctwin{n}"] = pltpu.VMEM((2, subs // 2, loads, 3 * slot), F32)
        scratch[f"csend{n}"] = dma((4,))
        scratch[f"crecv{n}"] = dma((4,))
        scratch[f"arriving{n}"] = face
        scratch[f"fsend{n}"] = dma((2, 4))
        scratch[f"frecv{n}"] = dma((2, 4))
    out = jax.ShapeDtypeStruct((loads, subs, interface), F32)
    results = pl.pallas_call(
        functools.partial(main_kernel, list(scratch)),
        out_shape=(out, out),
        in_specs=[hbm] * 6,
        out_specs=(vmem, vmem),
        scratch_shapes=list(scratch.values()),
        compiler_params=pltpu.CompilerParams(
            collective_id=0, has_side_effects=True, vmem_limit_bytes=56 * 1024 * 1024
        ),
        name="main",
    )(schur_block, *sources)
    return pl.pallas_call(
        deliver_kernel,
        out_shape=(out, out),
        in_specs=[hbm] * 2,
        out_specs=(hbm, hbm),
        scratch_shapes=[pltpu.VMEM((2, loads, subs, interface), F32), dma((2, 4))],
        compiler_params=pltpu.CompilerParams(vmem_limit_bytes=56 * 1024 * 1024),
        name="deliver",
    )(*results)


def shards(schur_block, rigid_modes, coarse_inverse, dual_rhs, stiff_diag, face_length):
    fits = dual_rhs.shape[0] == 8 and lax.axis_size("crs") == NCRS and lax.axis_size("sub") == NSUB
    build = by_kernels if fits else by_collectives
    return build(schur_block, rigid_modes, coarse_inverse, dual_rhs, stiff_diag, face_length)


def solution(mesh):
    return jax.shard_map(
        shards,
        mesh=mesh,
        in_specs=(
            P("sub", "crs", None),
            P("sub", None, None),
            P("crs", None),
            P("crs", "sub", None),
            P("sub", None),
            P("sub", None),
        ),
        out_specs=(P("crs", "sub", None), P("crs", "sub", None)),
        check_vma=False,
    )
```

```python
import functools

import jax
import jax.numpy as jnp
import numpy as np
from jax import lax
from jax.experimental import pallas as pl
from jax.experimental.pallas import tpu as pltpu
from jax.sharding import PartitionSpec as P

ITERS = 2
SY = 2
SZ = 4
SUBS = 8

PRECISE = lax.Precision.HIGHEST
SPLIT = lax.Precision.HIGH


def local_lookup():
    indices = np.arange(SUBS)
    coords = [indices // SZ, indices % SZ]
    extent = [SY, SZ]
    stride = [SZ, 1]
    lookup = np.zeros((4, SUBS), np.int32)
    for colour in range(4):
        axis_pick = colour // 2
        anchor = coords[axis_pick]
        offset = np.where(anchor % 2 == colour % 2, 1, -1)
        target = anchor + offset
        inside = (target >= 0) & (target < extent[axis_pick])
        lookup[colour] = np.where(inside, indices + offset * stride[axis_pick], indices)
    return lookup


def by_collectives(schur_block, rigid_modes, coarse_inverse, dual_rhs, stiff_diag, face_length):
    loads, subs, interface = dual_rhs.shape
    slot = interface // 6
    modes = rigid_modes.shape[1]
    own = subs * modes
    nsub = lax.axis_size("sub")
    sub_index = lax.axis_index("sub")
    even = sub_index % 2 == 0
    lookup = local_lookup()
    positions = jnp.arange(interface) % slot
    usable = (jnp.repeat(face_length, slot, axis=1) > positions[None, :]).astype(jnp.float32)
    up = [(i, i + 1) for i in range(nsub - 1)]
    down = [(i + 1, i) for i in range(nsub - 1)]

    def partner(vector):
        first = vector[..., :slot]
        second = vector[..., slot : 2 * slot]
        from_left = lax.ppermute(jnp.where(even, first, second), "sub", up)
        from_right = lax.ppermute(jnp.where(even, second, first), "sub", down)
        pieces = [jnp.where(even, from_right, from_left), jnp.where(even, from_left, from_right)]
        for colour in range(2, 6):
            window = vector[..., colour * slot : (colour + 1) * slot]
            pieces.append(
                jnp.concatenate([window[..., t : t + 1, :] for t in lookup[colour - 2]], axis=-2)
            )
        return jnp.concatenate(pieces, axis=-1)

    modes_first = jnp.swapaxes(rigid_modes, 0, 1)
    together = jnp.concatenate([dual_rhs, modes_first, stiff_diag[None]], axis=0)
    across = partner(together)
    residual = usable * (dual_rhs - across[:loads])
    modes_across = across[loads : loads + modes]
    precond = usable * (stiff_diag + across[-1])

    inverse = lax.all_gather(coarse_inverse, "crs", axis=0, tiled=True)

    def by_slot(array):
        return array.reshape(array.shape[:-1] + (6, slot))

    basis = by_slot(usable * jnp.concatenate([modes_first, -modes_across], axis=0))

    weighted = by_slot(modes_first * precond)
    blocks = jnp.einsum("msck,nsck->scmn", weighted, basis, precision=PRECISE)
    total_subs = nsub * subs
    here = sub_index * subs + jnp.arange(subs)
    left = here - subs
    right = here + subs
    targets = [jnp.where(even, right, left), jnp.where(even, left, right)]
    for colour in range(2, 6):
        targets.append(sub_index * subs + jnp.asarray(lookup[colour - 2]))
    targets = jnp.stack(targets, axis=1)
    hot_across = (targets[:, :, None] == jnp.arange(total_subs)).astype(jnp.float32)
    hot_here = (here[:, None] == jnp.arange(total_subs)).astype(jnp.float32)
    dense = jnp.einsum("smn,st->smtn", blocks[..., :modes].sum(axis=1), hot_here, precision=PRECISE)
    dense = dense + jnp.einsum("scmn,sct->smtn", blocks[..., modes:], hot_across, precision=PRECISE)
    dense = dense.reshape(own, total_subs * modes)
    middle = lax.all_gather(dense, "sub", axis=0, tiled=True)

    def coarse(vector):
        return jnp.einsum("lsi,msi->lsm", vector, modes_first, precision=PRECISE).reshape(loads, own)

    def dots(a, b):
        return jnp.sum(a * b, axis=(1, 2))[:, None]

    def shared(parts):
        gathered = lax.all_gather(jnp.concatenate(parts, axis=1), "sub", axis=0)
        count = own * (sum(part.shape[1] == own for part in parts))
        outs = []
        for at in range(0, count, own):
            outs.append(jnp.swapaxes(gathered[:, :, at : at + own], 0, 1).reshape(loads, nsub * own))
        sums = jnp.sum(gathered[:, :, count:], axis=0)
        return outs, [sums[:, j : j + 1] for j in range(sums.shape[1])]

    def solve(values):
        return jnp.einsum("lb,ab->la", values, inverse, precision=PRECISE)

    def lifted(values):
        grid = values.reshape(loads, nsub, subs, modes)
        padded = jnp.pad(grid, ((0, 0), (1, 1), (0, 0), (0, 0)))
        near = lax.dynamic_slice_in_dim(padded, sub_index, 3, axis=1)
        before, mine, after = near[:, 0], near[:, 1], near[:, 2]
        pieces = [jnp.where(even, after, before), jnp.where(even, before, after)]
        for colour in range(2, 6):
            pieces.append(jnp.stack([mine[:, t] for t in lookup[colour - 2]], axis=1))
        other = jnp.stack(pieces, axis=2)
        mine = jnp.broadcast_to(mine[:, :, None], other.shape)
        factors = jnp.concatenate([mine, other], axis=-1)
        out = jnp.einsum("lscm,msck->lsck", factors, basis, precision=PRECISE)
        return out.reshape(loads, subs, interface)

    def direction(residual, c_res, c_scaled, power):
        y = solve(c_res)
        my = jnp.einsum("lb,ab->la", y, middle, precision=PRECISE)
        energy = 0.5 * power - 2.0 * jnp.sum(y * c_scaled, axis=1, keepdims=True)
        energy = energy + jnp.sum(y * my, axis=1, keepdims=True)
        t = solve(c_scaled - my)
        return precond * (residual - lifted(y)) - lifted(t), energy

    scaled = precond * residual
    (c_res, c_scaled), (power,) = shared([coarse(residual), coarse(scaled), dots(residual, scaled)])
    search, energy = direction(residual, c_res, c_scaled, power)
    multipliers = None
    for iteration in range(ITERS):
        by_rows = jnp.einsum(
            "sij,lsj->lsi",
            schur_block,
            lax.all_gather(search, "crs", axis=0, tiled=True),
            precision=SPLIT,
        )
        product = lax.all_to_all(by_rows, "crs", split_axis=0, concat_axis=2, tiled=True)
        image = usable * (product - partner(product))
        last = iteration + 1 == ITERS
        curve = dots(search, product)
        if last:
            (c_image,), (curve,) = shared([coarse(image), curve])
        else:
            scaled_image = precond * image
            parts = [
                coarse(image),
                coarse(scaled_image),
                curve,
                dots(residual, scaled_image),
                dots(image, scaled_image),
            ]
            (c_image, c_scaled_image), (curve, cross, square) = shared(parts)
        step = energy / curve
        moved = step[:, :, None] * search
        multipliers = moved if multipliers is None else multipliers + moved
        residual = residual - step[:, :, None] * image
        c_res = c_res - step * c_image
        if last:
            projected = residual - lifted(solve(c_res))
        else:
            c_scaled = c_scaled - step * c_scaled_image
            power = power - 2.0 * step * cross + step * step * square
            fresh, energy_new = direction(residual, c_res, c_scaled, power)
            search = fresh + (energy_new / energy)[:, :, None] * search
            energy = energy_new
    return (multipliers, projected)


MESH = pl.DeviceIdType.MESH
F32 = jnp.float32
BF16 = jnp.bfloat16
NSUB = 8
NCRS = 4


def across_rows(a, b):
    return lax.dot_general(a, b, (((1,), (1,)), ((), ())), preferred_element_type=F32)


def along(a, b):
    return jnp.dot(a, b, preferred_element_type=F32)


def halves(x):
    high = x.astype(BF16)
    return high, (x - high.astype(F32)).astype(BF16)


def stacked(x):
    high = x.astype(BF16).astype(F32)
    return jnp.concatenate([high, x - high], axis=0).astype(BF16)


def folded(x):
    rows = x.shape[0] // 2
    return x[:rows] + x[rows:]


def by_two(product, x, pair):
    both = stacked(x)
    return folded(product(both, pair[0]) + product(both, pair[1]))


def near_of(block):
    low = block - 1 if block % 2 == 0 else block + 1
    return block ^ 1, (low if 0 <= low < NSUB else None)


def remote(src, dst, send, recv, target):
    return pltpu.make_async_remote_copy(
        src_ref=src,
        dst_ref=dst,
        send_sem=send,
        recv_sem=recv,
        device_id=target,
        device_id_type=MESH,
    )


class Place:
    def __init__(self):
        self.me = me = lax.axis_index("sub")
        self.q = q = lax.axis_index("crs")
        core = q % 2
        self.twin = q + 1 - 2 * core
        self.far = (q + 2) % NCRS
        self.diagonal = (self.twin + 2) % NCRS
        odd = me % 2
        self.first = me + 1 - 2 * odd
        self.second = me - 1 + 2 * odd
        self.has_second = jnp.logical_and(self.second >= 0, self.second < NSUB)

    def faces(self, src, dst, send, recv):
        return (
            remote(src(0), dst.at[0], send.at[0], recv.at[0], (self.first, self.q)),
            remote(src(1), dst.at[1], send.at[1], recv.at[1], (self.second, self.q)),
        )

    def start_faces(self, copies):
        copies[0].start()

        @pl.when(self.has_second)
        def _():
            copies[1].start()

    def wait_faces(self, copies):
        copies[0].wait()

        @pl.when(self.has_second)
        def _():
            copies[1].wait()

    def everywhere(self, src, gat, send, recv):
        def copy(k, block):
            return remote(
                src, gat.at[block], send.at[k], recv.at[k], ((self.me + k) % NSUB, self.q)
            )

        def start():
            for k in range(1, NSUB):
                copy(k, self.me).start()

        def wait():
            for k in range(1, NSUB):
                copy(k, (self.me + NSUB - k) % NSUB).wait_recv()
            for k in range(1, NSUB):
                copy(k, self.me).wait_send()

        return start, wait


def chunk_size(p):
    return 5 if p == 3 else 7


def operate(at, packed, hold, res, product, buffers, arriving, fsend, frecv):
    gath, gsend, grecv, asend, arecv, cres, ctwin, csend, crecv = buffers[:9]
    lres, ltwin, lsend, lrecv = buffers[9:]
    me, q = at.me, at.q
    lower = q < 2
    upper = q >= 2
    rows = hold.shape[2]
    loads = packed.shape[2]

    def to_far(p, span, block):
        return remote(
            packed.at[p, pl.ds(*span)],
            gath.at[p, block, pl.ds(*span)],
            gsend.at[1, p],
            grecv.at[1, p],
            (me, at.far),
        )

    def to_twin(p, n, block):
        return remote(
            packed.at[p, pl.ds(0, n)],
            gath.at[p, block, pl.ds(0, n)],
            gsend.at[0, p],
            grecv.at[0, p],
            (me, at.twin),
        )

    def relay(p, span, source, block):
        return remote(
            gath.at[p, source, pl.ds(*span)],
            gath.at[p, block, pl.ds(*span)],
            gsend.at[2, p],
            grecv.at[2, p],
            (me, at.twin),
        )

    wanted = {0: (5, 2), 1: (0, 7), 2: (0, 7)}

    def by_side(p, low, up, action):
        for side, span in ((lower, low), (upper, up)):
            if span is not None:
                pl.when(side)(functools.partial(action, span))

    def sending(p, action):
        by_side(p, wanted.get(p), (0, 5), action)

    def receiving(p, action):
        pl.when(lower)(functools.partial(action, (0, 5)))
        pl.when(jnp.logical_and(upper, p == 0))(functools.partial(action, (5, 2)))
        pl.when(jnp.logical_and(upper, fifth(p)))(functools.partial(action, (0, 7)))

    def send(p):
        n = chunk_size(p)
        sending(p, lambda span: to_far(p, span, q).start())
        to_twin(p, n, q).start()
        gath[p, q, 0:n] = packed[p, 0:n]

    def sized(small, action):
        pl.when(jnp.logical_not(small))(functools.partial(action, 7))
        pl.when(small)(functools.partial(action, 5))

    def forward(p, span):
        to_far(p, span, at.far).wait_recv()
        relay(p, span, at.far, at.far).start()

    peers = (at.twin, at.far, at.diagonal)

    def pieces(owner, p):
        if owner == 0:
            return [(lambda b: res.at[:, p, b], product.at[:, p, :, 0:384], 0, None)]
        if owner == 1:
            return [
                (lambda b: res.at[0, p, b], product.at[0, p, :, 384:768], 0, None),
                (lambda b: res.at[1, p, b, :, 0:128], product.at[1, p, :, 384:512], 1, None),
            ]
        odd = p % 2 == 1
        if owner == 2:
            source = lambda b: res.at[:, p - 1, b, :, 256:384]
            return [(source, product.at[:, p - 1, :, 1024:1152], 0, odd)]
        source = lambda b: res.at[:, p - 1, b, :, 0:128]
        inner = lambda b: res.at[:, 1, b, :, 128:384]
        return [
            (source, product.at[:, p - 1, :, 1152:1280], 0, odd),
            (inner, product.at[:, 1, :, 1280:1536], 1, p == 2),
        ]

    def give(piece, p, j):
        source, target, i, _ = piece
        return remote(
            source(peers[j]), target, asend.at[j, p, i], arecv.at[q, p, i], (me, peers[j])
        )

    def guarded(condition, action):
        if condition is None or condition is True:
            action()
        elif condition is not False:
            pl.when(condition)(action)

    def send_back(p):
        for owner in range(NCRS):

            @pl.when(q == owner)
            def _():
                for n, piece in enumerate(pieces(owner, p)):

                    def action():
                        if owner == 1 and n == 0:
                            res[0, p, :, :, 128:384] = (
                                res[0, p, :, :, 128:384] - res[1, p, :, :, 128:384]
                            )
                        if owner == 2:
                            res[:, p - 1, :, :, 256:384] = (
                                res[:, p - 1, :, :, 256:384] - res[:, p, :, :, 256:384]
                            )
                        if owner == 3 and n == 0:
                            res[:, p - 1, :, :, 0:128] = (
                                res[:, p - 1, :, :, 0:128] - res[:, p, :, :, 0:128]
                            )
                        if owner == 3 and n == 1:
                            res[:, 1, :, :, 128:384] = (
                                res[:, 1, :, :, 128:384] - res[:, 2, :, :, 128:384]
                            )
                        for j in range(3):
                            give(piece, p, j).start()
                        source, target, _, _ = piece
                        target[...] = source(owner)[...]

                    guarded(piece[3], action)

    def tripled(product_of, x, w):
        high_w, low_w = halves(w)
        return folded(product_of(x, high_w)) + product_of(x[: x.shape[0] // 2], low_w)

    def block(chunk, j, first, last):
        return gath[chunk, first:last, j].reshape((last - first) * loads, 256)

    def signs(p):
        sign = (1 - 2 * (p % 2)).astype(F32)
        last = jnp.where(p == 1, 1, jnp.where(p == 2, -1, 0)).astype(F32)
        return sign, p - p % 2, last, jnp.where(p == 0, 0, 1)

    def outer_slots(p, y, first=0, last=NCRS):
        middle = block(p, 4, first, last)
        return [
            block(p, 2 * y, first, last),
            block(p, 2 * y + 1, first, last),
            middle if y == 0 else -middle,
        ]

    def all_outer(p, y, first=0, last=NCRS):
        return stacked(jnp.concatenate(outer_slots(p, y, first, last), axis=1))

    def fifth(p):
        return jnp.logical_or(p == 1, p == 2)

    def share(p):
        return remote(
            cres.at[:, p, at.twin % 2], ctwin.at[:, p], csend.at[p], crecv.at[p], (me, at.twin)
        )

    def low_share(half):
        return remote(
            lres.at[half, :, at.twin % 2],
            ltwin.at[half],
            lsend.at[half],
            lrecv.at[half],
            (me, at.twin),
        )

    def prepare(p, carry):
        sized(p == 3, lambda n: to_twin(p, n, at.twin).wait_recv())
        sign, even, last, held = signs(p)

        @pl.when(lower)
        def _():
            for y in range(2):
                x = stacked(sign * block(even, 5 + y, 0, 2))
                out = tripled(across_rows, x, hold[y, p, :, 1024:1280])
                res[y, p, 0:2] = out.reshape(2, loads, rows)

            @pl.when(fifth(p))
            def _():
                for y in range(2):
                    x = stacked(last * block(held, 5 + y, 0, 2))
                    out = tripled(across_rows, x, hold[y, p, :, 1280:1536])
                    res[y, p, 0:2] = res[y, p, 0:2] + out.reshape(2, loads, rows)

            @pl.when(jnp.logical_not(fifth(p)))
            def _():
                half = p // 3
                for y in range(2):
                    zeroth, first, second = outer_slots(p, y, 0, 2)
                    x = jnp.where(
                        q == 0,
                        jnp.concatenate([zeroth, first[:, 0:128]], axis=1),
                        jnp.concatenate([first[:, 128:256], second], axis=1),
                    )
                    out = tripled(along, stacked(sign * x), hold[y, p, :, 1024:1280])
                    lres[half, y] = out.reshape(2, loads, 256)
                low_share(half).start()

        @pl.when(upper)
        def _():
            def part(x, y, first, end):
                return tripled(along, stacked(x), hold[y, p, first:end, 0:768])

            @pl.when(q == 2)
            def _():
                for y in range(2):
                    x = sign * block(even, 5 + y, 2, 4)
                    out = part(x[:, 0:128], y, 256, 384)
                    cres[y, p] = out.reshape(2, loads, 768)

            @pl.when(q == 3)
            def _():
                for y in range(2):
                    x = sign * block(even, 5 + y, 2, 4)
                    out = part(x[:, 128:256], y, 0, 128)
                    cres[y, p] = out.reshape(2, loads, 768)

                @pl.when(fifth(p))
                def _():
                    for y in range(2):
                        out = part(last * block(held, 5 + y, 2, 4), y, 128, 384)
                        cres[y, p] = cres[y, p] + out.reshape(2, loads, 768)

            cres[0, p, :, :, 512:768] = cres[0, p, :, :, 512:768] - cres[1, p, :, :, 512:768]
            share(p).start()

        return carry

    def multiply(p, carry):
        @pl.when(p < 3)
        def _():
            receiving(p + 1, lambda span: forward(p + 1, span))

        receiving(p, lambda span: relay(p, span, at.far, at.diagonal).wait_recv())
        sign, even, last, held = signs(p)

        @pl.when(lower)
        def _():
            for y in range(2):
                out = tripled(across_rows, all_outer(p, y), hold[y, p, :, 0:768])
                out = out.reshape(NCRS, loads, rows)
                res[y, p, 0:2] = res[y, p, 0:2] + out[0:2]
                res[y, p, 2:4] = out[2:4]

        def upper_rows(first, end, with_fifth):
            for y in range(2):
                inner = sign * block(even, 5 + y, 0, NCRS)
                size = 256
                if with_fifth:
                    inner = jnp.concatenate([inner, last * block(held, 5 + y, 0, NCRS)], axis=1)
                    size = 512
                inner = tripled(
                    across_rows, stacked(inner), hold[y, p, first:end, 1024 : 1024 + size]
                ).reshape(NCRS, loads, end - first)
                start = 0 if with_fifth else 2
                outer = tripled(
                    across_rows, all_outer(p, y, start, NCRS), hold[y, p, first:end, 0:768]
                ).reshape(NCRS - start, loads, end - first)
                res[y, p, start:NCRS, :, first:end] = inner[start:] + outer
                if start:
                    res[y, p, 0:start, :, first:end] = inner[:start]

        for owner, begin, middle, end in ((2, 256, 384, 384), (3, 0, 384, 128)):

            @pl.when(q == owner)
            def _():
                pl.when(fifth(p))(functools.partial(upper_rows, begin, middle, True))
                pl.when(jnp.logical_not(fifth(p)))(
                    functools.partial(upper_rows, begin, end, False)
                )

        send_back(p)
        return carry

    def run():
        lax.fori_loop(0, 4, prepare, 0)
        receiving(0, lambda span: forward(0, span))
        lax.fori_loop(0, 4, multiply, 0)

    def face(c, p):
        return remote(
            product.at[:, p, :, pl.ds(256 * c, 256)],
            arriving.at[c, :, p],
            fsend.at[c, p],
            frecv.at[c, p],
            (at.second if c else at.first, q),
        )

    def returned(owner, p):
        for piece in pieces(owner, p):
            if piece[3] is None or piece[3]:
                _, target, i, _ = piece
                remote(
                    target, target, asend.at[0, p, i], arecv.at[owner, p, i], (me, at.twin)
                ).wait_recv()

    def settle(p):
        for owner in range(2):
            pl.when(q != owner)(functools.partial(returned, owner, p))

        @pl.when(upper)
        def _():
            share(p).wait_recv()
            mine = q % 2
            for y in range(2):
                span = slice(0, 768 if y == 0 else 512)
                product[y, p, :, span] = product[y, p, :, span] + (
                    cres[y, p, mine, :, span] + ctwin[y, p, :, span]
                )

        face(0, p).start()
        pl.when(at.has_second)(face(1, p).start)
        for owner in (2, 3):
            if any(piece[3] for piece in pieces(owner, p)):
                pl.when(q != owner)(functools.partial(returned, owner, p))
        if p % 2 == 1:

            @pl.when(lower)
            def _():
                half = p // 3
                low_share(half).wait_recv()
                for y in range(2):
                    product[y, p - 1, :, 1024:1280] = product[y, p - 1, :, 1024:1280] + (
                        lres[half, y, q % 2] + ltwin[half, y]
                    )

    def faces():
        for p in range(4):
            face(0, p).wait()
            pl.when(at.has_second)(face(1, p).wait)

    def drain():
        for p in range(4):
            n = chunk_size(p)
            sending(p, lambda span: to_far(p, span, q).wait_send())
            to_twin(p, n, q).wait_send()
            by_side(
                p,
                (0, 5),
                wanted.get(p),
                lambda span: relay(p, span, at.far, at.far).wait_send(),
            )
            pl.when(upper)(lambda: share(p).wait_send())
            if p in (0, 3):
                pl.when(lower)(lambda: low_share(p // 3).wait_send())
        for owner in range(NCRS):

            @pl.when(q == owner)
            def _():
                for p in range(4):
                    for piece in pieces(owner, p):
                        if piece[3] is None or piece[3]:
                            for j in range(3):
                                give(piece, p, j).wait_send()

    return send, run, settle, drain, faces


class Held:
    def __init__(self, names, refs):
        refs = iter(refs)
        for name, count in names:
            setattr(self, name, [next(refs) for _ in range(count)] if count else next(refs))


def inner_partner(c, s):
    if c == 2:
        return s ^ 4
    if c == 4:
        return s ^ 1
    return s ^ 3 if s % 4 in (1, 2) else None


def main_kernel(names, schur, *refs):
    sources, (mult_out, proj_out) = refs[:5], refs[5:7]
    k = Held(names, refs[7:])
    inputs = k.input
    modes_in, inverse_in, rhs_in, stiff_in, length_in = inputs
    fetches = [
        pltpu.make_async_copy(source, held, k.input_sem.at[n])
        for n, (source, held) in enumerate(zip(sources, inputs))
    ]
    for copy in fetches:
        copy.start()
    loads, subs, interface = rhs_in.shape
    slot = interface // 6
    modes = modes_in.shape[0]
    at = Place()
    me, q = at.me, at.q
    hold, load_sem = k.hold, k.load_sem

    def lanes(c):
        return slice(c * slot, (c + 1) * slot)

    def load(s):
        return pltpu.make_async_copy(
            schur.at[s], hold.at[s // 4, s % 4], load_sem.at[s]
        )

    barrier = pltpu.get_barrier_semaphore()
    for j in range(1, NSUB):
        pl.semaphore_signal(
            barrier, inc=1, device_id=((me + j) % NSUB, q), device_id_type=MESH
        )
    for j in range(1, NCRS):
        pl.semaphore_signal(barrier, inc=1, device_id=(me, (q + j) % NCRS), device_id_type=MESH)

    for copy in fetches:
        copy.wait()
    edges, across = k.edges, k.across
    for c in range(2):
        edges[c, 0:modes] = modes_in[:, :, lanes(c)]
        edges[c, modes] = stiff_in[:, lanes(c)]
    pl.semaphore_wait(barrier, NSUB + NCRS - 2)

    core = q % 2

    def begin(c):
        target = (at.second if c else at.first, q)
        return remote(edges.at[c], across.at[c], k.bsend.at[c], k.brecv.at[c], target)

    def share(c):
        return remote(
            across.at[c], across.at[c], k.tsend.at[c], k.trecv.at[c], (me, at.twin)
        )

    pl.when(core == 0)(lambda: begin(0).start())
    pl.when((core == 1) & at.has_second)(lambda: begin(1).start())
    beyond = k.beyond
    right = at.faces(lambda c: rhs_in.at[:, :, lanes(c)], beyond, k.rsend, k.rrecv)
    at.start_faces(right)
    inverse, isend, irecv = k.inverse, k.isend, k.irecv

    def inverse_far(block):
        return remote(inverse_in, inverse.at[block], isend.at[1], irecv.at[1], (me, at.far))

    def inverse_twin(block):
        return remote(inverse_in, inverse.at[block], isend.at[0], irecv.at[0], (me, at.twin))

    def inverse_relay(block):
        return remote(
            inverse.at[at.far], inverse.at[block], isend.at[2], irecv.at[2], (me, at.twin)
        )

    inverse_far(q).start()
    inverse_twin(q).start()
    inverse[q] = inverse_in[...]

    @pl.when(jnp.logical_not(at.has_second))
    def _():
        across[1] = jnp.zeros(across.shape[1:], F32)
        beyond[1] = jnp.zeros(beyond.shape[1:], F32)

    wide, rhs, mask, precond = k.wide, k.rhs, k.mask, k.precond
    position = lax.broadcasted_iota(jnp.int32, (subs, slot), 1)
    for c in range(6):
        mask[:, lanes(c)] = (length_in[:, c : c + 1] > position).astype(F32)
    blank = jnp.zeros((8 - modes, interface), F32)
    for s in range(subs):
        rhs[s] = rhs_in[:, s, :]
        wide[s] = jnp.concatenate([modes_in[:, s, :], blank], axis=0)
    precond[:, lanes(3)] = jnp.zeros((subs, slot), F32)
    for c in (2, 4, 5):
        other = jnp.concatenate(
            [
                stiff_in[t : t + 1, lanes(c)]
                for t in [inner_partner(c, s) or 0 for s in range(subs)]
            ],
            axis=0,
        )
        precond[:, lanes(c)] = mask[:, lanes(c)] * (stiff_in[:, lanes(c)] + other)

    high, low = k.basis_high, k.basis_low

    def put(s, rows, window, value):
        a, b = halves(value)
        high[s, rows, window] = a
        low[s, rows, window] = b

    zero = jnp.zeros((8, slot), F32)
    for s in range(subs):
        inner = {}
        for c in (2, 4, 5):
            t = inner_partner(c, s)
            inner[c] = zero if t is None else -mask[s : s + 1, lanes(c)] * wide[t, :, lanes(c)]
        for c in range(6):
            upper = inner[2] if c == 2 else zero
            if c >= 2:
                put(s, slice(16, 32), lanes(c), jnp.concatenate([zero, upper], axis=0))
                own = mask[s : s + 1, lanes(c)] * wide[s, :, lanes(c)]
                put(s, slice(0, 16), lanes(c), jnp.concatenate([own, zero], axis=0))
            last = jnp.concatenate(
                [inner[4] if c == 4 else zero, inner[5] if c == 5 else zero], axis=0
            )
            put(s, slice(32, 48), lanes(c), last)


    @pl.when(core == 0)
    def _():
        begin(0).wait()
        share(0).start()
        pl.when(at.has_second)(lambda: share(1).wait_recv())
        share(0).wait_send()

    @pl.when(core == 1)
    def _():
        @pl.when(at.has_second)
        def _():
            begin(1).wait()
            share(1).start()

        share(0).wait_recv()
        pl.when(at.has_second)(lambda: share(1).wait_send())

    for c in range(2):
        precond[:, lanes(c)] = mask[:, lanes(c)] * (stiff_in[:, lanes(c)] + across[c, modes])
    small = jnp.zeros((8 - modes, slot), F32)
    for s in range(subs):
        for c in range(2):
            line = mask[s : s + 1, lanes(c)]
            own = line * wide[s, :, lanes(c)]
            outer = -line * jnp.concatenate([across[c, 0:modes, s, :], small], axis=0)
            put(
                s,
                slice(0, 16),
                lanes(c),
                jnp.concatenate([own, outer if c == 0 else zero], axis=0),
            )
            put(
                s,
                slice(16, 32),
                lanes(c),
                jnp.concatenate([outer if c == 1 else zero, zero], axis=0),
            )

    middle_msg, middle_all = k.middle_msg, k.middle_all
    middle_msg[...] = jnp.zeros(middle_msg.shape, F32)
    for s in range(subs):
        weighted = wide[s] * precond[s : s + 1]
        block = by_two(across_rows, weighted, (high[s], low[s]))
        line, first = 8 * (s % 4), 64 * (s // 4)
        middle_msg[line : line + 8, first : first + 48] = block
    start_middle, wait_middle = at.everywhere(
        middle_msg, middle_all, k.msend, k.mrecv
    )
    start_middle()
    middle_all[me] = middle_msg[...]

    residual = k.residual
    for s in range(subs):
        residual[s, :, lanes(3)] = jnp.zeros((loads, slot), F32)
        for c in (2, 4, 5):
            t = inner_partner(c, s)
            residual[s, :, lanes(c)] = mask[s : s + 1, lanes(c)] * (
                rhs[s, :, lanes(c)] - rhs[0 if t is None else t, :, lanes(c)]
            )
    at.wait_faces(right)
    for s in range(subs):
        for c in range(2):
            residual[s, :, lanes(c)] = mask[s : s + 1, lanes(c)] * (
                rhs[s, :, lanes(c)] - beyond[c, :, s, :]
            )

    gats = [(k.gat[n], k.esend[n], k.erecv[n], k.msg[n]) for n in range(4)]

    def coarse(msg, vector, tiles, scaled, chosen):
        for s in chosen:
            v = vector[s]
            if scaled:
                v = jnp.concatenate([v, precond[s : s + 1] * v], axis=0)
            out = by_two(across_rows, v, (high[s, 0:32], low[s, 0:32]))
            for t in range(tiles):
                part = out[:, 8 * t : 8 * t + 8]
                msg[t, :, 8 * s : 8 * s + 8] = part[:loads]
                if scaled:
                    msg[t, :, 64 + 8 * s : 72 + 8 * s] = part[loads:]

    lane = lax.broadcasted_iota(jnp.int32, (loads, 128), 1)
    gat, esend, erecv, msg = gats[0]
    coarse(msg, residual, 1, True, range(subs))
    start, wait_first = at.everywhere(msg, gat, esend, erecv)
    start()
    gat[me] = msg[...]
    for s in range(subs):
        load(s).start()

    inverse_far(at.far).wait_recv()
    inverse_relay(at.far).start()
    order = NSUB * 64
    full_order = NSUB * subs * modes
    row = lax.broadcasted_iota(jnp.int32, (order, full_order), 0)
    column = lax.broadcasted_iota(jnp.int32, (order, full_order), 1)
    widen = jnp.where((row % 8 < modes) & (row // 8 * modes + row % 8 == column), 1.0, 0.0)
    widen = widen.astype(BF16)
    row = lax.broadcasted_iota(jnp.int32, (order, 192), 0)
    column = lax.broadcasted_iota(jnp.int32, (order, 192), 1)
    s_of, j_of, n_of = row // 64, row // 8 % 8, row % 8
    source = jnp.where(j_of == 3, s_of ^ 4, jnp.where(j_of == 4, s_of ^ 1, s_of))
    source = jnp.where(j_of == 5, s_of ^ 3, source)
    wanted = jnp.where(j_of <= 2, 64 * j_of, 0) + 8 * source + n_of
    choose = jnp.where((j_of <= 5) & (wanted == column), 1.0, 0.0).astype(BF16)
    inverse_twin(at.twin).wait_recv()
    inverse_relay(at.diagonal).wait_recv()
    all_rows = inverse[...].reshape(full_order, full_order)
    present = at.has_second.astype(F32)
    there = jnp.where(at.has_second, at.second, 0)
    for part, whole, chosen in zip(
        halves(all_rows), (k.q_high, k.q_low), (k.near_high, k.near_low)
    ):
        tall = along(widen, part).astype(BF16)
        whole[...] = across_rows(tall, widen).astype(BF16)
        near = jnp.concatenate(
            [
                whole[pl.ds(pl.multiple_of(64 * me, 64), 64), :].astype(F32),
                whole[pl.ds(pl.multiple_of(64 * at.first, 64), 64), :].astype(F32),
                present * whole[pl.ds(pl.multiple_of(64 * there, 64), 64), :].astype(F32),
            ],
            axis=0,
        ).astype(BF16)
        chosen[...] = along(choose, near).astype(BF16)
    q_pair = (k.q_high, k.q_low)
    near_pair = (k.near_high, k.near_low)
    m_pair = (k.m_high, k.m_low)
    for ref in m_pair:
        ref[...] = jnp.zeros(ref.shape, BF16)
    inverse_far(q).wait_send()
    inverse_twin(q).wait_send()
    inverse_relay(at.far).wait_send()

    wait_middle()
    row = lax.broadcasted_iota(jnp.int32, (64, 384), 0)
    column = lax.broadcasted_iota(jnp.int32, (64, 384), 1)
    spread = jnp.where(row == column // 64 * 8 + column % 8, 1.0, 0.0).astype(BF16)
    row = lax.broadcasted_iota(jnp.int32, (64, 64), 0) // 8
    column = lax.broadcasted_iota(jnp.int32, (64, 64), 1) // 8
    same = (row == column).astype(F32)
    inner_masks = [(row ^ flip == column).astype(F32) for flip in (4, 1, 3)]
    compact = [middle_all[t, :, 64 * h : 64 * h + 64] for t in range(NSUB) for h in range(2)]
    for part, whole in zip(halves(jnp.concatenate(compact, axis=0)), m_pair):
        wide_part = along(part, spread)
        for t in range(NSUB):
            piece = wide_part[64 * t : 64 * t + 64]
            own = same * piece[:, 0:64]
            for j in range(3):
                own = own + inner_masks[j] * piece[:, 64 * (j + 3) : 64 * (j + 4)]
            first, second = near_of(t)
            whole[64 * t : 64 * t + 64, 64 * t : 64 * t + 64] = own.astype(BF16)
            whole[64 * t : 64 * t + 64, 64 * first : 64 * first + 64] = (
                same * piece[:, 64:128]
            ).astype(BF16)
            if second is not None:
                whole[64 * t : 64 * t + 64, 64 * second : 64 * second + 64] = (
                    same * piece[:, 128:192]
                ).astype(BF16)

    def pair_of(pair):
        return pair[0][...], pair[1][...]

    def joined(tiles, half):
        return jnp.concatenate([t[:, 64 * half : 64 * half + 64] for t in tiles], axis=1)

    def lift_of(coefficients, s):
        part = coefficients[:, 64 * s : 64 * s + 48]
        return by_two(along, part, (high[s], low[s]))

    packed = k.packed

    def pack(value, s):
        y, z = s // 4, s % 4
        packed[z, 2 * y] = value[:, lanes(0)]
        packed[z, 2 * y + 1] = value[:, lanes(1)]
        if y == 0:
            packed[z, 4] = value[:, lanes(2)]
        if z % 2 == 0:
            packed[z, 5 + y] = value[:, lanes(4)]
        if z == 1:
            packed[z, 5 + y] = value[:, lanes(5)]

    def direction(c_res, c_scaled, target, send):
        y = by_two(across_rows, c_res, pair_of(q_pair))
        c_scaled = c_scaled - by_two(across_rows, y, pair_of(m_pair))
        both = jnp.concatenate([c_res, c_scaled], axis=0)
        near = by_two(across_rows, both, pair_of(near_pair))
        total = jnp.zeros((loads, interface), F32)
        for p in range(subs // 2):
            for s in (p, p + subs // 2):
                lifted = lift_of(near, s)
                projected = residual[s] - lifted[:loads]
                scaled = precond[s : s + 1] * projected
                total = total + projected * scaled
                value = scaled - lifted[loads:]
                target[s] = value
                pack(value, s)
            send(p)
        return 0.5 * jnp.sum(total, axis=1, keepdims=True)

    wait_first()
    tiles = [gat[t, 0] for t in range(NSUB)]
    c_res, c_scaled = joined(tiles, 0), joined(tiles, 1)
    search, fresh = k.search, k.fresh
    product = k.product
    arrivals = [[k.arriving[n], k.fsend[n], k.frecv[n]] for n in range(2)]
    ops = [
        operate(
            at,
            packed,
            hold,
            k.res,
            product,
            [k.gath[n], k.gsend[n], k.grecv[n], k.asend[n], k.arecv[n]]
            + [k.cres, k.ctwin[n], k.csend[n], k.crecv[n]]
            + [k.lres, k.ltwin[n], k.lsend[n], k.lrecv[n]],
            *arrivals[n],
        )
        for n in range(ITERS)
    ]
    send, run, settle, drain, faces = ops[0]
    partial = direction(c_res, c_scaled, search, send)
    for s in range(subs):
        load(s).wait()
    image = k.image

    def mixed(target, s):
        y, z = s // 4, s % 4
        for c in range(2):
            target[s, :, lanes(c)] = mask[s : s + 1, lanes(c)] * product[y, z, :, lanes(c)]
        target[s, :, lanes(3)] = jnp.zeros((loads, slot), F32)
        for c in (2, 4, 5):
            t = inner_partner(c, s)
            if t is None:
                target[s, :, lanes(c)] = jnp.zeros((loads, slot), F32)
                continue
            owner = min(s, t)
            value = mask[s : s + 1, lanes(c)] * product[owner // 4, owner % 4, :, lanes(c)]
            target[s, :, lanes(c)] = value if s == owner else -value

    def finish_image(target, arriving):
        for s in range(subs):
            for c in range(2):
                target[s, :, lanes(c)] = (
                    target[s, :, lanes(c)]
                    - mask[s : s + 1, lanes(c)] * arriving[c, s // 4, s % 4]
                )

    def curve_of(direct, values, chosen, sums):
        for s in chosen:
            both = direct[s] * values[s]
            sums = (sums[0] + both[:, : 2 * slot], sums[1] + both[:, 2 * slot :])
        return sums

    def curve_end(sums):
        total = jnp.sum(sums[0], axis=1, keepdims=True)
        return total + 0.5 * jnp.sum(sums[1], axis=1, keepdims=True)

    groups = [[s for s in range(subs) if s % 4 // 2 == half] for half in range(2)]
    nothing = (jnp.zeros((loads, 2 * slot), F32), jnp.zeros((loads, 4 * slot), F32))

    def no_second():
        for n in range(2):
            k.arriving[n][1] = jnp.zeros(k.arriving[n].shape[1:], F32)

    pl.when(jnp.logical_not(at.has_second))(no_second)

    def gathered(gat, scaled):
        tiles = []
        for t in range(NSUB):
            first, second = near_of(t)
            if scaled:
                tile = gat[t, 0] + gat[first, 1]
                if second is not None:
                    tile = tile + gat[second, 2]
            else:
                tile = gat[t, 0][:, 0:64] + gat[first, 1][:, 0:64]
                if second is not None:
                    tile = tile + gat[second, 2][:, 0:64]
            tiles.append(tile)
        return tiles

    def summed(gat, at_lane):
        total = gat[0, 0]
        for t in range(1, NSUB):
            total = total + gat[t, 0]
        return [total[:, n : n + 1] for n in at_lane]

    run()
    gat, esend, erecv, msg = gats[1]
    sums = nothing
    for p in range(4):
        settle(p)
        if p >= 2:
            chosen = groups[p - 2]
            for s in chosen:
                mixed(image[0], s)
            coarse(msg, image[0], 3, True, chosen)
            sums = curve_of(search, image[0], chosen, sums)
    curve = curve_end(sums)
    msg[0] = jnp.where(lane == 6, curve, jnp.where(lane == 7, partial, msg[0]))
    start, wait = at.everywhere(msg, gat, esend, erecv)
    start()
    gat[me] = msg[...]
    drain()
    faces()
    finish_image(image[0], k.arriving[0])
    wait()
    tiles = gathered(gat, True)
    curve, energy = summed(gat, (6, 7))
    step_0 = energy / curve
    c_res = c_res - step_0 * joined(tiles, 0)
    c_scaled = c_scaled - step_0 * joined(tiles, 1)
    for s in range(subs):
        residual[s] = residual[s] - step_0 * image[0][s]
    send, run, settle, drain, faces = ops[1]
    partial = direction(c_res, c_scaled, fresh, send)

    gat_e, esend, erecv, msg = gats[2]
    msg[0] = jnp.broadcast_to(partial, (loads, 128))
    start, wait_energy = at.everywhere(msg, gat_e, esend, erecv)
    start()
    gat_e[me] = msg[...]
    run()
    wait_energy()
    fresh_energy = summed(gat_e, (0,))[0]
    ratio = fresh_energy / energy
    gat, esend, erecv, msg = gats[3]
    sums = nothing
    at_rest = slice(2 * slot, interface)
    for p in range(4):
        settle(p)
        if p < 2:
            continue
        chosen = groups[p - 2]
        for s in chosen:
            fresh[s] = fresh[s] + ratio * search[s]
            mixed(image[1], s)
            for c in range(2):
                before = image[0][s, :, lanes(c)] + (
                    mask[s : s + 1, lanes(c)] * k.arriving[0][c, s // 4, s % 4]
                )
                image[1][s, :, lanes(c)] = image[1][s, :, lanes(c)] + ratio * before
            image[1][s, :, at_rest] = image[1][s, :, at_rest] + ratio * image[0][s, :, at_rest]
        coarse(msg, image[1], 3, False, chosen)
        sums = curve_of(fresh, image[1], chosen, sums)
    curve = curve_end(sums)
    msg[0] = jnp.where(lane == 6, curve, msg[0])
    start, wait = at.everywhere(msg, gat, esend, erecv)
    start()
    gat[me] = msg[...]
    drain()
    faces()
    k.arriving[1][...] = k.arriving[1][...] + ratio * k.arriving[0][...]
    finish_image(image[1], k.arriving[1])
    wait()
    tiles = gathered(gat, False)
    step_1 = fresh_energy / summed(gat, (6,))[0]
    c_res = c_res - step_1 * jnp.concatenate(tiles, axis=1)
    near = by_two(across_rows, c_res, pair_of(near_pair))
    for s in range(subs):
        mult_out[:, s, :] = step_0 * search[s] + step_1 * fresh[s]
        proj_out[:, s, :] = residual[s] - step_1 * image[1][s] - lift_of(near, s)


def deliver_kernel(first_in, second_in, first_out, second_out, held, sems):
    parts, depth = 2, held.shape[1] // 2

    def copy(n, out):
        which, part = n // parts, n % parts
        rows = pl.ds(part * depth, depth)
        middle = held.at[which, rows]
        if out:
            target = (first_out, second_out)[which].at[rows]
            return pltpu.make_async_copy(middle, target, sems.at[1, n])
        source = (first_in, second_in)[which].at[rows]
        return pltpu.make_async_copy(source, middle, sems.at[0, n])

    for n in range(2 * parts):
        copy(n, False).start()
    for n in range(2 * parts):
        copy(n, False).wait()
        copy(n, True).start()
    for n in range(2 * parts):
        copy(n, True).wait()


def by_kernels(schur_block, rigid_modes, coarse_inverse, dual_rhs, stiff_diag, face_length):
    loads, subs, interface = dual_rhs.shape
    rows = schur_block.shape[1]
    slot = interface // 6
    modes = rigid_modes.shape[1]
    vmem = pl.BlockSpec(memory_space=pltpu.VMEM)
    hbm = pl.BlockSpec(memory_space=pltpu.HBM)
    dma = pltpu.SemaphoreType.DMA
    order = NSUB * 64
    vector = pltpu.VMEM((subs, loads, interface), F32)
    edge = pltpu.VMEM((2, modes + 1, subs, slot), F32)
    face = pltpu.VMEM((2, 2, subs // 2, loads, slot), F32)
    basis = pltpu.VMEM((subs, 48, interface), BF16)
    square = pltpu.VMEM((order, order), BF16)
    scratch = dict(
        hold=pltpu.VMEM((2, subs // 2, rows, interface), F32),
        load_sem=dma((subs,)),
        input_sem=dma((5,)),
        edges=edge,
        across=edge,
        beyond=pltpu.VMEM((2, loads, subs, slot), F32),
        rsend=dma((2,)),
        rrecv=dma((2,)),
        tsend=dma((2,)),
        trecv=dma((2,)),
        bsend=dma((2,)),
        brecv=dma((2,)),
        inverse=pltpu.VMEM((NCRS,) + coarse_inverse.shape, F32),
        isend=dma((3,)),
        irecv=dma((3,)),
        wide=pltpu.VMEM((subs, 8, interface), F32),
        rhs=vector,
        mask=pltpu.VMEM((subs, interface), F32),
        precond=pltpu.VMEM((subs, interface), F32),
        basis_high=basis,
        basis_low=basis,
        residual=vector,
        middle_msg=pltpu.VMEM((32, 128), F32),
        middle_all=pltpu.VMEM((NSUB, 32, 128), F32),
        msend=dma((NSUB,)),
        mrecv=dma((NSUB,)),
        q_high=square,
        q_low=square,
        near_high=square,
        near_low=square,
        m_high=square,
        m_low=square,
        packed=pltpu.VMEM((4, 7, loads, slot), F32),
        search=vector,
        fresh=vector,
        product=pltpu.VMEM((2, subs // 2, loads, interface), F32),
        image=[vector] * 2,
        res=pltpu.VMEM((2, subs // 2, NCRS, loads, rows), F32),
    )
    sources = [
        jnp.swapaxes(rigid_modes, 0, 1),
        coarse_inverse,
        dual_rhs,
        stiff_diag,
        face_length,
    ]
    tiles = (1, 3, 1, 3)
    third = pltpu.VMEM((2, subs // 2, loads, 3 * slot), F32)
    scratch.update(
        cres=pltpu.VMEM((2, subs // 2, 2, loads, 3 * slot), F32),
        input=[pltpu.VMEM(source.shape, source.dtype) for source in sources],
        msg=[pltpu.VMEM((n, loads, 128), F32) for n in tiles],
        gat=[pltpu.VMEM((NSUB, n, loads, 128), F32) for n in tiles],
        esend=[dma((NSUB,))] * 4,
        erecv=[dma((NSUB,))] * 4,
        gath=[pltpu.VMEM((4, NCRS, 7, loads, slot), F32)] * ITERS,
        gsend=[dma((3, 4))] * ITERS,
        grecv=[dma((3, 4))] * ITERS,
        asend=[dma((3, 4, 2))] * ITERS,
        arecv=[dma((NCRS, 4, 2))] * ITERS,
        ctwin=[third] * ITERS,
        csend=[dma((4,))] * ITERS,
        crecv=[dma((4,))] * ITERS,
        lres=pltpu.VMEM((2, 2, 2, loads, slot), F32),
        ltwin=[pltpu.VMEM((2, 2, loads, slot), F32)] * ITERS,
        lsend=[dma((2,))] * ITERS,
        lrecv=[dma((2,))] * ITERS,
        arriving=[face] * ITERS,
        fsend=[dma((2, 4))] * ITERS,
        frecv=[dma((2, 4))] * ITERS,
    )
    names = [(name, len(v) if isinstance(v, list) else 0) for name, v in scratch.items()]
    shapes = [one for v in scratch.values() for one in (v if isinstance(v, list) else [v])]
    out = jax.ShapeDtypeStruct((loads, subs, interface), F32)
    results = pl.pallas_call(
        functools.partial(main_kernel, names),
        out_shape=(out, out),
        in_specs=[hbm] * 6,
        out_specs=(vmem, vmem),
        scratch_shapes=shapes,
        compiler_params=pltpu.CompilerParams(
            collective_id=0, has_side_effects=True, vmem_limit_bytes=56 * 1024 * 1024
        ),
        name="main",
    )(schur_block, *sources)
    return pl.pallas_call(
        deliver_kernel,
        out_shape=(out, out),
        in_specs=[hbm] * 2,
        out_specs=(hbm, hbm),
        scratch_shapes=[pltpu.VMEM((2, loads, subs, interface), F32), dma((2, 4))],
        compiler_params=pltpu.CompilerParams(vmem_limit_bytes=56 * 1024 * 1024),
        name="deliver",
    )(*results)


def shards(schur_block, rigid_modes, coarse_inverse, dual_rhs, stiff_diag, face_length):
    fits = dual_rhs.shape[0] == 8 and lax.axis_size("crs") == NCRS and lax.axis_size("sub") == NSUB
    build = by_kernels if fits else by_collectives
    return build(schur_block, rigid_modes, coarse_inverse, dual_rhs, stiff_diag, face_length)


def solution(mesh):
    return jax.shard_map(
        shards,
        mesh=mesh,
        in_specs=(
            P("sub", "crs", None),
            P("sub", None, None),
            P("crs", None),
            P("crs", "sub", None),
            P("sub", None),
            P("sub", None),
        ),
        out_specs=(P("crs", "sub", None), P("crs", "sub", None)),
        check_vma=False,
    )
```

```python
import functools

import jax
import jax.numpy as jnp
import numpy as np
from jax import lax
from jax.experimental import pallas as pl
from jax.experimental.pallas import tpu as pltpu
from jax.sharding import PartitionSpec as P

ITERS = 2
SY = 2
SZ = 4
SUBS = 8

PRECISE = lax.Precision.HIGHEST
SPLIT = lax.Precision.HIGH


def local_lookup():
    indices = np.arange(SUBS)
    coords = [indices // SZ, indices % SZ]
    extent = [SY, SZ]
    stride = [SZ, 1]
    lookup = np.zeros((4, SUBS), np.int32)
    for colour in range(4):
        axis_pick = colour // 2
        anchor = coords[axis_pick]
        offset = np.where(anchor % 2 == colour % 2, 1, -1)
        target = anchor + offset
        inside = (target >= 0) & (target < extent[axis_pick])
        lookup[colour] = np.where(inside, indices + offset * stride[axis_pick], indices)
    return lookup


def by_collectives(schur_block, rigid_modes, coarse_inverse, dual_rhs, stiff_diag, face_length):
    loads, subs, interface = dual_rhs.shape
    slot = interface // 6
    modes = rigid_modes.shape[1]
    own = subs * modes
    nsub = lax.axis_size("sub")
    sub_index = lax.axis_index("sub")
    even = sub_index % 2 == 0
    lookup = local_lookup()
    positions = jnp.arange(interface) % slot
    usable = (jnp.repeat(face_length, slot, axis=1) > positions[None, :]).astype(jnp.float32)
    up = [(i, i + 1) for i in range(nsub - 1)]
    down = [(i + 1, i) for i in range(nsub - 1)]

    def partner(vector):
        first = vector[..., :slot]
        second = vector[..., slot : 2 * slot]
        from_left = lax.ppermute(jnp.where(even, first, second), "sub", up)
        from_right = lax.ppermute(jnp.where(even, second, first), "sub", down)
        pieces = [jnp.where(even, from_right, from_left), jnp.where(even, from_left, from_right)]
        for colour in range(2, 6):
            window = vector[..., colour * slot : (colour + 1) * slot]
            pieces.append(
                jnp.concatenate([window[..., t : t + 1, :] for t in lookup[colour - 2]], axis=-2)
            )
        return jnp.concatenate(pieces, axis=-1)

    modes_first = jnp.swapaxes(rigid_modes, 0, 1)
    together = jnp.concatenate([dual_rhs, modes_first, stiff_diag[None]], axis=0)
    across = partner(together)
    residual = usable * (dual_rhs - across[:loads])
    modes_across = across[loads : loads + modes]
    precond = usable * (stiff_diag + across[-1])

    inverse = lax.all_gather(coarse_inverse, "crs", axis=0, tiled=True)

    def by_slot(array):
        return array.reshape(array.shape[:-1] + (6, slot))

    basis = by_slot(usable * jnp.concatenate([modes_first, -modes_across], axis=0))

    weighted = by_slot(modes_first * precond)
    blocks = jnp.einsum("msck,nsck->scmn", weighted, basis, precision=PRECISE)
    total_subs = nsub * subs
    here = sub_index * subs + jnp.arange(subs)
    left = here - subs
    right = here + subs
    targets = [jnp.where(even, right, left), jnp.where(even, left, right)]
    for colour in range(2, 6):
        targets.append(sub_index * subs + jnp.asarray(lookup[colour - 2]))
    targets = jnp.stack(targets, axis=1)
    hot_across = (targets[:, :, None] == jnp.arange(total_subs)).astype(jnp.float32)
    hot_here = (here[:, None] == jnp.arange(total_subs)).astype(jnp.float32)
    dense = jnp.einsum("smn,st->smtn", blocks[..., :modes].sum(axis=1), hot_here, precision=PRECISE)
    dense = dense + jnp.einsum("scmn,sct->smtn", blocks[..., modes:], hot_across, precision=PRECISE)
    dense = dense.reshape(own, total_subs * modes)
    middle = lax.all_gather(dense, "sub", axis=0, tiled=True)

    def coarse(vector):
        return jnp.einsum("lsi,msi->lsm", vector, modes_first, precision=PRECISE).reshape(loads, own)

    def dots(a, b):
        return jnp.sum(a * b, axis=(1, 2))[:, None]

    def shared(parts):
        gathered = lax.all_gather(jnp.concatenate(parts, axis=1), "sub", axis=0)
        count = own * (sum(part.shape[1] == own for part in parts))
        outs = []
        for at in range(0, count, own):
            outs.append(jnp.swapaxes(gathered[:, :, at : at + own], 0, 1).reshape(loads, nsub * own))
        sums = jnp.sum(gathered[:, :, count:], axis=0)
        return outs, [sums[:, j : j + 1] for j in range(sums.shape[1])]

    def solve(values):
        return jnp.einsum("lb,ab->la", values, inverse, precision=PRECISE)

    def lifted(values):
        grid = values.reshape(loads, nsub, subs, modes)
        padded = jnp.pad(grid, ((0, 0), (1, 1), (0, 0), (0, 0)))
        near = lax.dynamic_slice_in_dim(padded, sub_index, 3, axis=1)
        before, mine, after = near[:, 0], near[:, 1], near[:, 2]
        pieces = [jnp.where(even, after, before), jnp.where(even, before, after)]
        for colour in range(2, 6):
            pieces.append(jnp.stack([mine[:, t] for t in lookup[colour - 2]], axis=1))
        other = jnp.stack(pieces, axis=2)
        mine = jnp.broadcast_to(mine[:, :, None], other.shape)
        factors = jnp.concatenate([mine, other], axis=-1)
        out = jnp.einsum("lscm,msck->lsck", factors, basis, precision=PRECISE)
        return out.reshape(loads, subs, interface)

    def direction(residual, c_res, c_scaled, power):
        y = solve(c_res)
        my = jnp.einsum("lb,ab->la", y, middle, precision=PRECISE)
        energy = 0.5 * power - 2.0 * jnp.sum(y * c_scaled, axis=1, keepdims=True)
        energy = energy + jnp.sum(y * my, axis=1, keepdims=True)
        t = solve(c_scaled - my)
        return precond * (residual - lifted(y)) - lifted(t), energy

    scaled = precond * residual
    (c_res, c_scaled), (power,) = shared([coarse(residual), coarse(scaled), dots(residual, scaled)])
    search, energy = direction(residual, c_res, c_scaled, power)
    multipliers = None
    for iteration in range(ITERS):
        by_rows = jnp.einsum(
            "sij,lsj->lsi",
            schur_block,
            lax.all_gather(search, "crs", axis=0, tiled=True),
            precision=SPLIT,
        )
        product = lax.all_to_all(by_rows, "crs", split_axis=0, concat_axis=2, tiled=True)
        image = usable * (product - partner(product))
        last = iteration + 1 == ITERS
        curve = dots(search, product)
        if last:
            (c_image,), (curve,) = shared([coarse(image), curve])
        else:
            scaled_image = precond * image
            parts = [
                coarse(image),
                coarse(scaled_image),
                curve,
                dots(residual, scaled_image),
                dots(image, scaled_image),
            ]
            (c_image, c_scaled_image), (curve, cross, square) = shared(parts)
        step = energy / curve
        moved = step[:, :, None] * search
        multipliers = moved if multipliers is None else multipliers + moved
        residual = residual - step[:, :, None] * image
        c_res = c_res - step * c_image
        if last:
            projected = residual - lifted(solve(c_res))
        else:
            c_scaled = c_scaled - step * c_scaled_image
            power = power - 2.0 * step * cross + step * step * square
            fresh, energy_new = direction(residual, c_res, c_scaled, power)
            search = fresh + (energy_new / energy)[:, :, None] * search
            energy = energy_new
    return (multipliers, projected)


MESH = pl.DeviceIdType.MESH
F32 = jnp.float32
BF16 = jnp.bfloat16
NSUB = 8
NCRS = 4


def across_rows(a, b):
    return lax.dot_general(a, b, (((1,), (1,)), ((), ())), preferred_element_type=F32)


def along(a, b):
    return jnp.dot(a, b, preferred_element_type=F32)


def halves(x):
    high = x.astype(BF16)
    return high, (x - high.astype(F32)).astype(BF16)


def stacked(x):
    high = x.astype(BF16).astype(F32)
    return jnp.concatenate([high, x - high], axis=0).astype(BF16)


def folded(x):
    rows = x.shape[0] // 2
    return x[:rows] + x[rows:]


def by_two(product, x, pair):
    both = stacked(x)
    return folded(product(both, pair[0]) + product(both, pair[1]))


def near_of(block):
    low = block - 1 if block % 2 == 0 else block + 1
    return block ^ 1, (low if 0 <= low < NSUB else None)


def remote(src, dst, send, recv, target):
    return pltpu.make_async_remote_copy(
        src_ref=src,
        dst_ref=dst,
        send_sem=send,
        recv_sem=recv,
        device_id=target,
        device_id_type=MESH,
    )


class Place:
    def __init__(self):
        self.me = me = lax.axis_index("sub")
        self.q = q = lax.axis_index("crs")
        core = q % 2
        self.twin = q + 1 - 2 * core
        self.far = (q + 2) % NCRS
        self.diagonal = (self.twin + 2) % NCRS
        odd = me % 2
        self.first = me + 1 - 2 * odd
        self.second = me - 1 + 2 * odd
        self.has_second = jnp.logical_and(self.second >= 0, self.second < NSUB)

    def faces(self, src, dst, send, recv):
        return (
            remote(src(0), dst.at[0], send.at[0], recv.at[0], (self.first, self.q)),
            remote(src(1), dst.at[1], send.at[1], recv.at[1], (self.second, self.q)),
        )

    def start_faces(self, copies):
        copies[0].start()

        @pl.when(self.has_second)
        def _():
            copies[1].start()

    def wait_faces(self, copies):
        copies[0].wait()

        @pl.when(self.has_second)
        def _():
            copies[1].wait()

    def everywhere(self, src, gat, send, recv):
        def copy(k, block):
            return remote(
                src, gat.at[block], send.at[k], recv.at[k], ((self.me + k) % NSUB, self.q)
            )

        def start():
            for k in range(1, NSUB):
                copy(k, self.me).start()

        def wait():
            for k in range(1, NSUB):
                copy(k, (self.me + NSUB - k) % NSUB).wait_recv()
            for k in range(1, NSUB):
                copy(k, self.me).wait_send()

        return start, wait


def chunk_size(p):
    return 5 if p == 3 else 7


def operate(at, packed, hold, res, product, buffers, arriving, fsend, frecv):
    gath, gsend, grecv, asend, arecv, cres, ctwin, csend, crecv = buffers[:9]
    lres, ltwin, lsend, lrecv = buffers[9:]
    me, q = at.me, at.q
    lower = q < 2
    upper = q >= 2
    rows = hold.shape[2]
    loads = packed.shape[2]

    def to_far(p, span, block):
        return remote(
            packed.at[p, pl.ds(*span)],
            gath.at[p, block, pl.ds(*span)],
            gsend.at[1, p],
            grecv.at[1, p],
            (me, at.far),
        )

    def to_twin(p, n, block):
        return remote(
            packed.at[p, pl.ds(0, n)],
            gath.at[p, block, pl.ds(0, n)],
            gsend.at[0, p],
            grecv.at[0, p],
            (me, at.twin),
        )

    def relay(p, span, source, block):
        return remote(
            gath.at[p, source, pl.ds(*span)],
            gath.at[p, block, pl.ds(*span)],
            gsend.at[2, p],
            grecv.at[2, p],
            (me, at.twin),
        )

    wanted = {0: (5, 2), 1: (0, 7), 2: (0, 7)}

    def by_side(p, low, up, action):
        for side, span in ((lower, low), (upper, up)):
            if span is not None:
                pl.when(side)(functools.partial(action, span))

    def sending(p, action):
        by_side(p, wanted.get(p), (0, 5), action)

    def receiving(p, action):
        pl.when(lower)(functools.partial(action, (0, 5)))
        pl.when(jnp.logical_and(upper, p == 0))(functools.partial(action, (5, 2)))
        pl.when(jnp.logical_and(upper, fifth(p)))(functools.partial(action, (0, 7)))

    def send(p):
        n = chunk_size(p)
        sending(p, lambda span: to_far(p, span, q).start())
        to_twin(p, n, q).start()
        gath[p, q, 0:n] = packed[p, 0:n]

    def sized(small, action):
        pl.when(jnp.logical_not(small))(functools.partial(action, 7))
        pl.when(small)(functools.partial(action, 5))

    def forward(p, span):
        to_far(p, span, at.far).wait_recv()
        relay(p, span, at.far, at.far).start()

    peers = (at.twin, at.far, at.diagonal)

    def pieces(owner, p):
        if owner == 0:
            return [(lambda b: res.at[:, p, b], product.at[:, p, :, 0:384], 0, None)]
        if owner == 1:
            return [
                (lambda b: res.at[0, p, b], product.at[0, p, :, 384:768], 0, None),
                (lambda b: res.at[1, p, b, :, 0:128], product.at[1, p, :, 384:512], 1, None),
            ]
        odd = p % 2 == 1
        if owner == 2:
            source = lambda b: res.at[:, p - 1, b, :, 256:384]
            return [(source, product.at[:, p - 1, :, 1024:1152], 0, odd)]
        source = lambda b: res.at[:, p - 1, b, :, 0:128]
        inner = lambda b: res.at[:, 1, b, :, 128:384]
        return [
            (source, product.at[:, p - 1, :, 1152:1280], 0, odd),
            (inner, product.at[:, 1, :, 1280:1536], 1, p == 2),
        ]

    def give(piece, p, j):
        source, target, i, _ = piece
        return remote(
            source(peers[j]), target, asend.at[j, p, i], arecv.at[q, p, i], (me, peers[j])
        )

    def guarded(condition, action):
        if condition is None or condition is True:
            action()
        elif condition is not False:
            pl.when(condition)(action)

    def send_back(p):
        for owner in range(NCRS):

            @pl.when(q == owner)
            def _():
                for n, piece in enumerate(pieces(owner, p)):

                    def action():
                        if owner == 1 and n == 0:
                            res[0, p, :, :, 128:384] = (
                                res[0, p, :, :, 128:384] - res[1, p, :, :, 128:384]
                            )
                        if owner == 2:
                            res[:, p - 1, :, :, 256:384] = (
                                res[:, p - 1, :, :, 256:384] - res[:, p, :, :, 256:384]
                            )
                        if owner == 3 and n == 0:
                            res[:, p - 1, :, :, 0:128] = (
                                res[:, p - 1, :, :, 0:128] - res[:, p, :, :, 0:128]
                            )
                        if owner == 3 and n == 1:
                            res[:, 1, :, :, 128:384] = (
                                res[:, 1, :, :, 128:384] - res[:, 2, :, :, 128:384]
                            )
                        for j in range(3):
                            give(piece, p, j).start()
                        source, target, _, _ = piece
                        target[...] = source(owner)[...]

                    guarded(piece[3], action)

    def tripled(product_of, x, w):
        high_w, low_w = halves(w)
        return folded(product_of(x, high_w)) + product_of(x[: x.shape[0] // 2], low_w)

    def block(chunk, j, first, last):
        return gath[chunk, first:last, j].reshape((last - first) * loads, 256)

    def signs(p):
        sign = (1 - 2 * (p % 2)).astype(F32)
        last = jnp.where(p == 1, 1, jnp.where(p == 2, -1, 0)).astype(F32)
        return sign, p - p % 2, last, jnp.where(p == 0, 0, 1)

    def outer_slots(p, y, first=0, last=NCRS):
        middle = block(p, 4, first, last)
        return [
            block(p, 2 * y, first, last),
            block(p, 2 * y + 1, first, last),
            middle if y == 0 else -middle,
        ]

    def all_outer(p, y, first=0, last=NCRS):
        return stacked(jnp.concatenate(outer_slots(p, y, first, last), axis=1))

    def fifth(p):
        return jnp.logical_or(p == 1, p == 2)

    def share(p):
        return remote(
            cres.at[:, p, at.twin % 2], ctwin.at[:, p], csend.at[p], crecv.at[p], (me, at.twin)
        )

    def low_share(half):
        return remote(
            lres.at[half, :, at.twin % 2],
            ltwin.at[half],
            lsend.at[half],
            lrecv.at[half],
            (me, at.twin),
        )

    def prepare(p, carry):
        sized(p == 3, lambda n: to_twin(p, n, at.twin).wait_recv())
        sign, even, last, held = signs(p)

        @pl.when(lower)
        def _():
            for y in range(2):
                x = stacked(sign * block(even, 5 + y, 0, 2))
                out = tripled(across_rows, x, hold[y, p, :, 1024:1280])
                res[y, p, 0:2] = out.reshape(2, loads, rows)

            @pl.when(fifth(p))
            def _():
                for y in range(2):
                    x = stacked(last * block(held, 5 + y, 0, 2))
                    out = tripled(across_rows, x, hold[y, p, :, 1280:1536])
                    res[y, p, 0:2] = res[y, p, 0:2] + out.reshape(2, loads, rows)

            @pl.when(jnp.logical_not(fifth(p)))
            def _():
                half = p // 3
                for y in range(2):
                    zeroth, first, second = outer_slots(p, y, 0, 2)
                    x = jnp.where(
                        q == 0,
                        jnp.concatenate([zeroth, first[:, 0:128]], axis=1),
                        jnp.concatenate([first[:, 128:256], second], axis=1),
                    )
                    out = tripled(along, stacked(sign * x), hold[y, p, :, 1024:1280])
                    lres[half, y] = out.reshape(2, loads, 256)
                low_share(half).start()

        @pl.when(upper)
        def _():
            def part(x, y, first, end):
                return tripled(along, stacked(x), hold[y, p, first:end, 0:768])

            @pl.when(q == 2)
            def _():
                for y in range(2):
                    x = sign * block(even, 5 + y, 2, 4)
                    out = part(x[:, 0:128], y, 256, 384)
                    cres[y, p] = out.reshape(2, loads, 768)

            @pl.when(q == 3)
            def _():
                for y in range(2):
                    x = sign * block(even, 5 + y, 2, 4)
                    out = part(x[:, 128:256], y, 0, 128)
                    cres[y, p] = out.reshape(2, loads, 768)

                @pl.when(fifth(p))
                def _():
                    for y in range(2):
                        out = part(last * block(held, 5 + y, 2, 4), y, 128, 384)
                        cres[y, p] = cres[y, p] + out.reshape(2, loads, 768)

            cres[0, p, :, :, 512:768] = cres[0, p, :, :, 512:768] - cres[1, p, :, :, 512:768]
            share(p).start()

        return carry

    def multiply(p, carry):
        @pl.when(p < 3)
        def _():
            receiving(p + 1, lambda span: forward(p + 1, span))

        receiving(p, lambda span: relay(p, span, at.far, at.diagonal).wait_recv())
        sign, even, last, held = signs(p)

        @pl.when(lower)
        def _():
            for y in range(2):
                out = tripled(across_rows, all_outer(p, y), hold[y, p, :, 0:768])
                out = out.reshape(NCRS, loads, rows)
                res[y, p, 0:2] = res[y, p, 0:2] + out[0:2]
                res[y, p, 2:4] = out[2:4]

        def upper_rows(first, end, with_fifth):
            for y in range(2):
                inner = sign * block(even, 5 + y, 0, NCRS)
                size = 256
                if with_fifth:
                    inner = jnp.concatenate([inner, last * block(held, 5 + y, 0, NCRS)], axis=1)
                    size = 512
                inner = tripled(
                    across_rows, stacked(inner), hold[y, p, first:end, 1024 : 1024 + size]
                ).reshape(NCRS, loads, end - first)
                start = 0 if with_fifth else 2
                outer = tripled(
                    across_rows, all_outer(p, y, start, NCRS), hold[y, p, first:end, 0:768]
                ).reshape(NCRS - start, loads, end - first)
                res[y, p, start:NCRS, :, first:end] = inner[start:] + outer
                if start:
                    res[y, p, 0:start, :, first:end] = inner[:start]

        for owner, begin, middle, end in ((2, 256, 384, 384), (3, 0, 384, 128)):

            @pl.when(q == owner)
            def _():
                pl.when(fifth(p))(functools.partial(upper_rows, begin, middle, True))
                pl.when(jnp.logical_not(fifth(p)))(
                    functools.partial(upper_rows, begin, end, False)
                )

        send_back(p)
        return carry

    def run():
        lax.fori_loop(0, 4, prepare, 0)
        receiving(0, lambda span: forward(0, span))
        lax.fori_loop(0, 4, multiply, 0)

    def face(c, p):
        return remote(
            product.at[:, p, :, pl.ds(256 * c, 256)],
            arriving.at[c, :, p],
            fsend.at[c, p],
            frecv.at[c, p],
            (at.second if c else at.first, q),
        )

    def returned(owner, p):
        for piece in pieces(owner, p):
            if piece[3] is None or piece[3]:
                _, target, i, _ = piece
                remote(
                    target, target, asend.at[0, p, i], arecv.at[owner, p, i], (me, at.twin)
                ).wait_recv()

    def settle(p):
        for owner in range(2):
            pl.when(q != owner)(functools.partial(returned, owner, p))

        @pl.when(upper)
        def _():
            share(p).wait_recv()
            mine = q % 2
            for y in range(2):
                span = slice(0, 768 if y == 0 else 512)
                product[y, p, :, span] = product[y, p, :, span] + (
                    cres[y, p, mine, :, span] + ctwin[y, p, :, span]
                )

        face(0, p).start()
        pl.when(at.has_second)(face(1, p).start)
        for owner in (2, 3):
            if any(piece[3] for piece in pieces(owner, p)):
                pl.when(q != owner)(functools.partial(returned, owner, p))
        if p % 2 == 1:

            @pl.when(lower)
            def _():
                half = p // 3
                low_share(half).wait_recv()
                for y in range(2):
                    product[y, p - 1, :, 1024:1280] = product[y, p - 1, :, 1024:1280] + (
                        lres[half, y, q % 2] + ltwin[half, y]
                    )

    def faces():
        for p in range(4):
            face(0, p).wait()
            pl.when(at.has_second)(face(1, p).wait)

    def drain():
        for p in range(4):
            n = chunk_size(p)
            sending(p, lambda span: to_far(p, span, q).wait_send())
            to_twin(p, n, q).wait_send()
            by_side(
                p,
                (0, 5),
                wanted.get(p),
                lambda span: relay(p, span, at.far, at.far).wait_send(),
            )
            pl.when(upper)(lambda: share(p).wait_send())
            if p in (0, 3):
                pl.when(lower)(lambda: low_share(p // 3).wait_send())
        for owner in range(NCRS):

            @pl.when(q == owner)
            def _():
                for p in range(4):
                    for piece in pieces(owner, p):
                        if piece[3] is None or piece[3]:
                            for j in range(3):
                                give(piece, p, j).wait_send()

    return send, run, settle, drain, faces


class Held:
    def __init__(self, names, refs):
        refs = iter(refs)
        for name, count in names:
            setattr(self, name, [next(refs) for _ in range(count)] if count else next(refs))


def inner_partner(c, s):
    if c == 2:
        return s ^ 4
    if c == 4:
        return s ^ 1
    return s ^ 3 if s % 4 in (1, 2) else None


def main_kernel(names, schur, *refs):
    sources, (mult_out, proj_out) = refs[:5], refs[5:7]
    k = Held(names, refs[7:])
    inputs = k.input
    modes_in, inverse_in, rhs_in, stiff_in, length_in = inputs
    fetches = [
        pltpu.make_async_copy(source, held, k.input_sem.at[n])
        for n, (source, held) in enumerate(zip(sources, inputs))
    ]
    for copy in fetches:
        copy.start()
    loads, subs, interface = rhs_in.shape
    slot = interface // 6
    modes = modes_in.shape[0]
    at = Place()
    me, q = at.me, at.q
    hold, load_sem = k.hold, k.load_sem

    def lanes(c):
        return slice(c * slot, (c + 1) * slot)

    def load(s):
        return pltpu.make_async_copy(
            schur.at[s], hold.at[s // 4, s % 4], load_sem.at[s]
        )

    barrier = pltpu.get_barrier_semaphore()
    for j in range(1, NSUB):
        pl.semaphore_signal(
            barrier, inc=1, device_id=((me + j) % NSUB, q), device_id_type=MESH
        )
    for j in range(1, NCRS):
        pl.semaphore_signal(barrier, inc=1, device_id=(me, (q + j) % NCRS), device_id_type=MESH)

    for copy in fetches:
        copy.wait()
    edges, across = k.edges, k.across
    for c in range(2):
        edges[c, 0:modes] = modes_in[:, :, lanes(c)]
        edges[c, modes] = stiff_in[:, lanes(c)]
    pl.semaphore_wait(barrier, NSUB + NCRS - 2)

    core = q % 2

    def begin(c):
        target = (at.second if c else at.first, q)
        return remote(edges.at[c], across.at[c], k.bsend.at[c], k.brecv.at[c], target)

    def share(c):
        return remote(
            across.at[c], across.at[c], k.tsend.at[c], k.trecv.at[c], (me, at.twin)
        )

    pl.when(core == 0)(lambda: begin(0).start())
    pl.when((core == 1) & at.has_second)(lambda: begin(1).start())
    beyond = k.beyond
    right = at.faces(lambda c: rhs_in.at[:, :, lanes(c)], beyond, k.rsend, k.rrecv)
    at.start_faces(right)
    inverse, isend, irecv = k.inverse, k.isend, k.irecv

    def inverse_far(block):
        return remote(inverse_in, inverse.at[block], isend.at[1], irecv.at[1], (me, at.far))

    def inverse_twin(block):
        return remote(inverse_in, inverse.at[block], isend.at[0], irecv.at[0], (me, at.twin))

    def inverse_relay(block):
        return remote(
            inverse.at[at.far], inverse.at[block], isend.at[2], irecv.at[2], (me, at.twin)
        )

    inverse_far(q).start()
    inverse_twin(q).start()
    inverse[q] = inverse_in[...]

    @pl.when(jnp.logical_not(at.has_second))
    def _():
        across[1] = jnp.zeros(across.shape[1:], F32)
        beyond[1] = jnp.zeros(beyond.shape[1:], F32)

    wide, rhs, mask, precond = k.wide, k.rhs, k.mask, k.precond
    position = lax.broadcasted_iota(jnp.int32, (subs, slot), 1)
    for c in range(6):
        mask[:, lanes(c)] = (length_in[:, c : c + 1] > position).astype(F32)
    blank = jnp.zeros((8 - modes, interface), F32)
    for s in range(subs):
        rhs[s] = rhs_in[:, s, :]
        wide[s] = jnp.concatenate([modes_in[:, s, :], blank], axis=0)
    precond[:, lanes(3)] = jnp.zeros((subs, slot), F32)
    for c in (2, 4, 5):
        other = jnp.concatenate(
            [
                stiff_in[t : t + 1, lanes(c)]
                for t in [inner_partner(c, s) or 0 for s in range(subs)]
            ],
            axis=0,
        )
        precond[:, lanes(c)] = mask[:, lanes(c)] * (stiff_in[:, lanes(c)] + other)

    high, low = k.basis_high, k.basis_low

    def put(s, rows, window, value):
        a, b = halves(value)
        high[s, rows, window] = a
        low[s, rows, window] = b

    zero = jnp.zeros((8, slot), F32)
    for s in range(subs):
        inner = {}
        for c in (2, 4, 5):
            t = inner_partner(c, s)
            inner[c] = zero if t is None else -mask[s : s + 1, lanes(c)] * wide[t, :, lanes(c)]
        for c in range(6):
            upper = inner[2] if c == 2 else zero
            if c >= 2:
                put(s, slice(16, 32), lanes(c), jnp.concatenate([zero, upper], axis=0))
                own = mask[s : s + 1, lanes(c)] * wide[s, :, lanes(c)]
                put(s, slice(0, 16), lanes(c), jnp.concatenate([own, zero], axis=0))
            last = jnp.concatenate(
                [inner[4] if c == 4 else zero, inner[5] if c == 5 else zero], axis=0
            )
            put(s, slice(32, 48), lanes(c), last)


    @pl.when(core == 0)
    def _():
        begin(0).wait()
        share(0).start()
        pl.when(at.has_second)(lambda: share(1).wait_recv())
        share(0).wait_send()

    @pl.when(core == 1)
    def _():
        @pl.when(at.has_second)
        def _():
            begin(1).wait()
            share(1).start()

        share(0).wait_recv()
        pl.when(at.has_second)(lambda: share(1).wait_send())

    for c in range(2):
        precond[:, lanes(c)] = mask[:, lanes(c)] * (stiff_in[:, lanes(c)] + across[c, modes])
    small = jnp.zeros((8 - modes, slot), F32)
    for s in range(subs):
        for c in range(2):
            line = mask[s : s + 1, lanes(c)]
            own = line * wide[s, :, lanes(c)]
            outer = -line * jnp.concatenate([across[c, 0:modes, s, :], small], axis=0)
            put(
                s,
                slice(0, 16),
                lanes(c),
                jnp.concatenate([own, outer if c == 0 else zero], axis=0),
            )
            put(
                s,
                slice(16, 32),
                lanes(c),
                jnp.concatenate([outer if c == 1 else zero, zero], axis=0),
            )

    middle_msg, middle_all = k.middle_msg, k.middle_all
    middle_msg[...] = jnp.zeros(middle_msg.shape, F32)
    for s in range(subs):
        weighted = wide[s] * precond[s : s + 1]
        block = by_two(across_rows, weighted, (high[s], low[s]))
        line, first = 8 * (s % 4), 64 * (s // 4)
        middle_msg[line : line + 8, first : first + 48] = block
    start_middle, wait_middle = at.everywhere(
        middle_msg, middle_all, k.msend, k.mrecv
    )
    start_middle()
    middle_all[me] = middle_msg[...]

    residual = k.residual
    for s in range(subs):
        residual[s, :, lanes(3)] = jnp.zeros((loads, slot), F32)
        for c in (2, 4, 5):
            t = inner_partner(c, s)
            residual[s, :, lanes(c)] = mask[s : s + 1, lanes(c)] * (
                rhs[s, :, lanes(c)] - rhs[0 if t is None else t, :, lanes(c)]
            )
    at.wait_faces(right)
    for s in range(subs):
        for c in range(2):
            residual[s, :, lanes(c)] = mask[s : s + 1, lanes(c)] * (
                rhs[s, :, lanes(c)] - beyond[c, :, s, :]
            )

    gats = [(k.gat[n], k.esend[n], k.erecv[n], k.msg[n]) for n in range(4)]

    def coarse(msg, vector, tiles, scaled, chosen):
        for s in chosen:
            v = vector[s]
            if scaled:
                v = jnp.concatenate([v, precond[s : s + 1] * v], axis=0)
            out = by_two(across_rows, v, (high[s, 0:32], low[s, 0:32]))
            for t in range(tiles):
                part = out[:, 8 * t : 8 * t + 8]
                if not scaled:
                    at_lane = 64 * (t % 2) + 8 * s
                    msg[t // 2, :, at_lane : at_lane + 8] = part
                    continue
                msg[t, :, 8 * s : 8 * s + 8] = part[:loads]
                if scaled:
                    msg[t, :, 64 + 8 * s : 72 + 8 * s] = part[loads:]

    lane = lax.broadcasted_iota(jnp.int32, (loads, 128), 1)
    gat, esend, erecv, msg = gats[0]
    coarse(msg, residual, 1, True, range(subs))
    start, wait_first = at.everywhere(msg, gat, esend, erecv)
    start()
    gat[me] = msg[...]
    for s in range(subs):
        load(s).start()

    inverse_far(at.far).wait_recv()
    inverse_relay(at.far).start()
    order = NSUB * 64
    full_order = NSUB * subs * modes
    row = lax.broadcasted_iota(jnp.int32, (order, full_order), 0)
    column = lax.broadcasted_iota(jnp.int32, (order, full_order), 1)
    widen = jnp.where((row % 8 < modes) & (row // 8 * modes + row % 8 == column), 1.0, 0.0)
    widen = widen.astype(BF16)
    row = lax.broadcasted_iota(jnp.int32, (order, 192), 0)
    column = lax.broadcasted_iota(jnp.int32, (order, 192), 1)
    s_of, j_of, n_of = row // 64, row // 8 % 8, row % 8
    source = jnp.where(j_of == 3, s_of ^ 4, jnp.where(j_of == 4, s_of ^ 1, s_of))
    source = jnp.where(j_of == 5, s_of ^ 3, source)
    wanted = jnp.where(j_of <= 2, 64 * j_of, 0) + 8 * source + n_of
    choose = jnp.where((j_of <= 5) & (wanted == column), 1.0, 0.0).astype(BF16)
    inverse_twin(at.twin).wait_recv()
    inverse_relay(at.diagonal).wait_recv()
    all_rows = inverse[...].reshape(full_order, full_order)
    present = at.has_second.astype(F32)
    there = jnp.where(at.has_second, at.second, 0)
    for part, whole, chosen in zip(
        halves(all_rows), (k.q_high, k.q_low), (k.near_high, k.near_low)
    ):
        tall = along(widen, part).astype(BF16)
        whole[...] = across_rows(tall, widen).astype(BF16)
        near = jnp.concatenate(
            [
                whole[pl.ds(pl.multiple_of(64 * me, 64), 64), :].astype(F32),
                whole[pl.ds(pl.multiple_of(64 * at.first, 64), 64), :].astype(F32),
                present * whole[pl.ds(pl.multiple_of(64 * there, 64), 64), :].astype(F32),
            ],
            axis=0,
        ).astype(BF16)
        chosen[...] = along(choose, near).astype(BF16)
    q_pair = (k.q_high, k.q_low)
    near_pair = (k.near_high, k.near_low)
    m_pair = (k.m_high, k.m_low)
    for ref in m_pair:
        ref[...] = jnp.zeros(ref.shape, BF16)
    inverse_far(q).wait_send()
    inverse_twin(q).wait_send()
    inverse_relay(at.far).wait_send()

    wait_middle()
    row = lax.broadcasted_iota(jnp.int32, (64, 384), 0)
    column = lax.broadcasted_iota(jnp.int32, (64, 384), 1)
    spread = jnp.where(row == column // 64 * 8 + column % 8, 1.0, 0.0).astype(BF16)
    row = lax.broadcasted_iota(jnp.int32, (64, 64), 0) // 8
    column = lax.broadcasted_iota(jnp.int32, (64, 64), 1) // 8
    same = (row == column).astype(F32)
    inner_masks = [(row ^ flip == column).astype(F32) for flip in (4, 1, 3)]
    compact = [middle_all[t, :, 64 * h : 64 * h + 64] for t in range(NSUB) for h in range(2)]
    for part, whole in zip(halves(jnp.concatenate(compact, axis=0)), m_pair):
        wide_part = along(part, spread)
        for t in range(NSUB):
            piece = wide_part[64 * t : 64 * t + 64]
            own = same * piece[:, 0:64]
            for j in range(3):
                own = own + inner_masks[j] * piece[:, 64 * (j + 3) : 64 * (j + 4)]
            first, second = near_of(t)
            whole[64 * t : 64 * t + 64, 64 * t : 64 * t + 64] = own.astype(BF16)
            whole[64 * t : 64 * t + 64, 64 * first : 64 * first + 64] = (
                same * piece[:, 64:128]
            ).astype(BF16)
            if second is not None:
                whole[64 * t : 64 * t + 64, 64 * second : 64 * second + 64] = (
                    same * piece[:, 128:192]
                ).astype(BF16)

    def pair_of(pair):
        return pair[0][...], pair[1][...]

    def joined(tiles, half):
        return jnp.concatenate([t[:, 64 * half : 64 * half + 64] for t in tiles], axis=1)

    def lift_of(coefficients, s):
        part = coefficients[:, 64 * s : 64 * s + 48]
        return by_two(along, part, (high[s], low[s]))

    packed = k.packed

    def pack(value, s):
        y, z = s // 4, s % 4
        packed[z, 2 * y] = value[:, lanes(0)]
        packed[z, 2 * y + 1] = value[:, lanes(1)]
        if y == 0:
            packed[z, 4] = value[:, lanes(2)]
        if z % 2 == 0:
            packed[z, 5 + y] = value[:, lanes(4)]
        if z == 1:
            packed[z, 5 + y] = value[:, lanes(5)]

    def direction(c_res, c_scaled, target, send, joint):
        y = c_res if joint else by_two(across_rows, c_res, pair_of(q_pair))
        c_scaled = c_scaled - by_two(across_rows, y, pair_of(m_pair))
        both = jnp.concatenate([c_res, c_scaled], axis=0)
        near = by_two(across_rows, both, pair_of(near_pair))
        total = jnp.zeros((loads, interface), F32)
        for p in range(subs // 2):
            for s in (p, p + subs // 2):
                lifted = lift_of(near, s)
                projected = residual[s] - lifted[:loads]
                scaled = precond[s : s + 1] * projected
                total = total + projected * scaled
                value = scaled - lifted[loads:]
                target[s] = value
                pack(value, s)
            send(p)
        return 0.5 * jnp.sum(total, axis=1, keepdims=True)

    wait_first()
    tiles = [gat[t, 0] for t in range(NSUB)]
    c_res, c_scaled = joined(tiles, 0), joined(tiles, 1)
    search, fresh = k.search, k.fresh
    product = k.product
    arrivals = [[k.arriving[n], k.fsend[n], k.frecv[n]] for n in range(2)]
    ops = [
        operate(
            at,
            packed,
            hold,
            k.res,
            product,
            [k.gath[n], k.gsend[n], k.grecv[n], k.asend[n], k.arecv[n]]
            + [k.cres, k.ctwin[n], k.csend[n], k.crecv[n]]
            + [k.lres, k.ltwin[n], k.lsend[n], k.lrecv[n]],
            *arrivals[n],
        )
        for n in range(ITERS)
    ]
    send, run, settle, drain, faces = ops[0]
    partial = direction(c_res, c_scaled, search, send, False)
    for s in range(subs):
        load(s).wait()
    image = k.image

    def mixed(target, s):
        y, z = s // 4, s % 4
        for c in range(2):
            target[s, :, lanes(c)] = mask[s : s + 1, lanes(c)] * product[y, z, :, lanes(c)]
        target[s, :, lanes(3)] = jnp.zeros((loads, slot), F32)
        for c in (2, 4, 5):
            t = inner_partner(c, s)
            if t is None:
                target[s, :, lanes(c)] = jnp.zeros((loads, slot), F32)
                continue
            owner = min(s, t)
            value = mask[s : s + 1, lanes(c)] * product[owner // 4, owner % 4, :, lanes(c)]
            target[s, :, lanes(c)] = value if s == owner else -value

    def finish_image(target, arriving):
        for s in range(subs):
            for c in range(2):
                target[s, :, lanes(c)] = (
                    target[s, :, lanes(c)]
                    - mask[s : s + 1, lanes(c)] * arriving[c, s // 4, s % 4]
                )

    def curve_of(direct, values, chosen, sums):
        for s in chosen:
            both = direct[s] * values[s]
            sums = (sums[0] + both[:, : 2 * slot], sums[1] + both[:, 2 * slot :])
        return sums

    def curve_end(sums):
        total = jnp.sum(sums[0], axis=1, keepdims=True)
        return total + 0.5 * jnp.sum(sums[1], axis=1, keepdims=True)

    groups = [[s for s in range(subs) if s % 4 // 2 == half] for half in range(2)]
    nothing = (jnp.zeros((loads, 2 * slot), F32), jnp.zeros((loads, 4 * slot), F32))

    def no_second():
        for n in range(2):
            k.arriving[n][1] = jnp.zeros(k.arriving[n].shape[1:], F32)

    pl.when(jnp.logical_not(at.has_second))(no_second)

    def gathered(gat, scaled):
        tiles = []
        for t in range(NSUB):
            first, second = near_of(t)
            if scaled:
                tile = gat[t, 0] + gat[first, 1]
                if second is not None:
                    tile = tile + gat[second, 2]
            else:
                tile = gat[t, 0][:, 0:64] + gat[first, 0][:, 64:128]
                if second is not None:
                    tile = tile + gat[second, 1][:, 0:64]
            tiles.append(tile)
        return tiles

    def summed(gat, at_lane):
        total = gat[0, 0]
        for t in range(1, NSUB):
            total = total + gat[t, 0]
        return [total[:, n : n + 1] for n in at_lane]

    run()
    for n in range(4):
        line = slice(128 * n, 128 * n + 128)
        top, rest = k.m_high[line], k.m_low[line]
        joint = along(top, k.q_high[...]) + along(rest, k.q_high[...]) + along(top, k.q_low[...])
        k.m_high[line], k.m_low[line] = halves(joint)
    gat, esend, erecv, msg = gats[1]
    sums = nothing
    for p in range(4):
        settle(p)
        if p >= 2:
            chosen = groups[p - 2]
            for s in chosen:
                mixed(image[0], s)
            coarse(msg, image[0], 3, True, chosen)
            sums = curve_of(search, image[0], chosen, sums)
    curve = curve_end(sums)
    msg[0] = jnp.where(lane == 6, curve, jnp.where(lane == 7, partial, msg[0]))
    start, wait = at.everywhere(msg, gat, esend, erecv)
    start()
    gat[me] = msg[...]
    drain()
    faces()
    finish_image(image[0], k.arriving[0])
    wait()
    tiles = gathered(gat, True)
    curve, energy = summed(gat, (6, 7))
    step_0 = energy / curve
    c_res = c_res - step_0 * joined(tiles, 0)
    c_scaled = c_scaled - step_0 * joined(tiles, 1)
    for s in range(subs):
        residual[s] = residual[s] - step_0 * image[0][s]
    send, run, settle, drain, faces = ops[1]
    partial = direction(c_res, c_scaled, fresh, send, True)

    gat_e, esend, erecv, msg = gats[2]
    msg[0] = jnp.broadcast_to(partial, (loads, 128))
    start, wait_energy = at.everywhere(msg, gat_e, esend, erecv)
    start()
    gat_e[me] = msg[...]
    run()
    wait_energy()
    fresh_energy = summed(gat_e, (0,))[0]
    ratio = fresh_energy / energy
    gat, esend, erecv, msg = gats[3]
    sums = nothing
    at_rest = slice(2 * slot, interface)
    for p in range(4):
        settle(p)
        if p < 2:
            continue
        chosen = groups[p - 2]
        for s in chosen:
            fresh[s] = fresh[s] + ratio * search[s]
            mixed(image[1], s)
            for c in range(2):
                before = image[0][s, :, lanes(c)] + (
                    mask[s : s + 1, lanes(c)] * k.arriving[0][c, s // 4, s % 4]
                )
                image[1][s, :, lanes(c)] = image[1][s, :, lanes(c)] + ratio * before
            image[1][s, :, at_rest] = image[1][s, :, at_rest] + ratio * image[0][s, :, at_rest]
        coarse(msg, image[1], 3, False, chosen)
        sums = curve_of(fresh, image[1], chosen, sums)
    curve = curve_end(sums)
    msg[0] = jnp.where(lane == 6, curve, msg[0])
    start, wait = at.everywhere(msg, gat, esend, erecv)
    start()
    gat[me] = msg[...]
    drain()
    faces()
    k.arriving[1][...] = k.arriving[1][...] + ratio * k.arriving[0][...]
    finish_image(image[1], k.arriving[1])
    wait()
    tiles = gathered(gat, False)
    step_1 = fresh_energy / summed(gat, (6,))[0]
    c_res = c_res - step_1 * jnp.concatenate(tiles, axis=1)
    near = by_two(across_rows, c_res, pair_of(near_pair))
    for s in range(subs):
        mult_out[:, s, :] = step_0 * search[s] + step_1 * fresh[s]
        proj_out[:, s, :] = residual[s] - step_1 * image[1][s] - lift_of(near, s)


def deliver_kernel(first_in, second_in, first_out, second_out, held, sems):
    parts, depth = 2, held.shape[1] // 2

    def copy(n, out):
        which, part = n // parts, n % parts
        rows = pl.ds(part * depth, depth)
        middle = held.at[which, rows]
        if out:
            target = (first_out, second_out)[which].at[rows]
            return pltpu.make_async_copy(middle, target, sems.at[1, n])
        source = (first_in, second_in)[which].at[rows]
        return pltpu.make_async_copy(source, middle, sems.at[0, n])

    for n in range(2 * parts):
        copy(n, False).start()
    for n in range(2 * parts):
        copy(n, False).wait()
        copy(n, True).start()
    for n in range(2 * parts):
        copy(n, True).wait()


def by_kernels(schur_block, rigid_modes, coarse_inverse, dual_rhs, stiff_diag, face_length):
    loads, subs, interface = dual_rhs.shape
    rows = schur_block.shape[1]
    slot = interface // 6
    modes = rigid_modes.shape[1]
    vmem = pl.BlockSpec(memory_space=pltpu.VMEM)
    hbm = pl.BlockSpec(memory_space=pltpu.HBM)
    dma = pltpu.SemaphoreType.DMA
    order = NSUB * 64
    vector = pltpu.VMEM((subs, loads, interface), F32)
    edge = pltpu.VMEM((2, modes + 1, subs, slot), F32)
    face = pltpu.VMEM((2, 2, subs // 2, loads, slot), F32)
    basis = pltpu.VMEM((subs, 48, interface), BF16)
    square = pltpu.VMEM((order, order), BF16)
    scratch = dict(
        hold=pltpu.VMEM((2, subs // 2, rows, interface), F32),
        load_sem=dma((subs,)),
        input_sem=dma((5,)),
        edges=edge,
        across=edge,
        beyond=pltpu.VMEM((2, loads, subs, slot), F32),
        rsend=dma((2,)),
        rrecv=dma((2,)),
        tsend=dma((2,)),
        trecv=dma((2,)),
        bsend=dma((2,)),
        brecv=dma((2,)),
        inverse=pltpu.VMEM((NCRS,) + coarse_inverse.shape, F32),
        isend=dma((3,)),
        irecv=dma((3,)),
        wide=pltpu.VMEM((subs, 8, interface), F32),
        rhs=vector,
        mask=pltpu.VMEM((subs, interface), F32),
        precond=pltpu.VMEM((subs, interface), F32),
        basis_high=basis,
        basis_low=basis,
        residual=vector,
        middle_msg=pltpu.VMEM((32, 128), F32),
        middle_all=pltpu.VMEM((NSUB, 32, 128), F32),
        msend=dma((NSUB,)),
        mrecv=dma((NSUB,)),
        q_high=square,
        q_low=square,
        near_high=square,
        near_low=square,
        m_high=square,
        m_low=square,
        packed=pltpu.VMEM((4, 7, loads, slot), F32),
        search=vector,
        fresh=vector,
        product=pltpu.VMEM((2, subs // 2, loads, interface), F32),
        image=[vector] * 2,
        res=pltpu.VMEM((2, subs // 2, NCRS, loads, rows), F32),
    )
    sources = [
        jnp.swapaxes(rigid_modes, 0, 1),
        coarse_inverse,
        dual_rhs,
        stiff_diag,
        face_length,
    ]
    tiles = (1, 3, 1, 2)
    third = pltpu.VMEM((2, subs // 2, loads, 3 * slot), F32)
    scratch.update(
        cres=pltpu.VMEM((2, subs // 2, 2, loads, 3 * slot), F32),
        input=[pltpu.VMEM(source.shape, source.dtype) for source in sources],
        msg=[pltpu.VMEM((n, loads, 128), F32) for n in tiles],
        gat=[pltpu.VMEM((NSUB, n, loads, 128), F32) for n in tiles],
        esend=[dma((NSUB,))] * 4,
        erecv=[dma((NSUB,))] * 4,
        gath=[pltpu.VMEM((4, NCRS, 7, loads, slot), F32)] * ITERS,
        gsend=[dma((3, 4))] * ITERS,
        grecv=[dma((3, 4))] * ITERS,
        asend=[dma((3, 4, 2))] * ITERS,
        arecv=[dma((NCRS, 4, 2))] * ITERS,
        ctwin=[third] * ITERS,
        csend=[dma((4,))] * ITERS,
        crecv=[dma((4,))] * ITERS,
        lres=pltpu.VMEM((2, 2, 2, loads, slot), F32),
        ltwin=[pltpu.VMEM((2, 2, loads, slot), F32)] * ITERS,
        lsend=[dma((2,))] * ITERS,
        lrecv=[dma((2,))] * ITERS,
        arriving=[face] * ITERS,
        fsend=[dma((2, 4))] * ITERS,
        frecv=[dma((2, 4))] * ITERS,
    )
    names = [(name, len(v) if isinstance(v, list) else 0) for name, v in scratch.items()]
    shapes = [one for v in scratch.values() for one in (v if isinstance(v, list) else [v])]
    out = jax.ShapeDtypeStruct((loads, subs, interface), F32)
    results = pl.pallas_call(
        functools.partial(main_kernel, names),
        out_shape=(out, out),
        in_specs=[hbm] * 6,
        out_specs=(vmem, vmem),
        scratch_shapes=shapes,
        compiler_params=pltpu.CompilerParams(
            collective_id=0, has_side_effects=True, vmem_limit_bytes=56 * 1024 * 1024
        ),
        name="main",
    )(schur_block, *sources)
    return pl.pallas_call(
        deliver_kernel,
        out_shape=(out, out),
        in_specs=[hbm] * 2,
        out_specs=(hbm, hbm),
        scratch_shapes=[pltpu.VMEM((2, loads, subs, interface), F32), dma((2, 4))],
        compiler_params=pltpu.CompilerParams(vmem_limit_bytes=56 * 1024 * 1024),
        name="deliver",
    )(*results)


def shards(schur_block, rigid_modes, coarse_inverse, dual_rhs, stiff_diag, face_length):
    fits = dual_rhs.shape[0] == 8 and lax.axis_size("crs") == NCRS and lax.axis_size("sub") == NSUB
    build = by_kernels if fits else by_collectives
    return build(schur_block, rigid_modes, coarse_inverse, dual_rhs, stiff_diag, face_length)


def solution(mesh):
    return jax.shard_map(
        shards,
        mesh=mesh,
        in_specs=(
            P("sub", "crs", None),
            P("sub", None, None),
            P("crs", None),
            P("crs", "sub", None),
            P("sub", None),
            P("sub", None),
        ),
        out_specs=(P("crs", "sub", None), P("crs", "sub", None)),
        check_vma=False,
    )
```

```python
import functools

import jax
import jax.numpy as jnp
import numpy as np
from jax import lax
from jax.experimental import pallas as pl
from jax.experimental.pallas import tpu as pltpu
from jax.sharding import PartitionSpec as P

ITERS = 2
SY = 2
SZ = 4
SUBS = 8

PRECISE = lax.Precision.HIGHEST
SPLIT = lax.Precision.HIGH


def local_lookup():
    indices = np.arange(SUBS)
    coords = [indices // SZ, indices % SZ]
    extent = [SY, SZ]
    stride = [SZ, 1]
    lookup = np.zeros((4, SUBS), np.int32)
    for colour in range(4):
        axis_pick = colour // 2
        anchor = coords[axis_pick]
        offset = np.where(anchor % 2 == colour % 2, 1, -1)
        target = anchor + offset
        inside = (target >= 0) & (target < extent[axis_pick])
        lookup[colour] = np.where(inside, indices + offset * stride[axis_pick], indices)
    return lookup


def by_collectives(schur_block, rigid_modes, coarse_inverse, dual_rhs, stiff_diag, face_length):
    loads, subs, interface = dual_rhs.shape
    slot = interface // 6
    modes = rigid_modes.shape[1]
    own = subs * modes
    nsub = lax.axis_size("sub")
    sub_index = lax.axis_index("sub")
    even = sub_index % 2 == 0
    lookup = local_lookup()
    positions = jnp.arange(interface) % slot
    usable = (jnp.repeat(face_length, slot, axis=1) > positions[None, :]).astype(jnp.float32)
    up = [(i, i + 1) for i in range(nsub - 1)]
    down = [(i + 1, i) for i in range(nsub - 1)]

    def partner(vector):
        first = vector[..., :slot]
        second = vector[..., slot : 2 * slot]
        from_left = lax.ppermute(jnp.where(even, first, second), "sub", up)
        from_right = lax.ppermute(jnp.where(even, second, first), "sub", down)
        pieces = [jnp.where(even, from_right, from_left), jnp.where(even, from_left, from_right)]
        for colour in range(2, 6):
            window = vector[..., colour * slot : (colour + 1) * slot]
            pieces.append(
                jnp.concatenate([window[..., t : t + 1, :] for t in lookup[colour - 2]], axis=-2)
            )
        return jnp.concatenate(pieces, axis=-1)

    modes_first = jnp.swapaxes(rigid_modes, 0, 1)
    together = jnp.concatenate([dual_rhs, modes_first, stiff_diag[None]], axis=0)
    across = partner(together)
    residual = usable * (dual_rhs - across[:loads])
    modes_across = across[loads : loads + modes]
    precond = usable * (stiff_diag + across[-1])

    inverse = lax.all_gather(coarse_inverse, "crs", axis=0, tiled=True)

    def by_slot(array):
        return array.reshape(array.shape[:-1] + (6, slot))

    basis = by_slot(usable * jnp.concatenate([modes_first, -modes_across], axis=0))

    weighted = by_slot(modes_first * precond)
    blocks = jnp.einsum("msck,nsck->scmn", weighted, basis, precision=PRECISE)
    total_subs = nsub * subs
    here = sub_index * subs + jnp.arange(subs)
    left = here - subs
    right = here + subs
    targets = [jnp.where(even, right, left), jnp.where(even, left, right)]
    for colour in range(2, 6):
        targets.append(sub_index * subs + jnp.asarray(lookup[colour - 2]))
    targets = jnp.stack(targets, axis=1)
    hot_across = (targets[:, :, None] == jnp.arange(total_subs)).astype(jnp.float32)
    hot_here = (here[:, None] == jnp.arange(total_subs)).astype(jnp.float32)
    dense = jnp.einsum("smn,st->smtn", blocks[..., :modes].sum(axis=1), hot_here, precision=PRECISE)
    dense = dense + jnp.einsum("scmn,sct->smtn", blocks[..., modes:], hot_across, precision=PRECISE)
    dense = dense.reshape(own, total_subs * modes)
    middle = lax.all_gather(dense, "sub", axis=0, tiled=True)

    def coarse(vector):
        return jnp.einsum("lsi,msi->lsm", vector, modes_first, precision=PRECISE).reshape(loads, own)

    def dots(a, b):
        return jnp.sum(a * b, axis=(1, 2))[:, None]

    def shared(parts):
        gathered = lax.all_gather(jnp.concatenate(parts, axis=1), "sub", axis=0)
        count = own * (sum(part.shape[1] == own for part in parts))
        outs = []
        for at in range(0, count, own):
            outs.append(jnp.swapaxes(gathered[:, :, at : at + own], 0, 1).reshape(loads, nsub * own))
        sums = jnp.sum(gathered[:, :, count:], axis=0)
        return outs, [sums[:, j : j + 1] for j in range(sums.shape[1])]

    def solve(values):
        return jnp.einsum("lb,ab->la", values, inverse, precision=PRECISE)

    def lifted(values):
        grid = values.reshape(loads, nsub, subs, modes)
        padded = jnp.pad(grid, ((0, 0), (1, 1), (0, 0), (0, 0)))
        near = lax.dynamic_slice_in_dim(padded, sub_index, 3, axis=1)
        before, mine, after = near[:, 0], near[:, 1], near[:, 2]
        pieces = [jnp.where(even, after, before), jnp.where(even, before, after)]
        for colour in range(2, 6):
            pieces.append(jnp.stack([mine[:, t] for t in lookup[colour - 2]], axis=1))
        other = jnp.stack(pieces, axis=2)
        mine = jnp.broadcast_to(mine[:, :, None], other.shape)
        factors = jnp.concatenate([mine, other], axis=-1)
        out = jnp.einsum("lscm,msck->lsck", factors, basis, precision=PRECISE)
        return out.reshape(loads, subs, interface)

    def direction(residual, c_res, c_scaled, power):
        y = solve(c_res)
        my = jnp.einsum("lb,ab->la", y, middle, precision=PRECISE)
        energy = 0.5 * power - 2.0 * jnp.sum(y * c_scaled, axis=1, keepdims=True)
        energy = energy + jnp.sum(y * my, axis=1, keepdims=True)
        t = solve(c_scaled - my)
        return precond * (residual - lifted(y)) - lifted(t), energy

    scaled = precond * residual
    (c_res, c_scaled), (power,) = shared([coarse(residual), coarse(scaled), dots(residual, scaled)])
    search, energy = direction(residual, c_res, c_scaled, power)
    multipliers = None
    for iteration in range(ITERS):
        by_rows = jnp.einsum(
            "sij,lsj->lsi",
            schur_block,
            lax.all_gather(search, "crs", axis=0, tiled=True),
            precision=SPLIT,
        )
        product = lax.all_to_all(by_rows, "crs", split_axis=0, concat_axis=2, tiled=True)
        image = usable * (product - partner(product))
        last = iteration + 1 == ITERS
        curve = dots(search, product)
        if last:
            (c_image,), (curve,) = shared([coarse(image), curve])
        else:
            scaled_image = precond * image
            parts = [
                coarse(image),
                coarse(scaled_image),
                curve,
                dots(residual, scaled_image),
                dots(image, scaled_image),
            ]
            (c_image, c_scaled_image), (curve, cross, square) = shared(parts)
        step = energy / curve
        moved = step[:, :, None] * search
        multipliers = moved if multipliers is None else multipliers + moved
        residual = residual - step[:, :, None] * image
        c_res = c_res - step * c_image
        if last:
            projected = residual - lifted(solve(c_res))
        else:
            c_scaled = c_scaled - step * c_scaled_image
            power = power - 2.0 * step * cross + step * step * square
            fresh, energy_new = direction(residual, c_res, c_scaled, power)
            search = fresh + (energy_new / energy)[:, :, None] * search
            energy = energy_new
    return (multipliers, projected)


MESH = pl.DeviceIdType.MESH
F32 = jnp.float32
BF16 = jnp.bfloat16
NSUB = 8
NCRS = 4


def across_rows(a, b):
    return lax.dot_general(a, b, (((1,), (1,)), ((), ())), preferred_element_type=F32)


def along(a, b):
    return jnp.dot(a, b, preferred_element_type=F32)


def halves(x):
    high = x.astype(BF16)
    return high, (x - high.astype(F32)).astype(BF16)


def stacked(x):
    high = x.astype(BF16).astype(F32)
    return jnp.concatenate([high, x - high], axis=0).astype(BF16)


def folded(x):
    rows = x.shape[0] // 2
    return x[:rows] + x[rows:]


def by_two(product, x, pair):
    both = stacked(x)
    return folded(product(both, pair[0]) + product(both, pair[1]))


def near_of(block):
    low = block - 1 if block % 2 == 0 else block + 1
    return block ^ 1, (low if 0 <= low < NSUB else None)


def remote(src, dst, send, recv, target):
    return pltpu.make_async_remote_copy(
        src_ref=src,
        dst_ref=dst,
        send_sem=send,
        recv_sem=recv,
        device_id=target,
        device_id_type=MESH,
    )


class Place:
    def __init__(self):
        self.me = me = lax.axis_index("sub")
        self.q = q = lax.axis_index("crs")
        core = q % 2
        self.twin = q + 1 - 2 * core
        self.far = (q + 2) % NCRS
        self.diagonal = (self.twin + 2) % NCRS
        odd = me % 2
        self.first = me + 1 - 2 * odd
        self.second = me - 1 + 2 * odd
        self.has_second = jnp.logical_and(self.second >= 0, self.second < NSUB)

    def faces(self, src, dst, send, recv):
        return (
            remote(src(0), dst.at[0], send.at[0], recv.at[0], (self.first, self.q)),
            remote(src(1), dst.at[1], send.at[1], recv.at[1], (self.second, self.q)),
        )

    def start_faces(self, copies):
        copies[0].start()

        @pl.when(self.has_second)
        def _():
            copies[1].start()

    def wait_faces(self, copies):
        copies[0].wait()

        @pl.when(self.has_second)
        def _():
            copies[1].wait()

    def everywhere(self, src, gat, send, recv):
        def copy(k, block):
            return remote(
                src, gat.at[block], send.at[k], recv.at[k], ((self.me + k) % NSUB, self.q)
            )

        def start():
            for k in (4, 3, 5, 2, 6, 1, 7):
                copy(k, self.me).start()

        def wait():
            for k in range(1, NSUB):
                copy(k, (self.me + NSUB - k) % NSUB).wait_recv()
            for k in range(1, NSUB):
                copy(k, self.me).wait_send()

        return start, wait


def chunk_size(p):
    return 5 if p == 3 else 7


def operate(at, packed, hold, res, product, buffers, arriving, fsend, frecv):
    gath, gsend, grecv, asend, arecv, cres, ctwin, csend, crecv = buffers[:9]
    lres, ltwin, lsend, lrecv = buffers[9:]
    me, q = at.me, at.q
    lower = q < 2
    upper = q >= 2
    rows = hold.shape[2]
    loads = packed.shape[2]

    def to_far(p, span, block):
        return remote(
            packed.at[p, pl.ds(*span)],
            gath.at[p, block, pl.ds(*span)],
            gsend.at[1, p],
            grecv.at[1, p],
            (me, at.far),
        )

    def to_twin(p, n, block):
        return remote(
            packed.at[p, pl.ds(0, n)],
            gath.at[p, block, pl.ds(0, n)],
            gsend.at[0, p],
            grecv.at[0, p],
            (me, at.twin),
        )

    def relay(p, span, source, block):
        return remote(
            gath.at[p, source, pl.ds(*span)],
            gath.at[p, block, pl.ds(*span)],
            gsend.at[2, p],
            grecv.at[2, p],
            (me, at.twin),
        )

    wanted = {0: (5, 2), 1: (0, 7), 2: (0, 7)}

    def by_side(p, low, up, action):
        for side, span in ((lower, low), (upper, up)):
            if span is not None:
                pl.when(side)(functools.partial(action, span))

    def sending(p, action):
        by_side(p, wanted.get(p), (0, 5), action)

    def receiving(p, action):
        pl.when(lower)(functools.partial(action, (0, 5)))
        pl.when(jnp.logical_and(upper, p == 0))(functools.partial(action, (5, 2)))
        pl.when(jnp.logical_and(upper, fifth(p)))(functools.partial(action, (0, 7)))

    def send(p):
        n = chunk_size(p)
        sending(p, lambda span: to_far(p, span, q).start())
        to_twin(p, n, q).start()
        gath[p, q, 0:n] = packed[p, 0:n]

    def sized(small, action):
        pl.when(jnp.logical_not(small))(functools.partial(action, 7))
        pl.when(small)(functools.partial(action, 5))

    def forward(p, span):
        to_far(p, span, at.far).wait_recv()
        relay(p, span, at.far, at.far).start()

    peers = (at.twin, at.far, at.diagonal)

    def pieces(owner, p):
        if owner == 0:
            return [(lambda b: res.at[:, p, b], product.at[:, p, :, 0:384], 0, None)]
        if owner == 1:
            return [
                (lambda b: res.at[0, p, b], product.at[0, p, :, 384:768], 0, None),
                (lambda b: res.at[1, p, b, :, 0:128], product.at[1, p, :, 384:512], 1, None),
            ]
        odd = p % 2 == 1
        if owner == 2:
            source = lambda b: res.at[:, p - 1, b, :, 256:384]
            return [(source, product.at[:, p - 1, :, 1024:1152], 0, odd)]
        source = lambda b: res.at[:, p - 1, b, :, 0:128]
        inner = lambda b: res.at[:, 1, b, :, 128:384]
        return [
            (source, product.at[:, p - 1, :, 1152:1280], 0, odd),
            (inner, product.at[:, 1, :, 1280:1536], 1, p == 2),
        ]

    def give(piece, p, j):
        source, target, i, _ = piece
        return remote(
            source(peers[j]), target, asend.at[j, p, i], arecv.at[q, p, i], (me, peers[j])
        )

    def guarded(condition, action):
        if condition is None or condition is True:
            action()
        elif condition is not False:
            pl.when(condition)(action)

    def send_back(p):
        for owner in range(NCRS):

            @pl.when(q == owner)
            def _():
                for n, piece in enumerate(pieces(owner, p)):

                    def action():
                        if owner == 1 and n == 0:
                            res[0, p, :, :, 128:384] = (
                                res[0, p, :, :, 128:384] - res[1, p, :, :, 128:384]
                            )
                        if owner == 2:
                            res[:, p - 1, :, :, 256:384] = (
                                res[:, p - 1, :, :, 256:384] - res[:, p, :, :, 256:384]
                            )
                        if owner == 3 and n == 0:
                            res[:, p - 1, :, :, 0:128] = (
                                res[:, p - 1, :, :, 0:128] - res[:, p, :, :, 0:128]
                            )
                        if owner == 3 and n == 1:
                            res[:, 1, :, :, 128:384] = (
                                res[:, 1, :, :, 128:384] - res[:, 2, :, :, 128:384]
                            )
                        for j in range(3):
                            give(piece, p, j).start()
                        source, target, _, _ = piece
                        target[...] = source(owner)[...]

                    guarded(piece[3], action)

    def tripled(product_of, x, w):
        high_w, low_w = halves(w)
        return folded(product_of(x, high_w)) + product_of(x[: x.shape[0] // 2], low_w)

    def block(chunk, j, first, last):
        return gath[chunk, first:last, j].reshape((last - first) * loads, 256)

    def signs(p):
        sign = (1 - 2 * (p % 2)).astype(F32)
        last = jnp.where(p == 1, 1, jnp.where(p == 2, -1, 0)).astype(F32)
        return sign, p - p % 2, last, jnp.where(p == 0, 0, 1)

    def outer_slots(p, y, first=0, last=NCRS):
        middle = block(p, 4, first, last)
        return [
            block(p, 2 * y, first, last),
            block(p, 2 * y + 1, first, last),
            middle if y == 0 else -middle,
        ]

    def all_outer(p, y, first=0, last=NCRS):
        return stacked(jnp.concatenate(outer_slots(p, y, first, last), axis=1))

    def fifth(p):
        return jnp.logical_or(p == 1, p == 2)

    def share(p):
        return remote(
            cres.at[:, p, at.twin % 2], ctwin.at[:, p], csend.at[p], crecv.at[p], (me, at.twin)
        )

    def low_share(half):
        return remote(
            lres.at[half, :, at.twin % 2],
            ltwin.at[half],
            lsend.at[half],
            lrecv.at[half],
            (me, at.twin),
        )

    def prepare(p, carry):
        sized(p == 3, lambda n: to_twin(p, n, at.twin).wait_recv())
        sign, even, last, held = signs(p)

        @pl.when(lower)
        def _():
            for y in range(2):
                x = stacked(sign * block(even, 5 + y, 0, 2))
                out = tripled(across_rows, x, hold[y, p, :, 1024:1280])
                res[y, p, 0:2] = out.reshape(2, loads, rows)

            @pl.when(fifth(p))
            def _():
                for y in range(2):
                    x = stacked(last * block(held, 5 + y, 0, 2))
                    out = tripled(across_rows, x, hold[y, p, :, 1280:1536])
                    res[y, p, 0:2] = res[y, p, 0:2] + out.reshape(2, loads, rows)

            @pl.when(jnp.logical_not(fifth(p)))
            def _():
                half = p // 3
                for y in range(2):
                    zeroth, first, second = outer_slots(p, y, 0, 2)
                    x = jnp.where(
                        q == 0,
                        jnp.concatenate([zeroth, first[:, 0:128]], axis=1),
                        jnp.concatenate([first[:, 128:256], second], axis=1),
                    )
                    out = tripled(along, stacked(sign * x), hold[y, p, :, 1024:1280])
                    lres[half, y] = out.reshape(2, loads, 256)
                low_share(half).start()

        @pl.when(upper)
        def _():
            def part(x, y, first, end):
                return tripled(along, stacked(x), hold[y, p, first:end, 0:768])

            @pl.when(q == 2)
            def _():
                for y in range(2):
                    x = sign * block(even, 5 + y, 2, 4)
                    out = part(x[:, 0:128], y, 256, 384)
                    cres[y, p] = out.reshape(2, loads, 768)

            @pl.when(q == 3)
            def _():
                for y in range(2):
                    x = sign * block(even, 5 + y, 2, 4)
                    out = part(x[:, 128:256], y, 0, 128)
                    cres[y, p] = out.reshape(2, loads, 768)

                @pl.when(fifth(p))
                def _():
                    for y in range(2):
                        out = part(last * block(held, 5 + y, 2, 4), y, 128, 384)
                        cres[y, p] = cres[y, p] + out.reshape(2, loads, 768)

            cres[0, p, :, :, 512:768] = cres[0, p, :, :, 512:768] - cres[1, p, :, :, 512:768]
            share(p).start()

        return carry

    def multiply(p, carry):
        @pl.when(p < 3)
        def _():
            receiving(p + 1, lambda span: forward(p + 1, span))

        receiving(p, lambda span: relay(p, span, at.far, at.diagonal).wait_recv())
        sign, even, last, held = signs(p)

        @pl.when(lower)
        def _():
            for y in range(2):
                out = tripled(across_rows, all_outer(p, y), hold[y, p, :, 0:768])
                out = out.reshape(NCRS, loads, rows)
                res[y, p, 0:2] = res[y, p, 0:2] + out[0:2]
                res[y, p, 2:4] = out[2:4]

        def upper_rows(first, end, with_fifth):
            for y in range(2):
                inner = sign * block(even, 5 + y, 0, NCRS)
                size = 256
                if with_fifth:
                    inner = jnp.concatenate([inner, last * block(held, 5 + y, 0, NCRS)], axis=1)
                    size = 512
                inner = tripled(
                    across_rows, stacked(inner), hold[y, p, first:end, 1024 : 1024 + size]
                ).reshape(NCRS, loads, end - first)
                start = 0 if with_fifth else 2
                outer = tripled(
                    across_rows, all_outer(p, y, start, NCRS), hold[y, p, first:end, 0:768]
                ).reshape(NCRS - start, loads, end - first)
                res[y, p, start:NCRS, :, first:end] = inner[start:] + outer
                if start:
                    res[y, p, 0:start, :, first:end] = inner[:start]

        for owner, begin, middle, end in ((2, 256, 384, 384), (3, 0, 384, 128)):

            @pl.when(q == owner)
            def _():
                pl.when(fifth(p))(functools.partial(upper_rows, begin, middle, True))
                pl.when(jnp.logical_not(fifth(p)))(
                    functools.partial(upper_rows, begin, end, False)
                )

        send_back(p)
        return carry

    def run():
        lax.fori_loop(0, 4, prepare, 0)
        receiving(0, lambda span: forward(0, span))
        lax.fori_loop(0, 4, multiply, 0)

    def face(c, p):
        return remote(
            product.at[:, p, :, pl.ds(256 * c, 256)],
            arriving.at[c, :, p],
            fsend.at[c, p],
            frecv.at[c, p],
            (at.second if c else at.first, q),
        )

    def returned(owner, p):
        for piece in pieces(owner, p):
            if piece[3] is None or piece[3]:
                _, target, i, _ = piece
                remote(
                    target, target, asend.at[0, p, i], arecv.at[owner, p, i], (me, at.twin)
                ).wait_recv()

    def settle(p):
        for owner in range(2):
            pl.when(q != owner)(functools.partial(returned, owner, p))

        @pl.when(upper)
        def _():
            share(p).wait_recv()
            mine = q % 2
            for y in range(2):
                span = slice(0, 768 if y == 0 else 512)
                product[y, p, :, span] = product[y, p, :, span] + (
                    cres[y, p, mine, :, span] + ctwin[y, p, :, span]
                )

        face(0, p).start()
        pl.when(at.has_second)(face(1, p).start)
        for owner in (2, 3):
            if any(piece[3] for piece in pieces(owner, p)):
                pl.when(q != owner)(functools.partial(returned, owner, p))
        if p % 2 == 1:

            @pl.when(lower)
            def _():
                half = p // 3
                low_share(half).wait_recv()
                for y in range(2):
                    product[y, p - 1, :, 1024:1280] = product[y, p - 1, :, 1024:1280] + (
                        lres[half, y, q % 2] + ltwin[half, y]
                    )

    def faces():
        for p in range(4):
            face(0, p).wait()
            pl.when(at.has_second)(face(1, p).wait)

    def drain():
        for p in range(4):
            n = chunk_size(p)
            sending(p, lambda span: to_far(p, span, q).wait_send())
            to_twin(p, n, q).wait_send()
            by_side(
                p,
                (0, 5),
                wanted.get(p),
                lambda span: relay(p, span, at.far, at.far).wait_send(),
            )
            pl.when(upper)(lambda: share(p).wait_send())
            if p in (0, 3):
                pl.when(lower)(lambda: low_share(p // 3).wait_send())
        for owner in range(NCRS):

            @pl.when(q == owner)
            def _():
                for p in range(4):
                    for piece in pieces(owner, p):
                        if piece[3] is None or piece[3]:
                            for j in range(3):
                                give(piece, p, j).wait_send()

    return send, run, settle, drain, faces


class Held:
    def __init__(self, names, refs):
        refs = iter(refs)
        for name, count in names:
            setattr(self, name, [next(refs) for _ in range(count)] if count else next(refs))


def inner_partner(c, s):
    if c == 2:
        return s ^ 4
    if c == 4:
        return s ^ 1
    return s ^ 3 if s % 4 in (1, 2) else None


def main_kernel(names, schur, *refs):
    sources, (mult_out, proj_out) = refs[:5], refs[5:7]
    k = Held(names, refs[7:])
    inputs = k.input
    modes_in, inverse_in, rhs_in, stiff_in, length_in = inputs
    fetches = [
        pltpu.make_async_copy(source, held, k.input_sem.at[n])
        for n, (source, held) in enumerate(zip(sources, inputs))
    ]
    for copy in fetches:
        copy.start()
    loads, subs, interface = rhs_in.shape
    slot = interface // 6
    modes = modes_in.shape[0]
    at = Place()
    me, q = at.me, at.q
    hold, load_sem = k.hold, k.load_sem

    def lanes(c):
        return slice(c * slot, (c + 1) * slot)

    def load(s):
        return pltpu.make_async_copy(
            schur.at[s], hold.at[s // 4, s % 4], load_sem.at[s]
        )

    barrier = pltpu.get_barrier_semaphore()
    for j in range(1, NSUB):
        pl.semaphore_signal(
            barrier, inc=1, device_id=((me + j) % NSUB, q), device_id_type=MESH
        )
    for j in range(1, NCRS):
        pl.semaphore_signal(barrier, inc=1, device_id=(me, (q + j) % NCRS), device_id_type=MESH)

    for copy in fetches:
        copy.wait()
    edges, across = k.edges, k.across
    for c in range(2):
        edges[c, 0:modes] = modes_in[:, :, lanes(c)]
        edges[c, modes] = stiff_in[:, lanes(c)]
    pl.semaphore_wait(barrier, NSUB + NCRS - 2)

    core = q % 2

    def begin(c):
        target = (at.second if c else at.first, q)
        return remote(edges.at[c], across.at[c], k.bsend.at[c], k.brecv.at[c], target)

    def share(c):
        return remote(
            across.at[c], across.at[c], k.tsend.at[c], k.trecv.at[c], (me, at.twin)
        )

    pl.when(core == 0)(lambda: begin(0).start())
    pl.when((core == 1) & at.has_second)(lambda: begin(1).start())
    beyond = k.beyond
    right = at.faces(lambda c: rhs_in.at[:, :, lanes(c)], beyond, k.rsend, k.rrecv)
    at.start_faces(right)
    inverse, isend, irecv = k.inverse, k.isend, k.irecv

    def inverse_far(block):
        return remote(inverse_in, inverse.at[block], isend.at[1], irecv.at[1], (me, at.far))

    def inverse_twin(block):
        return remote(inverse_in, inverse.at[block], isend.at[0], irecv.at[0], (me, at.twin))

    def inverse_relay(block):
        return remote(
            inverse.at[at.far], inverse.at[block], isend.at[2], irecv.at[2], (me, at.twin)
        )

    inverse_far(q).start()
    inverse_twin(q).start()
    inverse[q] = inverse_in[...]

    @pl.when(jnp.logical_not(at.has_second))
    def _():
        across[1] = jnp.zeros(across.shape[1:], F32)
        beyond[1] = jnp.zeros(beyond.shape[1:], F32)

    wide, rhs, mask, precond = k.wide, k.rhs, k.mask, k.precond
    position = lax.broadcasted_iota(jnp.int32, (subs, slot), 1)
    for c in range(6):
        mask[:, lanes(c)] = (length_in[:, c : c + 1] > position).astype(F32)
    blank = jnp.zeros((8 - modes, interface), F32)
    for s in range(subs):
        rhs[s] = rhs_in[:, s, :]
        wide[s] = jnp.concatenate([modes_in[:, s, :], blank], axis=0)
    precond[:, lanes(3)] = jnp.zeros((subs, slot), F32)
    for c in (2, 4, 5):
        other = jnp.concatenate(
            [
                stiff_in[t : t + 1, lanes(c)]
                for t in [inner_partner(c, s) or 0 for s in range(subs)]
            ],
            axis=0,
        )
        precond[:, lanes(c)] = mask[:, lanes(c)] * (stiff_in[:, lanes(c)] + other)

    high, low = k.basis_high, k.basis_low

    def put(s, rows, window, value):
        a, b = halves(value)
        high[s, rows, window] = a
        low[s, rows, window] = b

    zero = jnp.zeros((8, slot), F32)
    for s in range(subs):
        inner = {}
        for c in (2, 4, 5):
            t = inner_partner(c, s)
            inner[c] = zero if t is None else -mask[s : s + 1, lanes(c)] * wide[t, :, lanes(c)]
        for c in range(6):
            upper = inner[2] if c == 2 else zero
            if c >= 2:
                put(s, slice(16, 32), lanes(c), jnp.concatenate([zero, upper], axis=0))
                own = mask[s : s + 1, lanes(c)] * wide[s, :, lanes(c)]
                put(s, slice(0, 16), lanes(c), jnp.concatenate([own, zero], axis=0))
            last = jnp.concatenate(
                [inner[4] if c == 4 else zero, inner[5] if c == 5 else zero], axis=0
            )
            put(s, slice(32, 48), lanes(c), last)


    @pl.when(core == 0)
    def _():
        begin(0).wait()
        share(0).start()
        pl.when(at.has_second)(lambda: share(1).wait_recv())
        share(0).wait_send()

    @pl.when(core == 1)
    def _():
        @pl.when(at.has_second)
        def _():
            begin(1).wait()
            share(1).start()

        share(0).wait_recv()
        pl.when(at.has_second)(lambda: share(1).wait_send())

    for c in range(2):
        precond[:, lanes(c)] = mask[:, lanes(c)] * (stiff_in[:, lanes(c)] + across[c, modes])
    small = jnp.zeros((8 - modes, slot), F32)
    for s in range(subs):
        for c in range(2):
            line = mask[s : s + 1, lanes(c)]
            own = line * wide[s, :, lanes(c)]
            outer = -line * jnp.concatenate([across[c, 0:modes, s, :], small], axis=0)
            put(
                s,
                slice(0, 16),
                lanes(c),
                jnp.concatenate([own, outer if c == 0 else zero], axis=0),
            )
            put(
                s,
                slice(16, 32),
                lanes(c),
                jnp.concatenate([outer if c == 1 else zero, zero], axis=0),
            )

    middle_msg, middle_all = k.middle_msg, k.middle_all
    middle_msg[...] = jnp.zeros(middle_msg.shape, F32)
    for s in range(subs):
        weighted = wide[s] * precond[s : s + 1]
        block = by_two(across_rows, weighted, (high[s], low[s]))
        line, first = 8 * (s % 4), 64 * (s // 4)
        middle_msg[line : line + 8, first : first + 48] = block
    start_middle, wait_middle = at.everywhere(
        middle_msg, middle_all, k.msend, k.mrecv
    )
    start_middle()
    middle_all[me] = middle_msg[...]

    residual = k.residual
    for s in range(subs):
        residual[s, :, lanes(3)] = jnp.zeros((loads, slot), F32)
        for c in (2, 4, 5):
            t = inner_partner(c, s)
            residual[s, :, lanes(c)] = mask[s : s + 1, lanes(c)] * (
                rhs[s, :, lanes(c)] - rhs[0 if t is None else t, :, lanes(c)]
            )
    at.wait_faces(right)
    for s in range(subs):
        for c in range(2):
            residual[s, :, lanes(c)] = mask[s : s + 1, lanes(c)] * (
                rhs[s, :, lanes(c)] - beyond[c, :, s, :]
            )

    gats = [(k.gat[n], k.esend[n], k.erecv[n], k.msg[n]) for n in range(4)]

    def coarse(msg, vector, tiles, scaled, chosen):
        for s in chosen:
            v = vector[s]
            if scaled:
                v = jnp.concatenate([v, precond[s : s + 1] * v], axis=0)
            used = 16 if tiles == 1 else 32
            out = by_two(across_rows, v, (high[s, 0:used], low[s, 0:used]))
            for t in range(tiles):
                part = out[:, 8 * t : 8 * t + 8]
                if not scaled:
                    at_lane = 64 * (t % 2) + 8 * s
                    msg[t // 2, :, at_lane : at_lane + 8] = part
                    continue
                msg[t, :, 8 * s : 8 * s + 8] = part[:loads]
                if scaled:
                    msg[t, :, 64 + 8 * s : 72 + 8 * s] = part[loads:]

    lane = lax.broadcasted_iota(jnp.int32, (loads, 128), 1)
    gat, esend, erecv, msg = gats[0]
    coarse(msg, residual, 1, True, range(subs))
    start, wait_first = at.everywhere(msg, gat, esend, erecv)
    start()
    gat[me] = msg[...]
    for s in range(subs):
        load(s).start()

    inverse_far(at.far).wait_recv()
    inverse_relay(at.far).start()
    order = NSUB * 64
    full_order = NSUB * subs * modes
    row = lax.broadcasted_iota(jnp.int32, (order, full_order), 0)
    column = lax.broadcasted_iota(jnp.int32, (order, full_order), 1)
    widen = jnp.where((row % 8 < modes) & (row // 8 * modes + row % 8 == column), 1.0, 0.0)
    widen = widen.astype(BF16)
    row = lax.broadcasted_iota(jnp.int32, (order, 192), 0)
    column = lax.broadcasted_iota(jnp.int32, (order, 192), 1)
    s_of, j_of, n_of = row // 64, row // 8 % 8, row % 8
    source = jnp.where(j_of == 3, s_of ^ 4, jnp.where(j_of == 4, s_of ^ 1, s_of))
    source = jnp.where(j_of == 5, s_of ^ 3, source)
    wanted = jnp.where(j_of <= 2, 64 * j_of, 0) + 8 * source + n_of
    choose = jnp.where((j_of <= 5) & (wanted == column), 1.0, 0.0).astype(BF16)
    inverse_twin(at.twin).wait_recv()
    inverse_relay(at.diagonal).wait_recv()
    all_rows = inverse[...].reshape(full_order, full_order)
    present = at.has_second.astype(F32)
    there = jnp.where(at.has_second, at.second, 0)
    for part, whole, chosen in zip(
        halves(all_rows), (k.q_high, k.q_low), (k.near_high, k.near_low)
    ):
        tall = along(widen, part).astype(BF16)
        whole[...] = across_rows(tall, widen).astype(BF16)
        near = jnp.concatenate(
            [
                whole[pl.ds(pl.multiple_of(64 * me, 64), 64), :].astype(F32),
                whole[pl.ds(pl.multiple_of(64 * at.first, 64), 64), :].astype(F32),
                present * whole[pl.ds(pl.multiple_of(64 * there, 64), 64), :].astype(F32),
            ],
            axis=0,
        ).astype(BF16)
        chosen[...] = along(choose, near).astype(BF16)
    q_pair = (k.q_high, k.q_low)
    near_pair = (k.near_high, k.near_low)
    m_pair = (k.m_high, k.m_low)
    for ref in m_pair:
        ref[...] = jnp.zeros(ref.shape, BF16)
    inverse_far(q).wait_send()
    inverse_twin(q).wait_send()
    inverse_relay(at.far).wait_send()

    wait_middle()
    row = lax.broadcasted_iota(jnp.int32, (64, 384), 0)
    column = lax.broadcasted_iota(jnp.int32, (64, 384), 1)
    spread = jnp.where(row == column // 64 * 8 + column % 8, 1.0, 0.0).astype(BF16)
    row = lax.broadcasted_iota(jnp.int32, (64, 64), 0) // 8
    column = lax.broadcasted_iota(jnp.int32, (64, 64), 1) // 8
    same = (row == column).astype(F32)
    inner_masks = [(row ^ flip == column).astype(F32) for flip in (4, 1, 3)]
    compact = [middle_all[t, :, 64 * h : 64 * h + 64] for t in range(NSUB) for h in range(2)]
    for part, whole in zip(halves(jnp.concatenate(compact, axis=0)), m_pair):
        wide_part = along(part, spread)
        for t in range(NSUB):
            piece = wide_part[64 * t : 64 * t + 64]
            own = same * piece[:, 0:64]
            for j in range(3):
                own = own + inner_masks[j] * piece[:, 64 * (j + 3) : 64 * (j + 4)]
            first, second = near_of(t)
            whole[64 * t : 64 * t + 64, 64 * t : 64 * t + 64] = own.astype(BF16)
            whole[64 * t : 64 * t + 64, 64 * first : 64 * first + 64] = (
                same * piece[:, 64:128]
            ).astype(BF16)
            if second is not None:
                whole[64 * t : 64 * t + 64, 64 * second : 64 * second + 64] = (
                    same * piece[:, 128:192]
                ).astype(BF16)

    def pair_of(pair):
        return pair[0][...], pair[1][...]

    def joined(tiles, half):
        return jnp.concatenate([t[:, 64 * half : 64 * half + 64] for t in tiles], axis=1)

    def lift_of(coefficients, s):
        part = coefficients[:, 64 * s : 64 * s + 48]
        return by_two(along, part, (high[s], low[s]))

    packed = k.packed

    def pack(value, s):
        y, z = s // 4, s % 4
        packed[z, 2 * y] = value[:, lanes(0)]
        packed[z, 2 * y + 1] = value[:, lanes(1)]
        if y == 0:
            packed[z, 4] = value[:, lanes(2)]
        if z % 2 == 0:
            packed[z, 5 + y] = value[:, lanes(4)]
        if z == 1:
            packed[z, 5 + y] = value[:, lanes(5)]

    def direction(c_res, c_scaled, target, send, joint):
        y = c_res if joint else by_two(across_rows, c_res, pair_of(q_pair))
        c_scaled = c_scaled - by_two(across_rows, y, pair_of(m_pair))
        both = jnp.concatenate([c_res, c_scaled], axis=0)
        near = by_two(across_rows, both, pair_of(near_pair))
        total = jnp.zeros((loads, interface), F32)
        for p in range(subs // 2):
            for s in (p, p + subs // 2):
                lifted = lift_of(near, s)
                projected = residual[s] - lifted[:loads]
                scaled = precond[s : s + 1] * projected
                total = total + projected * scaled
                value = scaled - lifted[loads:]
                target[s] = value
                pack(value, s)
            send(p)
        return 0.5 * jnp.sum(total, axis=1, keepdims=True)

    wait_first()
    tiles = [gat[t, 0] for t in range(NSUB)]
    c_res, c_scaled = joined(tiles, 0), joined(tiles, 1)
    search, fresh = k.search, k.fresh
    product = k.product
    arrivals = [[k.arriving[n], k.fsend[n], k.frecv[n]] for n in range(2)]
    ops = [
        operate(
            at,
            packed,
            hold,
            k.res,
            product,
            [k.gath[n], k.gsend[n], k.grecv[n], k.asend[n], k.arecv[n]]
            + [k.cres, k.ctwin[n], k.csend[n], k.crecv[n]]
            + [k.lres, k.ltwin[n], k.lsend[n], k.lrecv[n]],
            *arrivals[n],
        )
        for n in range(ITERS)
    ]
    send, run, settle, drain, faces = ops[0]
    partial = direction(c_res, c_scaled, search, send, False)
    for s in range(subs):
        load(s).wait()
    image = k.image

    def mixed(target, s):
        y, z = s // 4, s % 4
        for c in range(2):
            target[s, :, lanes(c)] = mask[s : s + 1, lanes(c)] * product[y, z, :, lanes(c)]
        target[s, :, lanes(3)] = jnp.zeros((loads, slot), F32)
        for c in (2, 4, 5):
            t = inner_partner(c, s)
            if t is None:
                target[s, :, lanes(c)] = jnp.zeros((loads, slot), F32)
                continue
            owner = min(s, t)
            value = mask[s : s + 1, lanes(c)] * product[owner // 4, owner % 4, :, lanes(c)]
            target[s, :, lanes(c)] = value if s == owner else -value

    def finish_image(target, arriving):
        for s in range(subs):
            for c in range(2):
                target[s, :, lanes(c)] = (
                    target[s, :, lanes(c)]
                    - mask[s : s + 1, lanes(c)] * arriving[c, s // 4, s % 4]
                )

    def curve_of(direct, values, chosen, sums):
        for s in chosen:
            both = direct[s] * values[s]
            sums = (sums[0] + both[:, : 2 * slot], sums[1] + both[:, 2 * slot :])
        return sums

    def curve_end(sums):
        total = jnp.sum(sums[0], axis=1, keepdims=True)
        return total + 0.5 * jnp.sum(sums[1], axis=1, keepdims=True)

    groups = [[s for s in range(subs) if s % 4 // 2 == half] for half in range(2)]
    nothing = (jnp.zeros((loads, 2 * slot), F32), jnp.zeros((loads, 4 * slot), F32))

    def no_second():
        for n in range(2):
            k.arriving[n][1] = jnp.zeros(k.arriving[n].shape[1:], F32)

    pl.when(jnp.logical_not(at.has_second))(no_second)

    def gathered(gat, scaled):
        tiles = []
        for t in range(NSUB):
            first, second = near_of(t)
            if scaled:
                tile = gat[t, 0] + gat[first, 1]
                if second is not None:
                    tile = tile + gat[second, 2]
            else:
                tile = gat[t, 0][:, 0:64] + gat[first, 0][:, 64:128]
                if second is not None:
                    tile = tile + gat[second, 1][:, 0:64]
            tiles.append(tile)
        return tiles

    def summed(gat, at_lane):
        total = gat[0, 0]
        for t in range(1, NSUB):
            total = total + gat[t, 0]
        return [total[:, n : n + 1] for n in at_lane]

    run()
    for n in range(4):
        line = slice(128 * n, 128 * n + 128)
        top, rest = k.m_high[line], k.m_low[line]
        joint = along(top, k.q_high[...]) + along(rest, k.q_high[...]) + along(top, k.q_low[...])
        k.m_high[line], k.m_low[line] = halves(joint)
    gat, esend, erecv, msg = gats[1]
    sums = nothing
    for p in range(4):
        settle(p)
        if p >= 2:
            chosen = groups[p - 2]
            for s in chosen:
                mixed(image[0], s)
            coarse(msg, image[0], 3, True, chosen)
            sums = curve_of(search, image[0], chosen, sums)
    curve = curve_end(sums)
    msg[0] = jnp.where(lane == 6, curve, jnp.where(lane == 7, partial, msg[0]))
    start, wait = at.everywhere(msg, gat, esend, erecv)
    start()
    gat[me] = msg[...]
    drain()
    faces()
    finish_image(image[0], k.arriving[0])
    wait()
    tiles = gathered(gat, True)
    curve, energy = summed(gat, (6, 7))
    step_0 = energy / curve
    c_res = c_res - step_0 * joined(tiles, 0)
    c_scaled = c_scaled - step_0 * joined(tiles, 1)
    for s in range(subs):
        residual[s] = residual[s] - step_0 * image[0][s]
    send, run, settle, drain, faces = ops[1]
    partial = direction(c_res, c_scaled, fresh, send, True)

    gat_e, esend, erecv, msg = gats[2]
    msg[0] = jnp.broadcast_to(partial, (loads, 128))
    start, wait_energy = at.everywhere(msg, gat_e, esend, erecv)
    start()
    gat_e[me] = msg[...]
    run()
    wait_energy()
    fresh_energy = summed(gat_e, (0,))[0]
    ratio = fresh_energy / energy
    gat, esend, erecv, msg = gats[3]
    sums = nothing
    at_rest = slice(2 * slot, interface)
    for p in range(4):
        settle(p)
        if p < 2:
            continue
        chosen = groups[p - 2]
        for s in chosen:
            fresh[s] = fresh[s] + ratio * search[s]
            mixed(image[1], s)
            for c in range(2):
                before = image[0][s, :, lanes(c)] + (
                    mask[s : s + 1, lanes(c)] * k.arriving[0][c, s // 4, s % 4]
                )
                image[1][s, :, lanes(c)] = image[1][s, :, lanes(c)] + ratio * before
            image[1][s, :, at_rest] = image[1][s, :, at_rest] + ratio * image[0][s, :, at_rest]
        coarse(msg, image[1], 3, False, chosen)
        sums = curve_of(fresh, image[1], chosen, sums)
    curve = curve_end(sums)
    msg[0] = jnp.where(lane == 6, curve, msg[0])
    start, wait = at.everywhere(msg, gat, esend, erecv)
    start()
    gat[me] = msg[...]
    drain()
    faces()
    k.arriving[1][...] = k.arriving[1][...] + ratio * k.arriving[0][...]
    finish_image(image[1], k.arriving[1])
    wait()
    tiles = gathered(gat, False)
    step_1 = fresh_energy / summed(gat, (6,))[0]
    c_res = c_res - step_1 * jnp.concatenate(tiles, axis=1)
    near = by_two(across_rows, c_res, pair_of(near_pair))
    for s in range(subs):
        mult_out[:, s, :] = step_0 * search[s] + step_1 * fresh[s]
        proj_out[:, s, :] = residual[s] - step_1 * image[1][s] - lift_of(near, s)


def deliver_kernel(first_in, second_in, first_out, second_out, held, sems):
    parts, depth = 2, held.shape[1] // 2

    def copy(n, out):
        which, part = n // parts, n % parts
        rows = pl.ds(part * depth, depth)
        middle = held.at[which, rows]
        if out:
            target = (first_out, second_out)[which].at[rows]
            return pltpu.make_async_copy(middle, target, sems.at[1, n])
        source = (first_in, second_in)[which].at[rows]
        return pltpu.make_async_copy(source, middle, sems.at[0, n])

    for n in range(2 * parts):
        copy(n, False).start()
    for n in range(2 * parts):
        copy(n, False).wait()
        copy(n, True).start()
    for n in range(2 * parts):
        copy(n, True).wait()


def by_kernels(schur_block, rigid_modes, coarse_inverse, dual_rhs, stiff_diag, face_length):
    loads, subs, interface = dual_rhs.shape
    rows = schur_block.shape[1]
    slot = interface // 6
    modes = rigid_modes.shape[1]
    vmem = pl.BlockSpec(memory_space=pltpu.VMEM)
    hbm = pl.BlockSpec(memory_space=pltpu.HBM)
    dma = pltpu.SemaphoreType.DMA
    order = NSUB * 64
    vector = pltpu.VMEM((subs, loads, interface), F32)
    edge = pltpu.VMEM((2, modes + 1, subs, slot), F32)
    face = pltpu.VMEM((2, 2, subs // 2, loads, slot), F32)
    basis = pltpu.VMEM((subs, 48, interface), BF16)
    square = pltpu.VMEM((order, order), BF16)
    scratch = dict(
        hold=pltpu.VMEM((2, subs // 2, rows, interface), F32),
        load_sem=dma((subs,)),
        input_sem=dma((5,)),
        edges=edge,
        across=edge,
        beyond=pltpu.VMEM((2, loads, subs, slot), F32),
        rsend=dma((2,)),
        rrecv=dma((2,)),
        tsend=dma((2,)),
        trecv=dma((2,)),
        bsend=dma((2,)),
        brecv=dma((2,)),
        inverse=pltpu.VMEM((NCRS,) + coarse_inverse.shape, F32),
        isend=dma((3,)),
        irecv=dma((3,)),
        wide=pltpu.VMEM((subs, 8, interface), F32),
        rhs=vector,
        mask=pltpu.VMEM((subs, interface), F32),
        precond=pltpu.VMEM((subs, interface), F32),
        basis_high=basis,
        basis_low=basis,
        residual=vector,
        middle_msg=pltpu.VMEM((32, 128), F32),
        middle_all=pltpu.VMEM((NSUB, 32, 128), F32),
        msend=dma((NSUB,)),
        mrecv=dma((NSUB,)),
        q_high=square,
        q_low=square,
        near_high=square,
        near_low=square,
        m_high=square,
        m_low=square,
        packed=pltpu.VMEM((4, 7, loads, slot), F32),
        search=vector,
        fresh=vector,
        product=pltpu.VMEM((2, subs // 2, loads, interface), F32),
        image=[vector] * 2,
        res=pltpu.VMEM((2, subs // 2, NCRS, loads, rows), F32),
    )
    sources = [
        jnp.swapaxes(rigid_modes, 0, 1),
        coarse_inverse,
        dual_rhs,
        stiff_diag,
        face_length,
    ]
    tiles = (1, 3, 1, 2)
    third = pltpu.VMEM((2, subs // 2, loads, 3 * slot), F32)
    scratch.update(
        cres=pltpu.VMEM((2, subs // 2, 2, loads, 3 * slot), F32),
        input=[pltpu.VMEM(source.shape, source.dtype) for source in sources],
        msg=[pltpu.VMEM((n, loads, 128), F32) for n in tiles],
        gat=[pltpu.VMEM((NSUB, n, loads, 128), F32) for n in tiles],
        esend=[dma((NSUB,))] * 4,
        erecv=[dma((NSUB,))] * 4,
        gath=[pltpu.VMEM((4, NCRS, 7, loads, slot), F32)] * ITERS,
        gsend=[dma((3, 4))] * ITERS,
        grecv=[dma((3, 4))] * ITERS,
        asend=[dma((3, 4, 2))] * ITERS,
        arecv=[dma((NCRS, 4, 2))] * ITERS,
        ctwin=[third] * ITERS,
        csend=[dma((4,))] * ITERS,
        crecv=[dma((4,))] * ITERS,
        lres=pltpu.VMEM((2, 2, 2, loads, slot), F32),
        ltwin=[pltpu.VMEM((2, 2, loads, slot), F32)] * ITERS,
        lsend=[dma((2,))] * ITERS,
        lrecv=[dma((2,))] * ITERS,
        arriving=[face] * ITERS,
        fsend=[dma((2, 4))] * ITERS,
        frecv=[dma((2, 4))] * ITERS,
    )
    names = [(name, len(v) if isinstance(v, list) else 0) for name, v in scratch.items()]
    shapes = [one for v in scratch.values() for one in (v if isinstance(v, list) else [v])]
    out = jax.ShapeDtypeStruct((loads, subs, interface), F32)
    results = pl.pallas_call(
        functools.partial(main_kernel, names),
        out_shape=(out, out),
        in_specs=[hbm] * 6,
        out_specs=(vmem, vmem),
        scratch_shapes=shapes,
        compiler_params=pltpu.CompilerParams(
            collective_id=0, has_side_effects=True, vmem_limit_bytes=56 * 1024 * 1024
        ),
        name="main",
    )(schur_block, *sources)
    return pl.pallas_call(
        deliver_kernel,
        out_shape=(out, out),
        in_specs=[hbm] * 2,
        out_specs=(hbm, hbm),
        scratch_shapes=[pltpu.VMEM((2, loads, subs, interface), F32), dma((2, 4))],
        compiler_params=pltpu.CompilerParams(vmem_limit_bytes=56 * 1024 * 1024),
        name="deliver",
    )(*results)


def shards(schur_block, rigid_modes, coarse_inverse, dual_rhs, stiff_diag, face_length):
    fits = dual_rhs.shape[0] == 8 and lax.axis_size("crs") == NCRS and lax.axis_size("sub") == NSUB
    build = by_kernels if fits else by_collectives
    return build(schur_block, rigid_modes, coarse_inverse, dual_rhs, stiff_diag, face_length)


def solution(mesh):
    return jax.shard_map(
        shards,
        mesh=mesh,
        in_specs=(
            P("sub", "crs", None),
            P("sub", None, None),
            P("crs", None),
            P("crs", "sub", None),
            P("sub", None),
            P("sub", None),
        ),
        out_specs=(P("crs", "sub", None), P("crs", "sub", None)),
        check_vma=False,
    )
```
